32 devices in a mesh: groups: 2 (over y), slab: 4 (over z), tm: 4 (over x, core).
Axes of the slice: x: 2, y: 2, z: 4, core: 2. Of those that a mesh axis runs over, the one named last changes fastest.
Arguments:
- start_disp: float32 [4, 16, 32, 256], P('tm', 'slab', 'groups'), parts along dimension 2, may hold values from -6 to 6
- start_vel: float32 [4, 16, 32, 256], P('tm', 'slab', 'groups'), parts along dimension 2, may hold values from -6 to 6
- stiffness: float32 [16, 32, 256], P('slab', 'groups'), parts along dimension 1, may hold values from 0.2 to 1.6
- pressure: float32 [16, 32, 256], P('slab', 'groups'), parts along dimension 1, may hold values from -4 to 4
- wet_tiles: int32 [16, 32, 32], P('slab', 'groups'), parts along dimension 1, may hold values 0 or 1
Outputs:
- new_disp: float32 [4, 16, 32, 256], P('tm', 'slab', 'groups'), parts along dimension 2
- new_vel: float32 [4, 16, 32, 256], P('tm', 'slab', 'groups'), parts along dimension 2
The draws below stay inside these ranges and needn't reach their ends.
There are 2 independent parts, one for each index of `groups`. The reference program is written for one: setup_inputs(seed, part) draws one part's arguments, and reference() takes and returns one part's arrays. A program takes and returns all parts, laid end to end along the dimension named above; each array names one. Nothing has to cross between parts.
All inputs are finite; a program needn't handle non-finite values. No bound on the sum of `wet_tiles` on one device may be relied on, other than what follows from the above.
Results may differ from the reference program's by a relative error of at most 0.00002.
Values sent between devices are 32-bit elements; how exact they have to be, the bound alone decides.
No kernel may reach another device: no remote copies, remote signals or barrier semaphores. Data moves between devices by JAX's collectives and lax.ppermute only.
A program may use at most 64 MiB of HBM per device.

```python
import math
import jax
import jax.numpy as jnp

CY = 16
CZ = 256
FINE_STEPS = 4
COARSE_STEPS = 2
SLICES = 4
NX = 16


def touch_ends(values, own_key, least, top_value):
    extent = values.shape
    spot = [jax.random.randint(jax.random.fold_in(own_key, axis), (), 0, extent[axis]) for axis in range(len(extent))]
    values = values.at[tuple(spot)].set(least)
    longest = extent.index(max(extent))
    spot[longest] = (spot[longest] + 1) % extent[longest]
    return values.at[tuple(spot)].set(top_value)


def block_levels(stream_key, shape, pieces, smallest, top_value):
    def one(axis_at, parts):
        draws = jax.random.uniform(jax.random.fold_in(jax.random.fold_in(stream_key, 6), axis_at), (parts,), jnp.float32, smallest / len(pieces), top_value / len(pieces))
        return jnp.repeat(jnp.exp(draws), shape[axis_at] // parts).reshape((-1,) + (1,) * (len(shape) - axis_at - 1))

    level = one(*pieces[0])
    for cut in pieces[1:]:
        level = level * one(*cut)
    return level


def normal_values(stream_key, shape, width, most, cuts=(), kind=jnp.bfloat16):
    result = jax.random.normal(stream_key, shape, jnp.float32) * width
    if len(cuts) > 0:
        result = block_levels(stream_key, shape, cuts, -0.22, 0.18) * result
    return jnp.clip(result, min=-most, max=most).astype(kind)


def setup_inputs(seed: int = 0, part: int = 0) -> dict:
    keys = jax.random.split(jax.random.key(seed), 6)
    part_splits = jax.random.split(jax.random.fold_in(keys[5], part), 6)
    start_disp = normal_values(part_splits[0], (SLICES, NX, CY, CZ), 1.0, 6.0, ((0, 4), (1, 4)), jnp.float32)
    start_vel = normal_values(part_splits[1], (SLICES, NX, CY, CZ), 0.5, 6.0, ((0, 4), (1, 4)), jnp.float32)
    stiffness = jnp.clip(jnp.exp(math.log(1.6) - 2.0794415 * jax.random.uniform(part_splits[2], (NX, CY, CZ), jnp.float32) ** block_levels(part_splits[2], (NX, CY, CZ), ((0, 4),), -0.2, 0.2)), 0.2, 1.6)
    pressure = normal_values(part_splits[3], (NX, CY, CZ), 0.5, 4.0, ((0, 4),), jnp.float32)
    wet_tiles = touch_ends((jax.random.randint(part_splits[4], (NX, CY, CZ // 8), 0, 2) < 1).astype(jnp.int32), jax.random.fold_in(part_splits[4], 1), 0, 1)
    return dict(start_disp=start_disp, start_vel=start_vel, stiffness=stiffness, pressure=pressure, wet_tiles=wet_tiles)


DAMPING = 0.05


def pad_axis(array, axis):
    widths = [(0, 0)] * array.ndim
    widths[array.ndim + axis] = (1, 1)
    return jnp.pad(array, widths)


def neighbours27(padded, disp):
    along_x = padded[..., :-2, :, :] + padded[..., 1:-1, :, :] + padded[..., 2:, :, :]
    wide_y = pad_axis(along_x, -2)
    along_y = wide_y[..., :-2, :] + wide_y[..., 1:-1, :] + wide_y[..., 2:, :]
    wide_z = pad_axis(along_y, -1)
    box = wide_z[..., :-2] + wide_z[..., 1:-1] + wide_z[..., 2:]
    return box - disp


def neighbours7(padded, disp):
    total = padded[..., :-2, :, :] + padded[..., 2:, :, :]
    wide_y = pad_axis(disp, -2)
    total = total + wide_y[..., :-2, :] + wide_y[..., 2:, :]
    wide_z = pad_axis(disp, -1)
    return total + wide_z[..., :-2] + wide_z[..., 2:]


def restrict(array):
    lead = array.shape[:-3]
    sx, sy, sz = array.shape[-3:]
    blocks = array.reshape(lead + (sx // 2, 2, sy // 2, 2, sz // 2, 2))
    return jnp.mean(blocks, axis=(-5, -3, -1))


def prolong(array):
    array = jnp.repeat(array, 2, axis=-3)
    array = jnp.repeat(array, 2, axis=-2)
    return jnp.repeat(array, 2, axis=-1)


def coarse_step(state, coarse_stiff):
    disp = state[0]
    vel = state[1]
    padded = pad_axis(disp, -3)
    vel = (1.0 - DAMPING) * vel + coarse_stiff * (neighbours7(padded, disp) / 6.0 - disp)
    return jnp.stack([disp + vel, vel])


def propagate(state, coarse_stiff):
    for step in range(COARSE_STEPS):
        state = coarse_step(state, coarse_stiff)
    return state


def reference(start_disp, start_vel, stiffness, pressure, wet_tiles):
    load = jnp.repeat(wet_tiles, 8, axis=-1).astype(jnp.float32) * pressure
    disp, vel = start_disp, start_vel
    for step in range(FINE_STEPS):
        padded = pad_axis(disp, -3)
        vel = (1.0 - DAMPING) * vel + stiffness * (neighbours27(padded, disp) / 26.0 - disp) + load
        disp = disp + vel
    coarse_stiff = restrict(stiffness)
    rest_old = jnp.stack([restrict(start_disp), restrict(start_vel)])
    rest_fine = jnp.stack([restrict(disp), restrict(vel)])
    old_image = propagate(rest_old, coarse_stiff)
    weight = rest_fine - old_image
    weight = weight.at[:, 0].set(rest_fine[:, 0])
    current = weight[:, 0]
    chained_list = [current]
    for slice_index in range(1, SLICES):
        current = weight[:, slice_index] + propagate(current, coarse_stiff)
        chained_list.append(current)
    chained = jnp.stack(chained_list, axis=1)
    correction = chained - rest_fine
    new_disp = disp + prolong(correction[0])
    new_vel = vel + prolong(correction[1])
    return new_disp, new_vel
```

```python
import jax
import jax.numpy as jnp
from jax import lax
from jax.experimental import pallas as pl
from jax.experimental.pallas import tpu as pltpu
from jax.sharding import PartitionSpec as P

FINE_STEPS = 4
COARSE_STEPS = 2
KEEP = 0.95
HALO = 4
HIGH = lax.Precision.HIGHEST
F32 = jnp.float32


def vmem(count):
    return [pl.BlockSpec(memory_space=pltpu.VMEM)] * count


def shape(*dims):
    return jax.ShapeDtypeStruct(dims, F32)


def dot(left, right, precision=HIGH):
    return lax.dot_general(left, right, (((1,), (0,)), ((), ())), precision=precision, preferred_element_type=F32)


def selector(rows, cols, down, across):
    row = lax.broadcasted_iota(jnp.int32, (rows, cols), 0) // down
    col = lax.broadcasted_iota(jnp.int32, (rows, cols), 1) // across
    return (row == col).astype(F32)


def around(flat, axis, period):
    size = flat.shape[axis]
    at = lax.broadcasted_iota(jnp.int32, flat.shape, axis) % period
    before = jnp.where(at == 0, 0.0, pltpu.roll(flat, 1, axis))
    after = jnp.where(at == period - 1, 0.0, pltpu.roll(flat, size - 1, axis))
    return before + after


def flat2(x):
    return x.reshape(x.shape[0] * x.shape[1], x.shape[2])


def fine_step(disp, vel, stiff, load):
    count, ny, nz = vel.shape
    mid = disp[1:-1]
    along = flat2(disp[:-2] + mid + disp[2:])
    along = along + around(along, 0, ny)
    box = (along + around(along, 1, nz)).reshape(count, ny, nz)
    vel = KEEP * vel + (stiff * ((box - mid) * (1.0 / 26.0) - mid) + load)
    return mid + vel, vel


def coarse_step(disp, vel, stiff):
    count, ny, nz = vel.shape
    mid = disp[1:-1]
    flat = flat2(mid)
    side = (around(flat, 0, ny) + around(flat, 1, nz)).reshape(count, ny, nz)
    vel = KEEP * vel + stiff * ((disp[:-2] + disp[2:] + side) * (1.0 / 6.0) - mid)
    return mid + vel, vel


def restrict(x, scratch):
    planes, ny, nz = x.shape
    half = planes // 2
    pairs = x.reshape(half, 2, ny, nz)
    pairs = pairs[:, 0] + pairs[:, 1]
    thin = dot(flat2(pairs), selector(nz, nz // 2, 2, 1) * 0.125)
    rows = half * ny
    scratch[pl.ds(0, rows), :] = thin
    out = scratch[pl.ds(0, rows // 2, stride=2), :] + scratch[pl.ds(1, rows // 2, stride=2), :]
    return out.reshape(half, ny // 2, nz // 2)


def pack_kernel(disp, vel, stiff, press, tiles, own, send_a, send_b):
    nx, ny, nz = stiff.shape
    slab = lax.axis_index("slab")
    wet = flat2(tiles[...]).astype(F32)
    load = dot(wet, selector(tiles.shape[2], nz, 1, nz // tiles.shape[2])).reshape(nx, ny, nz) * press[...]
    for i in range(nx):
        own[i] = disp[0, i]
        own[nx + i] = vel[0, i]
        own[2 * nx + i] = stiff[i]
        own[3 * nx + i] = load[i]

    def fill(target, skip):
        for i in range(nx):
            target[i] = disp[0, i]
        for i in range(nx - 1):
            target[nx + i] = vel[0, i + skip]
            target[2 * nx - 1 + i] = stiff[i + skip]
            target[3 * nx - 2 + i] = load[i + skip]

    @pl.when(slab % 2 == 0)
    def _():
        fill(send_a, 1)
        fill(send_b, 0)

    @pl.when(slab % 2 == 1)
    def _():
        fill(send_a, 0)
        fill(send_b, 1)


def fine_kernel(count, own, recv_a, recv_b, fine_disp, fine_vel, message, old, scratch):
    nx = own.shape[0] // 4
    slab = lax.axis_index("slab")
    even = slab % 2 == 0
    has_low = slab > 0
    has_high = slab < count - 1

    def part(base, number):
        a = recv_a[pl.ds(base, number)]
        b = recv_b[pl.ds(base, number)]
        low = jnp.where(has_low, jnp.where(even, b, a), 0.0)
        high = jnp.where(has_high, jnp.where(even, a, b), 0.0)
        return low, high

    def joined(index, base, number):
        low, high = part(base, number)
        return jnp.concatenate([low, own[pl.ds(index * nx, nx)], high], axis=0)

    disp = joined(0, 0, nx)
    vel = joined(1, nx, nx - 1)
    stiff = joined(2, 2 * nx - 1, nx - 1)
    load = joined(3, 3 * nx - 2, nx - 1)

    coarse_disp = restrict(disp, scratch)
    coarse_vel = restrict(vel[1:-1], scratch)
    coarse_stiff = restrict(stiff[1:-1], scratch)
    for step in range(FINE_STEPS):
        cut = 0 if step == 0 else 1
        last = vel.shape[0] - cut
        disp, vel = fine_step(disp, vel[cut:last], stiff[step : stiff.shape[0] - step], load[step : load.shape[0] - step])
    fine_disp[...] = disp
    fine_vel[...] = vel
    rest_disp = restrict(disp, scratch)
    rest_vel = restrict(vel, scratch)
    one_disp, one_vel = coarse_step(coarse_disp, coarse_vel, coarse_stiff)
    two_disp, two_vel = coarse_step(one_disp, one_vel[1:-1], coarse_stiff[1:-1])
    first = lax.axis_index("tm") == 0
    half = nx // 2
    image_disp = jnp.where(first, 0.0, two_disp)
    image_vel = jnp.where(first, 0.0, two_vel)
    old[pl.ds(0, half)] = image_disp
    old[pl.ds(half, half)] = image_vel
    message[pl.ds(0, half)] = rest_disp - image_disp
    message[pl.ds(half, half)] = rest_vel - image_vel
    message[pl.ds(2 * half, half)] = coarse_stiff[1:-1]


def chain_kernel(times, partners, *refs):
    inputs = refs[: len(partners)]
    outputs = refs[len(partners) : len(partners) + times - 1]
    window = refs[-1]
    half = inputs[0].shape[0] // 3
    slab = lax.axis_index("slab")
    reach = times - 1
    window[...] = jnp.zeros(window.shape, F32)
    for ref, place in zip(inputs, partners):
        at = (place(slab) - slab + reach) * half
        for field in range(3):
            window[field, pl.ds(at, half)] = ref[pl.ds(field * half, half)]
    disp, vel, stiff = window[0], window[1], window[2]
    powers = []
    for power in range(reach):
        for _ in range(COARSE_STEPS):
            disp, vel = coarse_step(disp, vel[1:-1], stiff[1:-1])
            stiff = stiff[1:-1]
        edge = (disp.shape[0] - half) // 2
        powers.append((disp[edge : edge + half], vel[edge : edge + half]))
    slot = lax.axis_index("tm")
    for k in range(1, times):
        gap = (slot ^ k) - slot
        pick_disp, pick_vel = powers[0]
        for power in range(1, reach):
            pick_disp = jnp.where(gap == power + 1, powers[power][0], pick_disp)
            pick_vel = jnp.where(gap == power + 1, powers[power][1], pick_vel)
        outputs[k - 1][pl.ds(0, half)] = pick_disp
        outputs[k - 1][pl.ds(half, half)] = pick_vel


def finish_kernel(times, *refs):
    fine_disp, fine_vel, old = refs[:3]
    received = refs[3 : 3 + times - 1]
    new_disp, new_vel = refs[3 + times - 1 : 5 + times - 1]
    tall = refs[-1]
    slot = lax.axis_index("tm")
    total = -old[...]
    for k in range(1, times):
        total = total + jnp.where((slot ^ k) < slot, received[k - 1][...], 0.0)
    half2, cy, cz = total.shape
    rows = half2 * cy
    tall[pl.ds(0, rows, stride=2), :] = flat2(total)
    tall[pl.ds(1, rows, stride=2), :] = flat2(total)
    wide = dot(tall[...], selector(cz, 2 * cz, 1, 2)).reshape(half2, 2 * cy, 2 * cz)
    for i in range(fine_disp.shape[0]):
        new_disp[0, i] = fine_disp[i] + wide[i // 2]
        new_vel[0, i] = fine_vel[i] + wide[half2 // 2 + i // 2]


def local(start_disp, start_vel, stiffness, pressure, wet_tiles):
    slabs = lax.axis_size("slab")
    times = lax.axis_size("tm")
    _, nx, ny, nz = start_disp.shape
    half = nx // 2
    pair = ("slab", "tm")

    def at(s, t):
        return s * times + t

    low_pairs = [(at(s, t), at(s ^ 1, t)) for s in range(slabs) for t in range(times)]
    high_pairs = []
    for s in range(slabs):
        for t in range(times):
            if s == 0 or s == slabs - 1:
                high_pairs.append((at(s, t), at(s, t ^ 1)))
            else:
                high_pairs.append((at(s, t), at(s + 1 if s % 2 else s - 1, t)))

    packed = shape(4 * nx - 3, ny, nz)
    own, send_a, send_b = pl.pallas_call(
        pack_kernel, out_shape=(shape(4 * nx, ny, nz), packed, packed), in_specs=vmem(5), out_specs=vmem(3), name="pack"
    )(start_disp, start_vel, stiffness, pressure, wet_tiles)
    recv_a = lax.ppermute(send_a, pair, low_pairs)
    recv_b = lax.ppermute(send_b, pair, high_pairs)

    def fine_body(*refs):
        fine_kernel(slabs, *refs)

    grid = shape(nx, ny, nz)
    fine_disp, fine_vel, message, old = pl.pallas_call(
        fine_body,
        out_shape=(grid, grid, shape(3 * half, ny // 2, nz // 2), shape(2 * half, ny // 2, nz // 2)),
        in_specs=vmem(3),
        out_specs=vmem(4),
        scratch_shapes=[pltpu.VMEM(((nx + 2 * HALO) // 2 * ny, nz // 2), F32)],
        name="fine",
    )(own, recv_a, recv_b)

    messages, places = [message], [lambda s: s]
    if slabs <= times and slabs & (slabs - 1) == 0:
        for k in range(1, slabs):
            messages.append(lax.ppermute(message, "slab", [(s, s ^ k) for s in range(slabs)]))
            places.append(lambda s, k=k: s ^ k)
    else:
        for k in range(1, times):
            for shift in (k, -k):
                route = [(s - shift, s) for s in range(slabs) if 0 <= s - shift < slabs]
                messages.append(lax.ppermute(message, "slab", route))
                places.append(lambda s, shift=shift: s - shift)

    def chain_body(*refs):
        chain_kernel(times, places, *refs)

    link = shape(2 * half, ny // 2, nz // 2)
    sends = pl.pallas_call(
        chain_body,
        out_shape=(link,) * (times - 1),
        in_specs=vmem(len(messages)),
        out_specs=vmem(times - 1),
        scratch_shapes=[pltpu.VMEM((3, (2 * times - 1) * half, ny // 2, nz // 2), F32)],
        name="chain",
    )(*messages)
    received = [lax.ppermute(sends[k - 1], "tm", [(t, t ^ k) for t in range(times)]) for k in range(1, times)]

    def finish_body(*refs):
        finish_kernel(times, *refs)

    return pl.pallas_call(
        finish_body,
        out_shape=(shape(1, nx, ny, nz), shape(1, nx, ny, nz)),
        in_specs=vmem(3 + times - 1),
        out_specs=vmem(2),
        scratch_shapes=[pltpu.VMEM((nx * ny, nz // 2), F32)],
        name="finish",
    )(fine_disp, fine_vel, old, *received)


def solution(mesh):
    in_specs = (
        P("tm", "slab", "groups", None),
        P("tm", "slab", "groups", None),
        P("slab", "groups", None),
        P("slab", "groups", None),
        P("slab", "groups", None),
    )
    out_specs = (P("tm", "slab", "groups", None), P("tm", "slab", "groups", None))
    return jax.shard_map(local, mesh=mesh, in_specs=in_specs, out_specs=out_specs, check_vma=False)
```

```python
import jax
import jax.numpy as jnp
from jax import lax
from jax.experimental import pallas as pl
from jax.experimental.pallas import tpu as pltpu
from jax.sharding import PartitionSpec as P

FINE_STEPS = 4
COARSE_STEPS = 2
KEEP = 0.95
HALO = 4
HIGH = lax.Precision.HIGHEST
F32 = jnp.float32


def vmem(count):
    return [pl.BlockSpec(memory_space=pltpu.VMEM)] * count


def shape(*dims):
    return jax.ShapeDtypeStruct(dims, F32)


def resident(*dims):
    return pltpu.VMEM(dims, F32)


def pinned(*arrays):
    return [pltpu.with_memory_space_constraint(x, pltpu.VMEM) for x in arrays]


def dot(left, right, precision=HIGH):
    return lax.dot_general(left, right, (((1,), (0,)), ((), ())), precision=precision, preferred_element_type=F32)


def selector(rows, cols, down, across):
    row = lax.broadcasted_iota(jnp.int32, (rows, cols), 0) // down
    col = lax.broadcasted_iota(jnp.int32, (rows, cols), 1) // across
    return (row == col).astype(F32)


def around(flat, axis, period):
    size = flat.shape[axis]
    at = lax.broadcasted_iota(jnp.int32, flat.shape, axis) % period
    before = jnp.where(at == 0, 0.0, pltpu.roll(flat, 1, axis))
    after = jnp.where(at == period - 1, 0.0, pltpu.roll(flat, size - 1, axis))
    return before + after


def flat2(x):
    return x.reshape(x.shape[0] * x.shape[1], x.shape[2])


def fine_step(disp, vel, stiff, load):
    count, ny, nz = vel.shape
    mid = disp[1:-1]
    along = flat2(disp[:-2] + mid + disp[2:])
    along = along + around(along, 0, ny)
    box = (along + around(along, 1, nz)).reshape(count, ny, nz)
    vel = KEEP * vel + (stiff * ((box - mid) * (1.0 / 26.0) - mid) + load)
    return mid + vel, vel


def coarse_step(disp, vel, stiff):
    count, ny, nz = vel.shape
    mid = disp[1:-1]
    flat = flat2(mid)
    side = (around(flat, 0, ny) + around(flat, 1, nz)).reshape(count, ny, nz)
    vel = KEEP * vel + stiff * ((disp[:-2] + disp[2:] + side) * (1.0 / 6.0) - mid)
    return mid + vel, vel


def restrict(x, scratch):
    planes, ny, nz = x.shape
    half = planes // 2
    pairs = x.reshape(half, 2, ny, nz)
    pairs = pairs[:, 0] + pairs[:, 1]
    thin = dot(flat2(pairs), selector(nz, nz // 2, 2, 1) * 0.125)
    rows = half * ny
    scratch[pl.ds(0, rows), :] = thin
    out = scratch[pl.ds(0, rows // 2, stride=2), :] + scratch[pl.ds(1, rows // 2, stride=2), :]
    return out.reshape(half, ny // 2, nz // 2)


def pack_kernel(disp, vel, stiff, press, tiles, own, send_a, send_b):
    nx, ny, nz = stiff.shape
    slab = lax.axis_index("slab")
    wet = flat2(tiles[...]).astype(F32)
    load = dot(wet, selector(tiles.shape[2], nz, 1, nz // tiles.shape[2])).reshape(nx, ny, nz) * press[...]
    for i in range(nx):
        own[i] = disp[0, i]
        own[nx + i] = vel[0, i]
        own[2 * nx + i] = stiff[i]
        own[3 * nx + i] = load[i]

    def fill(target, skip):
        for i in range(nx):
            target[i] = disp[0, i]
        for i in range(nx - 1):
            target[nx + i] = vel[0, i + skip]
            target[2 * nx - 1 + i] = stiff[i + skip]
            target[3 * nx - 2 + i] = load[i + skip]

    @pl.when(slab % 2 == 0)
    def _():
        fill(send_a, 1)
        fill(send_b, 0)

    @pl.when(slab % 2 == 1)
    def _():
        fill(send_a, 0)
        fill(send_b, 1)


def fine_kernel(count, own, recv_a, recv_b, fine_disp, fine_vel, message, old, scratch):
    nx = own.shape[0] // 4
    slab = lax.axis_index("slab")
    even = slab % 2 == 0
    has_low = slab > 0
    has_high = slab < count - 1

    def part(base, number):
        a = recv_a[pl.ds(base, number)]
        b = recv_b[pl.ds(base, number)]
        low = jnp.where(has_low, jnp.where(even, b, a), 0.0)
        high = jnp.where(has_high, jnp.where(even, a, b), 0.0)
        return low, high

    def joined(index, base, number):
        low, high = part(base, number)
        return jnp.concatenate([low, own[pl.ds(index * nx, nx)], high], axis=0)

    disp = joined(0, 0, nx)
    vel = joined(1, nx, nx - 1)
    stiff = joined(2, 2 * nx - 1, nx - 1)
    load = joined(3, 3 * nx - 2, nx - 1)

    coarse_disp = restrict(disp, scratch)
    coarse_vel = restrict(vel[1:-1], scratch)
    coarse_stiff = restrict(stiff[1:-1], scratch)
    for step in range(FINE_STEPS):
        cut = 0 if step == 0 else 1
        last = vel.shape[0] - cut
        disp, vel = fine_step(disp, vel[cut:last], stiff[step : stiff.shape[0] - step], load[step : load.shape[0] - step])
    fine_disp[...] = disp
    fine_vel[...] = vel
    rest_disp = restrict(disp, scratch)
    rest_vel = restrict(vel, scratch)
    one_disp, one_vel = coarse_step(coarse_disp, coarse_vel, coarse_stiff)
    two_disp, two_vel = coarse_step(one_disp, one_vel[1:-1], coarse_stiff[1:-1])
    first = lax.axis_index("tm") == 0
    half = nx // 2
    image_disp = jnp.where(first, 0.0, two_disp)
    image_vel = jnp.where(first, 0.0, two_vel)
    old[pl.ds(0, half)] = image_disp
    old[pl.ds(half, half)] = image_vel
    message[pl.ds(0, half)] = rest_disp - image_disp
    message[pl.ds(half, half)] = rest_vel - image_vel
    message[pl.ds(2 * half, half)] = coarse_stiff[1:-1]


def chain_kernel(times, partners, *refs):
    inputs = refs[: len(partners)]
    outputs = refs[len(partners) : len(partners) + times - 1]
    window = refs[-1]
    half = inputs[0].shape[0] // 3
    slab = lax.axis_index("slab")
    reach = times - 1
    window[...] = jnp.zeros(window.shape, F32)
    for ref, place in zip(inputs, partners):
        at = (place(slab) - slab + reach) * half
        for field in range(3):
            window[field, pl.ds(at, half)] = ref[pl.ds(field * half, half)]
    disp, vel, stiff = window[0], window[1], window[2]
    powers = []
    for power in range(reach):
        for _ in range(COARSE_STEPS):
            disp, vel = coarse_step(disp, vel[1:-1], stiff[1:-1])
            stiff = stiff[1:-1]
        edge = (disp.shape[0] - half) // 2
        powers.append((disp[edge : edge + half], vel[edge : edge + half]))
    slot = lax.axis_index("tm")
    for k in range(1, times):
        gap = (slot ^ k) - slot
        pick_disp, pick_vel = powers[0]
        for power in range(1, reach):
            pick_disp = jnp.where(gap == power + 1, powers[power][0], pick_disp)
            pick_vel = jnp.where(gap == power + 1, powers[power][1], pick_vel)
        outputs[k - 1][pl.ds(0, half)] = pick_disp
        outputs[k - 1][pl.ds(half, half)] = pick_vel


def finish_kernel(times, *refs):
    fine_disp, fine_vel, old = refs[:3]
    received = refs[3 : 3 + times - 1]
    new_disp, new_vel = refs[3 + times - 1 : 5 + times - 1]
    tall = refs[-1]
    slot = lax.axis_index("tm")
    total = -old[...]
    for k in range(1, times):
        total = total + jnp.where((slot ^ k) < slot, received[k - 1][...], 0.0)
    half2, cy, cz = total.shape
    rows = half2 * cy
    tall[pl.ds(0, rows, stride=2), :] = flat2(total)
    tall[pl.ds(1, rows, stride=2), :] = flat2(total)
    wide = dot(tall[...], selector(cz, 2 * cz, 1, 2)).reshape(half2, 2 * cy, 2 * cz)
    for i in range(fine_disp.shape[0]):
        new_disp[0, i] = fine_disp[i] + wide[i // 2]
        new_vel[0, i] = fine_vel[i] + wide[half2 // 2 + i // 2]


def local(start_disp, start_vel, stiffness, pressure, wet_tiles):
    slabs = lax.axis_size("slab")
    times = lax.axis_size("tm")
    _, nx, ny, nz = start_disp.shape
    half = nx // 2
    pair = ("slab", "tm")

    def at(s, t):
        return s * times + t

    low_pairs = [(at(s, t), at(s ^ 1, t)) for s in range(slabs) for t in range(times)]
    high_pairs = []
    for s in range(slabs):
        for t in range(times):
            if s == 0 or s == slabs - 1:
                high_pairs.append((at(s, t), at(s, t ^ 1)))
            else:
                high_pairs.append((at(s, t), at(s + 1 if s % 2 else s - 1, t)))

    packed = resident(4 * nx - 3, ny, nz)
    own, send_a, send_b = pl.pallas_call(
        pack_kernel, out_shape=(resident(4 * nx, ny, nz), packed, packed), in_specs=vmem(5), out_specs=vmem(3), name="pack"
    )(start_disp, start_vel, stiffness, pressure, wet_tiles)
    recv_a = lax.ppermute(send_a, pair, low_pairs)
    recv_b = lax.ppermute(send_b, pair, high_pairs)

    def fine_body(*refs):
        fine_kernel(slabs, *refs)

    grid = resident(nx, ny, nz)
    fine_disp, fine_vel, message, old = pl.pallas_call(
        fine_body,
        out_shape=(grid, grid, resident(3 * half, ny // 2, nz // 2), resident(2 * half, ny // 2, nz // 2)),
        in_specs=vmem(3),
        out_specs=vmem(4),
        scratch_shapes=[pltpu.VMEM(((nx + 2 * HALO) // 2 * ny, nz // 2), F32)],
        name="fine",
    )(*pinned(own, recv_a, recv_b))

    messages, places = [message], [lambda s: s]
    if slabs <= times and slabs & (slabs - 1) == 0:
        for k in range(1, slabs):
            messages.append(lax.ppermute(message, "slab", [(s, s ^ k) for s in range(slabs)]))
            places.append(lambda s, k=k: s ^ k)
    else:
        for k in range(1, times):
            for shift in (k, -k):
                route = [(s - shift, s) for s in range(slabs) if 0 <= s - shift < slabs]
                messages.append(lax.ppermute(message, "slab", route))
                places.append(lambda s, shift=shift: s - shift)

    def chain_body(*refs):
        chain_kernel(times, places, *refs)

    link = resident(2 * half, ny // 2, nz // 2)
    sends = pl.pallas_call(
        chain_body,
        out_shape=(link,) * (times - 1),
        in_specs=vmem(len(messages)),
        out_specs=vmem(times - 1),
        scratch_shapes=[pltpu.VMEM((3, (2 * times - 1) * half, ny // 2, nz // 2), F32)],
        name="chain",
    )(*pinned(*messages))
    received = [lax.ppermute(sends[k - 1], "tm", [(t, t ^ k) for t in range(times)]) for k in range(1, times)]

    def finish_body(*refs):
        finish_kernel(times, *refs)

    return pl.pallas_call(
        finish_body,
        out_shape=(shape(1, nx, ny, nz), shape(1, nx, ny, nz)),
        in_specs=vmem(3 + times - 1),
        out_specs=vmem(2),
        scratch_shapes=[pltpu.VMEM((nx * ny, nz // 2), F32)],
        name="finish",
    )(*pinned(fine_disp, fine_vel, old, *received))


def solution(mesh):
    in_specs = (
        P("tm", "slab", "groups", None),
        P("tm", "slab", "groups", None),
        P("slab", "groups", None),
        P("slab", "groups", None),
        P("slab", "groups", None),
    )
    out_specs = (P("tm", "slab", "groups", None), P("tm", "slab", "groups", None))
    return jax.shard_map(local, mesh=mesh, in_specs=in_specs, out_specs=out_specs, check_vma=False)
```

```python
import jax
import jax.numpy as jnp
from jax import lax
from jax.experimental import pallas as pl
from jax.experimental.pallas import tpu as pltpu
from jax.sharding import PartitionSpec as P

FINE_STEPS = 4
COARSE_STEPS = 2
KEEP = 0.95
HIGH = lax.Precision.HIGHEST
F32 = jnp.float32


def vmem(count):
    return [pl.BlockSpec(memory_space=pltpu.VMEM)] * count


def shape(*dims):
    return jax.ShapeDtypeStruct(dims, F32)


def resident(*dims):
    return pltpu.VMEM(dims, F32)


def pinned(*arrays):
    return [pltpu.with_memory_space_constraint(x, pltpu.VMEM) for x in arrays]


def dot(left, right, precision=HIGH):
    return lax.dot_general(left, right, (((1,), (0,)), ((), ())), precision=precision, preferred_element_type=F32)


def selector(rows, cols, down, across):
    row = lax.broadcasted_iota(jnp.int32, (rows, cols), 0) // down
    col = lax.broadcasted_iota(jnp.int32, (rows, cols), 1) // across
    return (row == col).astype(F32)


def around(flat, axis, period):
    size = flat.shape[axis]
    at = lax.broadcasted_iota(jnp.int32, flat.shape, axis) % period
    before = jnp.where(at == 0, 0.0, pltpu.roll(flat, 1, axis))
    after = jnp.where(at == period - 1, 0.0, pltpu.roll(flat, size - 1, axis))
    return before + after


def flat2(x):
    return x.reshape(x.shape[0] * x.shape[1], x.shape[2])


def box9(x):
    flat = flat2(x)
    flat = flat + around(flat, 0, x.shape[1])
    flat = flat + around(flat, 1, x.shape[2])
    return flat.reshape(x.shape)


def face4(x):
    flat = flat2(x)
    return (around(flat, 0, x.shape[1]) + around(flat, 1, x.shape[2])).reshape(x.shape)


def three(box):
    none = jnp.zeros_like(box[:1])
    return box + jnp.concatenate([none, box[:-1]], axis=0) + jnp.concatenate([box[1:], none], axis=0)


def push(stiff, boxes, disp):
    return stiff * ((boxes - disp) * (1.0 / 26.0) - disp)


def pull(stiff, faces, disp):
    return stiff * (faces * (1.0 / 6.0) - disp)


def coarse_step(disp, vel, stiff):
    mid = disp[1:-1]
    vel = KEEP * vel + pull(stiff, disp[:-2] + disp[2:] + face4(mid), mid)
    return mid + vel, vel


def restrict(x, scratch):
    planes, ny, nz = x.shape
    half = planes // 2
    pairs = x.reshape(half, 2, ny, nz)
    pairs = pairs[:, 0] + pairs[:, 1]
    thin = dot(flat2(pairs), selector(nz, nz // 2, 2, 1) * 0.125)
    rows = half * ny
    scratch[pl.ds(0, rows), :] = thin
    out = scratch[pl.ds(0, rows // 2, stride=2), :] + scratch[pl.ds(1, rows // 2, stride=2), :]
    return out.reshape(half, ny // 2, nz // 2)


def pack_kernel(disp, vel, stiff, press, tiles, own, coarse, send_a, send_b, scratch):
    nx, ny, nz = stiff.shape
    half = nx // 2
    slab = lax.axis_index("slab")
    start = disp[0]
    k = stiff[...]
    wet = flat2(tiles[...]).astype(F32)
    load = dot(wet, selector(tiles.shape[2], nz, 1, nz // tiles.shape[2])).reshape(nx, ny, nz) * press[...]
    boxes = box9(start)
    first = KEEP * vel[0] + load + push(k, three(boxes), start)
    moved = start + first
    inner = slice(1, nx - 1)
    box_moved = box9(moved[inner])
    near = jnp.concatenate([box_moved[:1] + box_moved[1:2], box_moved[-2:-1] + box_moved[-1:]], axis=0)
    spots = (1, nx - 2)

    def at(x):
        return jnp.concatenate([x[i : i + 1] for i in spots], axis=0)

    second = at(moved) + KEEP * at(first) + at(load) + push(at(k), near, at(moved))
    box_second = box9(second)

    fields = restrict(jnp.concatenate([start, vel[0], k], axis=0), scratch)
    wide_disp, wide_vel, wide_k = fields[:half], fields[half : 2 * half], fields[2 * half :]
    none = jnp.zeros_like(wide_disp[:1])
    faces = face4(wide_disp) + jnp.concatenate([none, wide_disp[:-1]], axis=0) + jnp.concatenate([wide_disp[1:], none], axis=0)
    wide_first = KEEP * wide_vel + pull(wide_k, faces, wide_disp)

    own[pl.ds(0, nx)] = start
    own[pl.ds(nx, nx)] = first
    own[pl.ds(2 * nx, nx)] = k
    own[pl.ds(3 * nx, nx)] = load
    coarse[pl.ds(0, half)] = wide_disp
    coarse[pl.ds(half, half)] = wide_first
    coarse[pl.ds(2 * half, half)] = wide_k

    def fill(target, edge, spot, end, which):
        share = k[edge] * (1.0 / 26.0)
        target[0] = start[edge]
        target[1] = first[edge]
        target[2] = k[edge]
        target[3] = load[edge] + share * box_moved[spot - 1]
        target[4] = load[edge] + share * box_second[which]
        target[5] = k[spot]
        cy, cz = ny // 2, nz // 2
        target[6, pl.ds(0, cy), pl.ds(0, cz)] = wide_disp[end]
        target[6, pl.ds(0, cy), pl.ds(cz, cz)] = wide_disp[end] + wide_first[end]
        target[6, pl.ds(cy, cy), pl.ds(0, cz)] = wide_k[end]
        target[6, pl.ds(cy, cy), pl.ds(cz, cz)] = wide_k[end]

    @pl.when(slab % 2 == 0)
    def _():
        fill(send_a, nx - 1, nx - 2, half - 1, 1)
        fill(send_b, 0, 1, 0, 0)

    @pl.when(slab % 2 == 1)
    def _():
        fill(send_a, 0, 1, 0, 0)
        fill(send_b, nx - 1, nx - 2, half - 1, 1)


def fine_kernel(count, own, coarse, recv_a, recv_b, fine_disp, fine_vel, message, old, scratch):
    nx, ny, nz = fine_disp.shape
    half = nx // 2
    slab = lax.axis_index("slab")
    even = slab % 2 == 0
    a, b = recv_a[...], recv_b[...]
    low = jnp.where(slab > 0, jnp.where(even, b, a), 0.0)
    high = jnp.where(slab < count - 1, jnp.where(even, a, b), 0.0)

    def outer(i):
        return jnp.concatenate([low[i : i + 1], high[i : i + 1]], axis=0)

    def joined(i, inner):
        return jnp.concatenate([low[i : i + 1], inner, high[i : i + 1]], axis=0)

    start = own[pl.ds(0, nx)]
    k = joined(2, own[pl.ds(2 * nx, nx)])
    load = own[pl.ds(3 * nx, nx)]
    disp = joined(0, start)
    box = box9(jnp.concatenate([disp[1:2], disp[:1], disp[-1:], disp[-2:-1]], axis=0))
    box = jnp.concatenate([box[:2], jnp.zeros_like(disp[2:-2]), box[2:]], axis=0)
    vel = joined(1, own[pl.ds(nx, nx)]) + k * (1.0 / 26.0) * box
    disp = disp + vel
    box = box9(disp)
    vel = KEEP * vel + joined(3, load) + push(k, three(box), disp)
    far = outer(5) * (1.0 / 26.0) * jnp.concatenate([box[:1], box[-1:]], axis=0)
    disp = disp + vel
    box = box9(jnp.concatenate([far[:1], disp, far[1:]], axis=0))
    boxes = box[:-2] + box[1:-1] + box[2:]
    vel = KEEP * vel + joined(4, load) + push(k, boxes, disp)
    disp = disp + vel
    box = box9(disp)
    boxes = box[:-2] + box[1:-1] + box[2:]
    vel = KEEP * vel[1:-1] + load + push(k[1:-1], boxes, disp[1:-1])
    disp = disp[1:-1] + vel
    fine_disp[...] = disp
    fine_vel[...] = vel
    rest = restrict(jnp.concatenate([disp, vel], axis=0), scratch)

    cy, cz = ny // 2, nz // 2
    wide_disp = coarse[pl.ds(0, half)]
    wide_k = coarse[pl.ds(2 * half, half)]
    out_disp = outer(6)[:, :cy, :cz]
    out_moved = outer(6)[:, :cy, cz:]
    out_k = outer(6)[:, cy:, :cz]
    none = [jnp.zeros_like(wide_disp[:1])] * (half - 2)
    ends = jnp.concatenate([out_disp[:1], *none, out_disp[1:]], axis=0)
    wide_vel = coarse[pl.ds(half, half)] + wide_k * (1.0 / 6.0) * ends
    inner = jnp.concatenate([wide_disp[:1], wide_disp[-1:]], axis=0)
    out_moved = out_moved + out_k * (1.0 / 6.0) * inner
    moved = jnp.concatenate([out_moved[:1], wide_disp + wide_vel, out_moved[1:]], axis=0)
    image_disp, image_vel = coarse_step(moved, wide_vel, wide_k)
    first = lax.axis_index("tm") == 0
    image_disp = jnp.where(first, 0.0, image_disp)
    image_vel = jnp.where(first, 0.0, image_vel)
    old[pl.ds(0, half)] = image_disp
    old[pl.ds(half, half)] = image_vel
    message[pl.ds(0, half)] = rest[:half] - image_disp
    message[pl.ds(half, half)] = rest[half:] - image_vel
    message[pl.ds(2 * half, half)] = wide_k


def chain_kernel(times, partners, *refs):
    inputs = refs[: len(partners)]
    outputs = refs[len(partners) : len(partners) + times - 1]
    window = refs[-1]
    half = inputs[0].shape[0] // 3
    slab = lax.axis_index("slab")
    reach = times - 1
    window[...] = jnp.zeros(window.shape, F32)
    for ref, place in zip(inputs, partners):
        at = (place(slab) - slab + reach) * half
        for field in range(3):
            window[field, pl.ds(at, half)] = ref[pl.ds(field * half, half)]
    disp, vel, stiff = window[0], window[1], window[2]
    powers = []
    for power in range(reach):
        for _ in range(COARSE_STEPS):
            disp, vel = coarse_step(disp, vel[1:-1], stiff[1:-1])
            stiff = stiff[1:-1]
        edge = (disp.shape[0] - half) // 2
        powers.append((disp[edge : edge + half], vel[edge : edge + half]))
    slot = lax.axis_index("tm")
    for k in range(1, times):
        gap = (slot ^ k) - slot
        pick_disp, pick_vel = powers[0]
        for power in range(1, reach):
            pick_disp = jnp.where(gap == power + 1, powers[power][0], pick_disp)
            pick_vel = jnp.where(gap == power + 1, powers[power][1], pick_vel)
        outputs[k - 1][pl.ds(0, half)] = pick_disp
        outputs[k - 1][pl.ds(half, half)] = pick_vel


def finish_kernel(times, *refs):
    fine_disp, fine_vel, old = refs[:3]
    received = refs[3 : 3 + times - 1]
    new_disp, new_vel = refs[3 + times - 1 : 5 + times - 1]
    tall = refs[-1]
    slot = lax.axis_index("tm")
    total = -old[...]
    for k in range(1, times):
        total = total + jnp.where((slot ^ k) < slot, received[k - 1][...], 0.0)
    half2, cy, cz = total.shape
    rows = half2 * cy
    tall[pl.ds(0, rows, stride=2), :] = flat2(total)
    tall[pl.ds(1, rows, stride=2), :] = flat2(total)
    wide = dot(tall[...], selector(cz, 2 * cz, 1, 2)).reshape(half2, 2 * cy, 2 * cz)
    for i in range(fine_disp.shape[0]):
        new_disp[0, i] = fine_disp[i] + wide[i // 2]
        new_vel[0, i] = fine_vel[i] + wide[half2 // 2 + i // 2]


def local(start_disp, start_vel, stiffness, pressure, wet_tiles):
    slabs = lax.axis_size("slab")
    times = lax.axis_size("tm")
    _, nx, ny, nz = start_disp.shape
    half = nx // 2
    pair = ("slab", "tm")

    def at(s, t):
        return s * times + t

    low_pairs = [(at(s, t), at(s ^ 1, t)) for s in range(slabs) for t in range(times)]
    high_pairs = []
    for s in range(slabs):
        for t in range(times):
            if s == 0 or s == slabs - 1:
                high_pairs.append((at(s, t), at(s, t ^ 1)))
            else:
                high_pairs.append((at(s, t), at(s + 1 if s % 2 else s - 1, t)))

    packed = resident(7, ny, nz)
    coarse_cells = (ny // 2, nz // 2)
    own, coarse, send_a, send_b = pl.pallas_call(
        pack_kernel,
        out_shape=(resident(4 * nx, ny, nz), resident(3 * half, *coarse_cells), packed, packed),
        in_specs=vmem(5),
        out_specs=vmem(4),
        scratch_shapes=[pltpu.VMEM((3 * half * ny, nz // 2), F32)],
        name="pack",
    )(start_disp, start_vel, stiffness, pressure, wet_tiles)
    recv_a = lax.ppermute(send_a, pair, low_pairs)
    recv_b = lax.ppermute(send_b, pair, high_pairs)

    def fine_body(*refs):
        fine_kernel(slabs, *refs)

    grid = resident(nx, ny, nz)
    fine_disp, fine_vel, message, old = pl.pallas_call(
        fine_body,
        out_shape=(grid, grid, resident(3 * half, *coarse_cells), resident(2 * half, *coarse_cells)),
        in_specs=vmem(4),
        out_specs=vmem(4),
        scratch_shapes=[pltpu.VMEM((2 * half * ny, nz // 2), F32)],
        name="fine",
    )(*pinned(own, coarse, recv_a, recv_b))

    messages, places = [message], [lambda s: s]
    if slabs <= times and slabs & (slabs - 1) == 0:
        for k in range(1, slabs):
            messages.append(lax.ppermute(message, "slab", [(s, s ^ k) for s in range(slabs)]))
            places.append(lambda s, k=k: s ^ k)
    else:
        for k in range(1, times):
            for shift in (k, -k):
                route = [(s - shift, s) for s in range(slabs) if 0 <= s - shift < slabs]
                messages.append(lax.ppermute(message, "slab", route))
                places.append(lambda s, shift=shift: s - shift)

    def chain_body(*refs):
        chain_kernel(times, places, *refs)

    link = resident(2 * half, ny // 2, nz // 2)
    sends = pl.pallas_call(
        chain_body,
        out_shape=(link,) * (times - 1),
        in_specs=vmem(len(messages)),
        out_specs=vmem(times - 1),
        scratch_shapes=[pltpu.VMEM((3, (2 * times - 1) * half, ny // 2, nz // 2), F32)],
        name="chain",
    )(*pinned(*messages))
    received = [lax.ppermute(sends[k - 1], "tm", [(t, t ^ k) for t in range(times)]) for k in reversed(range(1, times))]
    received.reverse()

    def finish_body(*refs):
        finish_kernel(times, *refs)

    return pl.pallas_call(
        finish_body,
        out_shape=(shape(1, nx, ny, nz), shape(1, nx, ny, nz)),
        in_specs=vmem(3 + times - 1),
        out_specs=vmem(2),
        scratch_shapes=[pltpu.VMEM((nx * ny, nz // 2), F32)],
        name="finish",
    )(*pinned(fine_disp, fine_vel, old, *received))


def solution(mesh):
    in_specs = (
        P("tm", "slab", "groups", None),
        P("tm", "slab", "groups", None),
        P("slab", "groups", None),
        P("slab", "groups", None),
        P("slab", "groups", None),
    )
    out_specs = (P("tm", "slab", "groups", None), P("tm", "slab", "groups", None))
    return jax.shard_map(local, mesh=mesh, in_specs=in_specs, out_specs=out_specs, check_vma=False)
```

```python
import jax
import jax.numpy as jnp
from jax import lax
from jax.experimental import pallas as pl
from jax.experimental.pallas import tpu as pltpu
from jax.sharding import PartitionSpec as P

FINE_STEPS = 4
COARSE_STEPS = 2
KEEP = 0.95
HIGH = lax.Precision.HIGHEST
F32 = jnp.float32


def vmem(count):
    return [pl.BlockSpec(memory_space=pltpu.VMEM)] * count


def shape(*dims):
    return jax.ShapeDtypeStruct(dims, F32)


def resident(*dims):
    return pltpu.VMEM(dims, F32)


def pinned(*arrays):
    return [pltpu.with_memory_space_constraint(x, pltpu.VMEM) for x in arrays]


def dot(left, right, precision=HIGH):
    return lax.dot_general(left, right, (((1,), (0,)), ((), ())), precision=precision, preferred_element_type=F32)


def selector(rows, cols, down, across):
    row = lax.broadcasted_iota(jnp.int32, (rows, cols), 0) // down
    col = lax.broadcasted_iota(jnp.int32, (rows, cols), 1) // across
    return (row == col).astype(F32)


def around(flat, axis, period):
    size = flat.shape[axis]
    at = lax.broadcasted_iota(jnp.int32, flat.shape, axis) % period
    before = jnp.where(at == 0, 0.0, pltpu.roll(flat, 1, axis))
    after = jnp.where(at == period - 1, 0.0, pltpu.roll(flat, size - 1, axis))
    return before + after


def flat2(x):
    return x.reshape(x.shape[0] * x.shape[1], x.shape[2])


def box9(x):
    flat = flat2(x)
    flat = flat + around(flat, 0, x.shape[1])
    flat = flat + around(flat, 1, x.shape[2])
    return flat.reshape(x.shape)


def face4(x):
    flat = flat2(x)
    return (around(flat, 0, x.shape[1]) + around(flat, 1, x.shape[2])).reshape(x.shape)


def three(box):
    none = jnp.zeros_like(box[:1])
    return box + jnp.concatenate([none, box[:-1]], axis=0) + jnp.concatenate([box[1:], none], axis=0)


def push(stiff, boxes, disp):
    return stiff * ((boxes - disp) * (1.0 / 26.0) - disp)


def pull(stiff, faces, disp):
    return stiff * (faces * (1.0 / 6.0) - disp)


def coarse_step(disp, vel, stiff):
    mid = disp[1:-1]
    vel = KEEP * vel + pull(stiff, disp[:-2] + disp[2:] + face4(mid), mid)
    return mid + vel, vel


def restrict(x, scratch):
    planes, ny, nz = x.shape
    half = planes // 2
    pairs = x.reshape(half, 2, ny, nz)
    pairs = pairs[:, 0] + pairs[:, 1]
    thin = dot(flat2(pairs), selector(nz, nz // 2, 2, 1) * 0.125)
    rows = half * ny
    scratch[pl.ds(0, rows), :] = thin
    out = scratch[pl.ds(0, rows // 2, stride=2), :] + scratch[pl.ds(1, rows // 2, stride=2), :]
    return out.reshape(half, ny // 2, nz // 2)


def pack_kernel(disp, vel, stiff, press, tiles, own, coarse, send_a, send_b, scratch):
    nx, ny, nz = stiff.shape
    half = nx // 2
    slab = lax.axis_index("slab")
    start = disp[0]
    k = stiff[...]
    wet = flat2(tiles[...]).astype(F32)
    load = dot(wet, selector(tiles.shape[2], nz, 1, nz // tiles.shape[2])).reshape(nx, ny, nz) * press[...]
    boxes = box9(start)
    first = KEEP * vel[0] + load + push(k, three(boxes), start)
    moved = start + first
    inner = slice(1, nx - 1)
    box_moved = box9(moved[inner])
    near = jnp.concatenate([box_moved[:1] + box_moved[1:2], box_moved[-2:-1] + box_moved[-1:]], axis=0)
    spots = (1, nx - 2)

    def at(x):
        return jnp.concatenate([x[i : i + 1] for i in spots], axis=0)

    second = at(moved) + KEEP * at(first) + at(load) + push(at(k), near, at(moved))
    box_second = box9(second)

    fields = restrict(jnp.concatenate([start, vel[0], k], axis=0), scratch)
    wide_disp, wide_vel, wide_k = fields[:half], fields[half : 2 * half], fields[2 * half :]
    none = jnp.zeros_like(wide_disp[:1])
    faces = face4(wide_disp) + jnp.concatenate([none, wide_disp[:-1]], axis=0) + jnp.concatenate([wide_disp[1:], none], axis=0)
    wide_first = KEEP * wide_vel + pull(wide_k, faces, wide_disp)

    own[pl.ds(0, nx)] = start
    own[pl.ds(nx, nx)] = first
    own[pl.ds(2 * nx, nx)] = k
    own[pl.ds(3 * nx, nx)] = load
    coarse[pl.ds(0, half)] = wide_disp
    coarse[pl.ds(half, half)] = wide_first
    coarse[pl.ds(2 * half, half)] = wide_k

    def fill(target, edge, spot, end, which):
        share = k[edge] * (1.0 / 26.0)
        target[0] = start[edge]
        target[1] = first[edge]
        target[2] = k[edge]
        target[3] = load[edge] + share * box_moved[spot - 1]
        target[4] = load[edge] + share * box_second[which]
        target[5] = k[spot]
        cy, cz = ny // 2, nz // 2
        target[6, pl.ds(0, cy), pl.ds(0, cz)] = wide_disp[end]
        target[6, pl.ds(0, cy), pl.ds(cz, cz)] = wide_disp[end] + wide_first[end]
        target[6, pl.ds(cy, cy), pl.ds(0, cz)] = wide_k[end]
        target[6, pl.ds(cy, cy), pl.ds(cz, cz)] = wide_k[end]

    @pl.when(slab % 2 == 0)
    def _():
        fill(send_a, nx - 1, nx - 2, half - 1, 1)
        fill(send_b, 0, 1, 0, 0)

    @pl.when(slab % 2 == 1)
    def _():
        fill(send_a, 0, 1, 0, 0)
        fill(send_b, nx - 1, nx - 2, half - 1, 1)


def fine_kernel(count, own, coarse, recv_a, recv_b, fine_disp, fine_vel, message, old, scratch):
    nx, ny, nz = fine_disp.shape
    half = nx // 2
    slab = lax.axis_index("slab")
    even = slab % 2 == 0
    a, b = recv_a[...], recv_b[...]
    low = jnp.where(slab > 0, jnp.where(even, b, a), 0.0)
    high = jnp.where(slab < count - 1, jnp.where(even, a, b), 0.0)

    def outer(i):
        return jnp.concatenate([low[i : i + 1], high[i : i + 1]], axis=0)

    def joined(i, inner):
        return jnp.concatenate([low[i : i + 1], inner, high[i : i + 1]], axis=0)

    start = own[pl.ds(0, nx)]
    k = joined(2, own[pl.ds(2 * nx, nx)])
    load = own[pl.ds(3 * nx, nx)]
    disp = joined(0, start)
    box = box9(jnp.concatenate([disp[1:2], disp[:1], disp[-1:], disp[-2:-1]], axis=0))
    box = jnp.concatenate([box[:2], jnp.zeros_like(disp[2:-2]), box[2:]], axis=0)
    vel = joined(1, own[pl.ds(nx, nx)]) + k * (1.0 / 26.0) * box
    disp = disp + vel
    box = box9(disp)
    vel = KEEP * vel + joined(3, load) + push(k, three(box), disp)
    far = outer(5) * (1.0 / 26.0) * jnp.concatenate([box[:1], box[-1:]], axis=0)
    disp = disp + vel
    box = box9(jnp.concatenate([far[:1], disp, far[1:]], axis=0))
    boxes = box[:-2] + box[1:-1] + box[2:]
    vel = KEEP * vel + joined(4, load) + push(k, boxes, disp)
    disp = disp + vel
    box = box9(disp)
    boxes = box[:-2] + box[1:-1] + box[2:]
    vel = KEEP * vel[1:-1] + load + push(k[1:-1], boxes, disp[1:-1])
    disp = disp[1:-1] + vel
    fine_disp[...] = disp
    fine_vel[...] = vel
    rest = restrict(jnp.concatenate([disp, vel], axis=0), scratch)

    cy, cz = ny // 2, nz // 2
    wide_disp = coarse[pl.ds(0, half)]
    wide_k = coarse[pl.ds(2 * half, half)]
    out_disp = outer(6)[:, :cy, :cz]
    out_moved = outer(6)[:, :cy, cz:]
    out_k = outer(6)[:, cy:, :cz]
    none = [jnp.zeros_like(wide_disp[:1])] * (half - 2)
    ends = jnp.concatenate([out_disp[:1], *none, out_disp[1:]], axis=0)
    wide_vel = coarse[pl.ds(half, half)] + wide_k * (1.0 / 6.0) * ends
    inner = jnp.concatenate([wide_disp[:1], wide_disp[-1:]], axis=0)
    out_moved = out_moved + out_k * (1.0 / 6.0) * inner
    moved = jnp.concatenate([out_moved[:1], wide_disp + wide_vel, out_moved[1:]], axis=0)
    image_disp, image_vel = coarse_step(moved, wide_vel, wide_k)
    first = lax.axis_index("tm") == 0
    image_disp = jnp.where(first, 0.0, image_disp)
    image_vel = jnp.where(first, 0.0, image_vel)
    old[pl.ds(0, half)] = image_disp
    old[pl.ds(half, half)] = image_vel
    message[pl.ds(0, half)] = rest[:half] - image_disp
    message[pl.ds(half, half)] = rest[half:] - image_vel
    message[pl.ds(2 * half, half)] = wide_k


def chain_kernel(times, partners, *refs):
    inputs = refs[: len(partners)]
    outputs = refs[len(partners) : len(partners) + times - 1]
    window = refs[-1]
    half = inputs[0].shape[0] // 3
    slab = lax.axis_index("slab")
    reach = times - 1
    window[...] = jnp.zeros(window.shape, F32)
    for ref, place in zip(inputs, partners):
        at = (place(slab) - slab + reach) * half
        for field in range(3):
            window[field, pl.ds(at, half)] = ref[pl.ds(field * half, half)]
    disp, vel, stiff = window[0], window[1], window[2]
    powers = []
    for power in range(reach):
        for _ in range(COARSE_STEPS):
            disp, vel = coarse_step(disp, vel[1:-1], stiff[1:-1])
            stiff = stiff[1:-1]
        edge = (disp.shape[0] - half) // 2
        powers.append((disp[edge : edge + half], vel[edge : edge + half]))
    slot = lax.axis_index("tm")
    for k, output in zip(range(times - 1, 0, -1), outputs):
        gap = (slot ^ k) - slot
        pick_disp, pick_vel = powers[0]
        for power in range(1, reach):
            pick_disp = jnp.where(gap == power + 1, powers[power][0], pick_disp)
            pick_vel = jnp.where(gap == power + 1, powers[power][1], pick_vel)
        output[pl.ds(0, half)] = pick_disp
        output[pl.ds(half, half)] = pick_vel


def finish_kernel(times, *refs):
    fine_disp, fine_vel, old = refs[:3]
    received = refs[3 : 3 + times - 1]
    new_disp, new_vel = refs[3 + times - 1 : 5 + times - 1]
    tall = refs[-1]
    slot = lax.axis_index("tm")
    total = -old[...]
    for k, part in zip(range(times - 1, 0, -1), received):
        total = total + jnp.where((slot ^ k) < slot, part[...], 0.0)
    half2, cy, cz = total.shape
    rows = half2 * cy
    tall[pl.ds(0, rows, stride=2), :] = flat2(total)
    tall[pl.ds(1, rows, stride=2), :] = flat2(total)
    wide = dot(tall[...], selector(cz, 2 * cz, 1, 2)).reshape(half2, 2 * cy, 2 * cz)
    for i in range(fine_disp.shape[0]):
        new_disp[0, i] = fine_disp[i] + wide[i // 2]
        new_vel[0, i] = fine_vel[i] + wide[half2 // 2 + i // 2]


def local(start_disp, start_vel, stiffness, pressure, wet_tiles):
    slabs = lax.axis_size("slab")
    times = lax.axis_size("tm")
    _, nx, ny, nz = start_disp.shape
    half = nx // 2
    pair = ("slab", "tm")

    def at(s, t):
        return s * times + t

    low_pairs = [(at(s, t), at(s ^ 1, t)) for s in range(slabs) for t in range(times)]
    high_pairs = []
    for s in range(slabs):
        for t in range(times):
            if s == 0 or s == slabs - 1:
                high_pairs.append((at(s, t), at(s, t ^ 1)))
            else:
                high_pairs.append((at(s, t), at(s + 1 if s % 2 else s - 1, t)))

    packed = resident(7, ny, nz)
    coarse_cells = (ny // 2, nz // 2)
    own, coarse, send_a, send_b = pl.pallas_call(
        pack_kernel,
        out_shape=(resident(4 * nx, ny, nz), resident(3 * half, *coarse_cells), packed, packed),
        in_specs=vmem(5),
        out_specs=vmem(4),
        scratch_shapes=[pltpu.VMEM((3 * half * ny, nz // 2), F32)],
        name="pack",
    )(start_disp, start_vel, stiffness, pressure, wet_tiles)
    recv_a = lax.ppermute(send_a, pair, low_pairs)
    recv_b = lax.ppermute(send_b, pair, high_pairs)

    def fine_body(*refs):
        fine_kernel(slabs, *refs)

    grid = resident(nx, ny, nz)
    fine_disp, fine_vel, message, old = pl.pallas_call(
        fine_body,
        out_shape=(grid, grid, resident(3 * half, *coarse_cells), resident(2 * half, *coarse_cells)),
        in_specs=vmem(4),
        out_specs=vmem(4),
        scratch_shapes=[pltpu.VMEM((2 * half * ny, nz // 2), F32)],
        name="fine",
    )(*pinned(own, coarse, recv_a, recv_b))

    messages, places = [message], [lambda s: s]
    if slabs <= times and slabs & (slabs - 1) == 0:
        for k in range(1, slabs):
            messages.append(lax.ppermute(message, "slab", [(s, s ^ k) for s in range(slabs)]))
            places.append(lambda s, k=k: s ^ k)
    else:
        for k in range(1, times):
            for shift in (k, -k):
                route = [(s - shift, s) for s in range(slabs) if 0 <= s - shift < slabs]
                messages.append(lax.ppermute(message, "slab", route))
                places.append(lambda s, shift=shift: s - shift)

    def chain_body(*refs):
        chain_kernel(times, places, *refs)

    link = resident(2 * half, ny // 2, nz // 2)
    sends = pl.pallas_call(
        chain_body,
        out_shape=(link,) * (times - 1),
        in_specs=vmem(len(messages)),
        out_specs=vmem(times - 1),
        scratch_shapes=[pltpu.VMEM((3, (2 * times - 1) * half, ny // 2, nz // 2), F32)],
        name="chain",
    )(*pinned(*messages))
    jumps = list(range(times - 1, 0, -1))
    received = [lax.ppermute(send, "tm", [(t, t ^ k) for t in range(times)]) for k, send in zip(jumps, sends)]

    def finish_body(*refs):
        finish_kernel(times, *refs)

    return pl.pallas_call(
        finish_body,
        out_shape=(shape(1, nx, ny, nz), shape(1, nx, ny, nz)),
        in_specs=vmem(3 + times - 1),
        out_specs=vmem(2),
        scratch_shapes=[pltpu.VMEM((nx * ny, nz // 2), F32)],
        name="finish",
    )(*pinned(fine_disp, fine_vel, old, *received))


def solution(mesh):
    in_specs = (
        P("tm", "slab", "groups", None),
        P("tm", "slab", "groups", None),
        P("slab", "groups", None),
        P("slab", "groups", None),
        P("slab", "groups", None),
    )
    out_specs = (P("tm", "slab", "groups", None), P("tm", "slab", "groups", None))
    return jax.shard_map(local, mesh=mesh, in_specs=in_specs, out_specs=out_specs, check_vma=False)
```

```python
import jax
import jax.numpy as jnp
from jax import lax
from jax.experimental import pallas as pl
from jax.experimental.pallas import tpu as pltpu
from jax.sharding import PartitionSpec as P

FINE_STEPS = 4
COARSE_STEPS = 2
KEEP = 0.95
F32 = jnp.float32


def vmem(count):
    return [pl.BlockSpec(memory_space=pltpu.VMEM)] * count


def shape(*dims):
    return jax.ShapeDtypeStruct(dims, F32)


def resident(*dims):
    return pltpu.VMEM(dims, F32)


def pinned(*arrays):
    return [pltpu.with_memory_space_constraint(x, pltpu.VMEM) for x in arrays]


def dot(left, right):
    return lax.dot_general(left, right, (((1,), (0,)), ((), ())), preferred_element_type=F32)


def pick(x, selected):
    high = x.astype(jnp.bfloat16)
    rest = x - high.astype(F32)
    mid = rest.astype(jnp.bfloat16)
    low = (rest - mid.astype(F32)).astype(jnp.bfloat16)
    return dot(high, selected) + (dot(mid, selected) + dot(low, selected))


def selector(rows, cols, down, across, value=1.0):
    row = lax.shift_right_logical(lax.broadcasted_iota(jnp.int32, (rows, cols), 0), down)
    col = lax.shift_right_logical(lax.broadcasted_iota(jnp.int32, (rows, cols), 1), across)
    return jnp.where(row == col, value, 0.0).astype(jnp.bfloat16)


def flat2(x):
    return x.reshape(x.shape[0] * x.shape[1], x.shape[2])


def around(x, axis):
    size = x.shape[axis]
    flat = flat2(x)
    at = lax.broadcasted_iota(jnp.int32, x.shape, axis)
    before = pltpu.roll(flat, 1, axis - 1).reshape(x.shape)
    after = pltpu.roll(flat, flat.shape[axis - 1] - 1, axis - 1).reshape(x.shape)
    return jnp.where(at == 0, 0.0, before) + jnp.where(at == size - 1, 0.0, after)


def box9(x):
    x = x + around(x, 1)
    return x + around(x, 2)


def face4(x):
    return around(x, 1) + around(x, 2)


def three(box):
    none = jnp.zeros_like(box[:1])
    return box + jnp.concatenate([none, box[:-1]], axis=0) + jnp.concatenate([box[1:], none], axis=0)


def push(stiff, boxes, disp):
    return stiff * ((boxes - disp) * (1.0 / 26.0) - disp)


def pull(stiff, faces, disp):
    return stiff * (faces * (1.0 / 6.0) - disp)


def coarse_step(disp, vel, stiff):
    mid = disp[1:-1]
    vel = KEEP * vel + pull(stiff, disp[:-2] + disp[2:] + face4(mid), mid)
    return mid + vel, vel


def restrict(x, scratch):
    planes, ny, nz = x.shape
    half = planes // 2
    pairs = x.reshape(half, 2, ny, nz)
    pairs = pairs[:, 0] + pairs[:, 1]
    thin = pick(flat2(pairs), selector(nz, nz // 2, 1, 0, 0.125))
    rows = half * ny
    scratch[pl.ds(0, rows), :] = thin
    out = scratch[pl.ds(0, rows // 2, stride=2), :] + scratch[pl.ds(1, rows // 2, stride=2), :]
    return out.reshape(half, ny // 2, nz // 2)


def pack_kernel(disp, vel, stiff, press, tiles, own, coarse, send_a, send_b, scratch, vel_in, press_in, tiles_in, sems):
    nx, ny, nz = stiff.shape
    half = nx // 2
    moves = [
        pltpu.make_async_copy(disp.at[0], own.at[pl.ds(0, nx)], sems.at[0]),
        pltpu.make_async_copy(stiff, own.at[pl.ds(2 * nx, nx)], sems.at[1]),
        pltpu.make_async_copy(vel.at[0], vel_in, sems.at[2]),
        pltpu.make_async_copy(tiles, tiles_in, sems.at[3]),
        pltpu.make_async_copy(press, press_in, sems.at[4]),
    ]
    for move in moves:
        move.start()
    slab = lax.axis_index("slab")
    for move in moves:
        move.wait()
    start = own[pl.ds(0, nx)]
    k = own[pl.ds(2 * nx, nx)]
    speed = vel_in[...]
    wet = flat2(tiles_in[...]).astype(F32).astype(jnp.bfloat16)
    shift = (nz // tiles.shape[2]).bit_length() - 1
    load = dot(wet, selector(tiles.shape[2], nz, 0, shift)).reshape(nx, ny, nz) * press_in[...]
    boxes = box9(start)
    first = KEEP * speed + load + push(k, three(boxes), start)
    moved = start + first
    inner = slice(1, nx - 1)
    box_moved = box9(moved[inner])
    near = jnp.concatenate([box_moved[:1] + box_moved[1:2], box_moved[-2:-1] + box_moved[-1:]], axis=0)
    spots = (1, nx - 2)

    def at(x):
        return jnp.concatenate([x[i : i + 1] for i in spots], axis=0)

    second = at(moved) + KEEP * at(first) + at(load) + push(at(k), near, at(moved))
    box_second = box9(second)

    fields = restrict(jnp.concatenate([start, speed, k], axis=0), scratch)
    wide_disp, wide_vel, wide_k = fields[:half], fields[half : 2 * half], fields[2 * half :]
    none = jnp.zeros_like(wide_disp[:1])
    faces = face4(wide_disp) + jnp.concatenate([none, wide_disp[:-1]], axis=0) + jnp.concatenate([wide_disp[1:], none], axis=0)
    wide_first = KEEP * wide_vel + pull(wide_k, faces, wide_disp)

    own[pl.ds(nx, nx)] = first
    own[pl.ds(3 * nx, nx)] = load
    coarse[pl.ds(0, half)] = wide_disp
    coarse[pl.ds(half, half)] = wide_first
    coarse[pl.ds(2 * half, half)] = wide_k

    def fill(target, edge, spot, end, which):
        share = k[edge] * (1.0 / 26.0)
        target[0] = start[edge]
        target[1] = first[edge]
        target[2] = k[edge]
        target[3] = load[edge] + share * box_moved[spot - 1]
        target[4] = load[edge] + share * box_second[which]
        target[5] = k[spot]
        cy, cz = ny // 2, nz // 2
        target[6, pl.ds(0, cy), pl.ds(0, cz)] = wide_disp[end]
        target[6, pl.ds(0, cy), pl.ds(cz, cz)] = wide_disp[end] + wide_first[end]
        target[6, pl.ds(cy, cy), pl.ds(0, cz)] = wide_k[end]
        target[6, pl.ds(cy, cy), pl.ds(cz, cz)] = wide_k[end]

    @pl.when(slab % 2 == 0)
    def _():
        fill(send_a, nx - 1, nx - 2, half - 1, 1)
        fill(send_b, 0, 1, 0, 0)

    @pl.when(slab % 2 == 1)
    def _():
        fill(send_a, 0, 1, 0, 0)
        fill(send_b, nx - 1, nx - 2, half - 1, 1)


def fine_kernel(count, own, coarse, recv_a, recv_b, fine_disp, fine_vel, message, old, scratch):
    nx, ny, nz = fine_disp.shape
    half = nx // 2
    slab = lax.axis_index("slab")
    even = slab % 2 == 0
    a, b = recv_a[...], recv_b[...]
    low = jnp.where(slab > 0, jnp.where(even, b, a), 0.0)
    high = jnp.where(slab < count - 1, jnp.where(even, a, b), 0.0)

    def outer(i):
        return jnp.concatenate([low[i : i + 1], high[i : i + 1]], axis=0)

    def joined(i, inner):
        return jnp.concatenate([low[i : i + 1], inner, high[i : i + 1]], axis=0)

    start = own[pl.ds(0, nx)]
    k = joined(2, own[pl.ds(2 * nx, nx)])
    load = own[pl.ds(3 * nx, nx)]
    disp = joined(0, start)
    box = box9(jnp.concatenate([disp[1:2], disp[:1], disp[-1:], disp[-2:-1]], axis=0))
    box = jnp.concatenate([box[:2], jnp.zeros_like(disp[2:-2]), box[2:]], axis=0)
    vel = joined(1, own[pl.ds(nx, nx)]) + k * (1.0 / 26.0) * box
    disp = disp + vel
    box = box9(disp)
    vel = KEEP * vel + joined(3, load) + push(k, three(box), disp)
    far = outer(5) * (1.0 / 26.0) * jnp.concatenate([box[:1], box[-1:]], axis=0)
    disp = disp + vel
    box = box9(jnp.concatenate([far[:1], disp, far[1:]], axis=0))
    boxes = box[:-2] + box[1:-1] + box[2:]
    vel = KEEP * vel + joined(4, load) + push(k, boxes, disp)
    disp = disp + vel
    box = box9(disp)
    boxes = box[:-2] + box[1:-1] + box[2:]
    vel = KEEP * vel[1:-1] + load + push(k[1:-1], boxes, disp[1:-1])
    disp = disp[1:-1] + vel
    fine_disp[...] = disp
    fine_vel[...] = vel
    rest = restrict(jnp.concatenate([disp, vel], axis=0), scratch)

    cy, cz = ny // 2, nz // 2
    wide_disp = coarse[pl.ds(0, half)]
    wide_k = coarse[pl.ds(2 * half, half)]
    out_disp = outer(6)[:, :cy, :cz]
    out_moved = outer(6)[:, :cy, cz:]
    out_k = outer(6)[:, cy:, :cz]
    none = [jnp.zeros_like(wide_disp[:1])] * (half - 2)
    ends = jnp.concatenate([out_disp[:1], *none, out_disp[1:]], axis=0)
    wide_vel = coarse[pl.ds(half, half)] + wide_k * (1.0 / 6.0) * ends
    inner = jnp.concatenate([wide_disp[:1], wide_disp[-1:]], axis=0)
    out_moved = out_moved + out_k * (1.0 / 6.0) * inner
    moved = jnp.concatenate([out_moved[:1], wide_disp + wide_vel, out_moved[1:]], axis=0)
    image_disp, image_vel = coarse_step(moved, wide_vel, wide_k)
    first = lax.axis_index("tm") == 0
    image_disp = jnp.where(first, 0.0, image_disp)
    image_vel = jnp.where(first, 0.0, image_vel)
    old[pl.ds(0, half)] = image_disp
    old[pl.ds(half, half)] = image_vel
    message[pl.ds(0, half)] = rest[:half] - image_disp
    message[pl.ds(half, half)] = rest[half:] - image_vel
    message[pl.ds(2 * half, half)] = wide_k


def chain_kernel(times, jumps, partners, *refs):
    inputs = refs[: len(partners)]
    outputs = refs[len(partners) : len(partners) + len(jumps)]
    window = refs[-1]
    half = inputs[0].shape[0] // 3
    slab = lax.axis_index("slab")
    reach = times - 1
    window[...] = jnp.zeros(window.shape, F32)
    for ref, place in zip(inputs, partners):
        at = (place(slab) - slab + reach) * half
        for field in range(3):
            window[field, pl.ds(at, half)] = ref[pl.ds(field * half, half)]
    disp, vel, stiff = window[0], window[1], window[2]
    powers = []
    for power in range(reach):
        for _ in range(COARSE_STEPS):
            disp, vel = coarse_step(disp, vel[1:-1], stiff[1:-1])
            stiff = stiff[1:-1]
        edge = (disp.shape[0] - half) // 2
        powers.append((disp[edge : edge + half], vel[edge : edge + half]))
    slot = lax.axis_index("tm")
    for k, output in zip(jumps, outputs):
        gap = (slot ^ k) - (slot ^ 1)
        pick_disp, pick_vel = powers[0]
        for power in range(1, reach):
            pick_disp = jnp.where(gap == power + 1, powers[power][0], pick_disp)
            pick_vel = jnp.where(gap == power + 1, powers[power][1], pick_vel)
        output[pl.ds(0, half)] = pick_disp
        output[pl.ds(half, half)] = pick_vel


def finish_kernel(jumps, *refs):
    fine_disp, fine_vel, old = refs[:3]
    parts = refs[3 : 3 + len(jumps)]
    new_disp, new_vel = refs[3 + len(jumps) : 5 + len(jumps)]
    tall = refs[-1]
    slot = lax.axis_index("tm")
    total = -old[...]
    for k, part in zip(jumps, parts):
        total = total + jnp.where((slot ^ k ^ 1) < slot, part[...], 0.0)
    half2, cy, cz = total.shape
    rows = half2 * cy
    tall[pl.ds(0, rows, stride=2), :] = flat2(total)
    tall[pl.ds(1, rows, stride=2), :] = flat2(total)
    wide = pick(tall[...], selector(cz, 2 * cz, 0, 1)).reshape(half2, 2 * cy, 2 * cz)
    for i in range(fine_disp.shape[0]):
        new_disp[0, i] = fine_disp[i] + wide[i // 2]
        new_vel[0, i] = fine_vel[i] + wide[half2 // 2 + i // 2]


def local(start_disp, start_vel, stiffness, pressure, wet_tiles):
    slabs = lax.axis_size("slab")
    times = lax.axis_size("tm")
    _, nx, ny, nz = start_disp.shape
    half = nx // 2
    pair = ("slab", "tm")

    def at(s, t):
        return s * times + t

    low_pairs = [(at(s, t), at(s ^ 1, t)) for s in range(slabs) for t in range(times)]
    high_pairs = []
    for s in range(slabs):
        for t in range(times):
            if s == 0 or s == slabs - 1:
                high_pairs.append((at(s, t), at(s, t ^ 1)))
            else:
                high_pairs.append((at(s, t), at(s + 1 if s % 2 else s - 1, t)))

    packed = resident(7, ny, nz)
    coarse_cells = (ny // 2, nz // 2)
    own, coarse, send_a, send_b = pl.pallas_call(
        pack_kernel,
        out_shape=(resident(4 * nx, ny, nz), resident(3 * half, *coarse_cells), packed, packed),
        in_specs=[pl.BlockSpec(memory_space=pl.ANY)] * 5,
        out_specs=vmem(4),
        scratch_shapes=[
            pltpu.VMEM((3 * half * ny, nz // 2), F32),
            pltpu.VMEM((nx, ny, nz), F32),
            pltpu.VMEM((nx, ny, nz), F32),
            pltpu.VMEM(wet_tiles.shape, jnp.int32),
            pltpu.SemaphoreType.DMA((5,)),
        ],
        name="pack",
    )(start_disp, start_vel, stiffness, pressure, wet_tiles)
    recv_a = lax.ppermute(send_a, pair, low_pairs)
    recv_b = lax.ppermute(send_b, pair, high_pairs)

    def fine_body(*refs):
        fine_kernel(slabs, *refs)

    grid = resident(nx, ny, nz)
    fine_disp, fine_vel, message, old = pl.pallas_call(
        fine_body,
        out_shape=(grid, grid, resident(3 * half, *coarse_cells), resident(2 * half, *coarse_cells)),
        in_specs=vmem(4),
        out_specs=vmem(4),
        scratch_shapes=[pltpu.VMEM((2 * half * ny, nz // 2), F32)],
        name="fine",
    )(*pinned(own, coarse, recv_a, recv_b))

    messages, places = [], []
    if slabs <= times and slabs & (slabs - 1) == 0:
        for k in range(slabs):
            route = [(at(s, t), at(s ^ k, t ^ 1)) for s in range(slabs) for t in range(times)]
            messages.append(lax.ppermute(message, pair, route))
            places.append(lambda s, k=k: s ^ k)
    else:
        for shift in range(1 - times, times):
            route = [(at(s - shift, t ^ 1), at(s, t)) for s in range(slabs) if 0 <= s - shift < slabs for t in range(times)]
            messages.append(lax.ppermute(message, pair, route))
            places.append(lambda s, shift=shift: s - shift)

    jumps = [*range(2, times), 0]

    def chain_body(*refs):
        chain_kernel(times, jumps, places, *refs)

    link = resident(2 * half, *coarse_cells)
    sends = pl.pallas_call(
        chain_body,
        out_shape=(link,) * len(jumps),
        in_specs=vmem(len(messages)),
        out_specs=vmem(len(jumps)),
        scratch_shapes=[pltpu.VMEM((3, (2 * times - 1) * half, *coarse_cells), F32)],
        name="chain",
    )(*pinned(*messages))
    parts = [lax.ppermute(send, "tm", [(t, t ^ k) for t in range(times)]) for k, send in zip(jumps[:-1], sends)]

    def finish_body(*refs):
        finish_kernel(jumps, *refs)

    return pl.pallas_call(
        finish_body,
        out_shape=(shape(1, nx, ny, nz), shape(1, nx, ny, nz)),
        in_specs=vmem(3 + len(jumps)),
        out_specs=vmem(2),
        scratch_shapes=[pltpu.VMEM((nx * ny, nz // 2), F32)],
        name="finish",
    )(*pinned(fine_disp, fine_vel, old, *parts, sends[-1]))


def solution(mesh):
    in_specs = (
        P("tm", "slab", "groups", None),
        P("tm", "slab", "groups", None),
        P("slab", "groups", None),
        P("slab", "groups", None),
        P("slab", "groups", None),
    )
    out_specs = (P("tm", "slab", "groups", None), P("tm", "slab", "groups", None))
    return jax.shard_map(local, mesh=mesh, in_specs=in_specs, out_specs=out_specs, check_vma=False)
```

```python
import jax
import jax.numpy as jnp
from jax import lax
from jax.experimental import pallas as pl
from jax.experimental.pallas import tpu as pltpu
from jax.sharding import PartitionSpec as P

FINE_STEPS = 4
COARSE_STEPS = 2
KEEP = 0.95
F32 = jnp.float32


def vmem(count):
    return [pl.BlockSpec(memory_space=pltpu.VMEM)] * count


def shape(*dims):
    return jax.ShapeDtypeStruct(dims, F32)


def resident(*dims):
    return pltpu.VMEM(dims, F32)


def pinned(*arrays):
    return [pltpu.with_memory_space_constraint(x, pltpu.VMEM) for x in arrays]


def dot(left, right):
    return lax.dot_general(left, right, (((1,), (0,)), ((), ())), preferred_element_type=F32)


def selector(rows, cols, down, across, value=1.0):
    row = lax.shift_right_logical(lax.broadcasted_iota(jnp.int32, (rows, cols), 0), down)
    col = lax.shift_right_logical(lax.broadcasted_iota(jnp.int32, (rows, cols), 1), across)
    return jnp.where(row == col, value, 0.0).astype(jnp.bfloat16)


def flat2(x):
    return x.reshape(x.shape[0] * x.shape[1], x.shape[2])


def around(x, axis):
    size = x.shape[axis]
    none = jnp.zeros_like(lax.slice_in_dim(x, 0, 1, axis=axis))
    before = jnp.concatenate([none, lax.slice_in_dim(x, 0, size - 1, axis=axis)], axis)
    after = jnp.concatenate([lax.slice_in_dim(x, 1, size, axis=axis), none], axis)
    return before + after


def box9(x):
    x = x + around(x, 1)
    return x + around(x, 2)


def face4(x):
    return around(x, 1) + around(x, 2)


def three(box):
    none = jnp.zeros_like(box[:1])
    return box + jnp.concatenate([none, box[:-1]], axis=0) + jnp.concatenate([box[1:], none], axis=0)


def push(stiff, boxes, disp):
    return stiff * ((boxes - disp) * (1.0 / 26.0) - disp)


def pull(stiff, faces, disp):
    return stiff * (faces * (1.0 / 6.0) - disp)


def coarse_step(disp, vel, stiff):
    mid = disp[1:-1]
    vel = KEEP * vel + pull(stiff, disp[:-2] + disp[2:] + face4(mid), mid)
    return mid + vel, vel


def restrict(x, left, right):
    planes, ny, nz = x.shape
    half, lanes = planes // 2, nz // 2
    pairs = x.reshape(half, 2, ny, nz)
    pairs = flat2(pairs[:, 0] + pairs[:, 1])
    rows = half * ny
    lane = lax.broadcasted_iota(jnp.int32, (rows // 2, lanes), 1)
    even = (lane * 2) & (lanes - 1)

    def squeeze(scratch, part):
        scratch[pl.ds(0, rows), :] = part
        both = scratch[pl.ds(0, rows // 2, stride=2), :] + scratch[pl.ds(1, rows // 2, stride=2), :]
        return jnp.take_along_axis(both, even, axis=1) + jnp.take_along_axis(both, even + 1, axis=1)

    out = jnp.where(lane < lanes // 2, squeeze(left, pairs[:, :lanes]), squeeze(right, pairs[:, lanes:]))
    return (0.125 * out).reshape(half, ny // 2, lanes)


def pack_kernel(disp, vel, stiff, press, tiles, own, coarse, send_a, send_b, left, right, vel_in, press_in, tiles_in, sems):
    nx, ny, nz = stiff.shape
    half = nx // 2
    moves = [
        pltpu.make_async_copy(disp.at[0], own.at[pl.ds(0, nx)], sems.at[0]),
        pltpu.make_async_copy(stiff, own.at[pl.ds(2 * nx, nx)], sems.at[1]),
        pltpu.make_async_copy(vel.at[0], vel_in, sems.at[2]),
        pltpu.make_async_copy(tiles, tiles_in, sems.at[3]),
        pltpu.make_async_copy(press, press_in, sems.at[4]),
    ]
    for move in moves:
        move.start()
    slab = lax.axis_index("slab")
    for move in moves:
        move.wait()
    start = own[pl.ds(0, nx)]
    k = own[pl.ds(2 * nx, nx)]
    speed = vel_in[...]
    wet = flat2(tiles_in[...]).astype(F32).astype(jnp.bfloat16)
    shift = (nz // tiles.shape[2]).bit_length() - 1
    load = dot(wet, selector(tiles.shape[2], nz, 0, shift)).reshape(nx, ny, nz) * press_in[...]
    boxes = box9(start)
    first = KEEP * speed + load + push(k, three(boxes), start)
    moved = start + first
    inner = slice(1, nx - 1)
    box_moved = box9(moved[inner])
    near = jnp.concatenate([box_moved[:1] + box_moved[1:2], box_moved[-2:-1] + box_moved[-1:]], axis=0)
    spots = (1, nx - 2)

    def at(x):
        return jnp.concatenate([x[i : i + 1] for i in spots], axis=0)

    second = KEEP * at(first) + at(load) + push(at(k), near, at(moved))

    fields = restrict(jnp.concatenate([start, speed, k], axis=0), left, right)
    wide_disp, wide_vel, wide_k = fields[:half], fields[half : 2 * half], fields[2 * half :]
    none = jnp.zeros_like(wide_disp[:1])
    faces = face4(wide_disp) + jnp.concatenate([none, wide_disp[:-1]], axis=0) + jnp.concatenate([wide_disp[1:], none], axis=0)
    wide_first = KEEP * wide_vel + pull(wide_k, faces, wide_disp)

    own[pl.ds(nx, nx)] = first
    own[pl.ds(3 * nx, nx)] = load
    coarse[pl.ds(0, half)] = wide_disp
    coarse[pl.ds(half, half)] = wide_first
    coarse[pl.ds(2 * half, half)] = wide_k

    def fill(target, edge, spot, end, which):
        share = k[edge] * (1.0 / 26.0)
        target[0] = start[edge]
        target[1] = first[edge]
        target[2] = k[edge]
        target[3] = load[edge] + share * box_moved[spot - 1]
        target[4] = second[which]
        target[5] = k[spot]
        cy, cz = ny // 2, nz // 2
        target[6, pl.ds(0, cy), pl.ds(0, cz)] = wide_disp[end]
        target[6, pl.ds(0, cy), pl.ds(cz, cz)] = wide_disp[end] + wide_first[end]
        target[6, pl.ds(cy, cy), pl.ds(0, cz)] = wide_k[end]
        target[6, pl.ds(cy, cy), pl.ds(cz, cz)] = wide_k[end]

    @pl.when(slab % 2 == 0)
    def _():
        fill(send_a, nx - 1, nx - 2, half - 1, 1)
        fill(send_b, 0, 1, 0, 0)

    @pl.when(slab % 2 == 1)
    def _():
        fill(send_a, 0, 1, 0, 0)
        fill(send_b, nx - 1, nx - 2, half - 1, 1)


def fine_kernel(count, own, coarse, recv_a, recv_b, fine_disp, fine_vel, message, old, left, right):
    nx, ny, nz = fine_disp.shape
    half = nx // 2
    slab = lax.axis_index("slab")
    even = slab % 2 == 0
    a, b = recv_a[...], recv_b[...]
    low = jnp.where(slab > 0, jnp.where(even, b, a), 0.0)
    high = jnp.where(slab < count - 1, jnp.where(even, a, b), 0.0)

    def outer(i):
        return jnp.concatenate([low[i : i + 1], high[i : i + 1]], axis=0)

    def joined(i, inner):
        return jnp.concatenate([low[i : i + 1], inner, high[i : i + 1]], axis=0)

    start = own[pl.ds(0, nx)]
    k = joined(2, own[pl.ds(2 * nx, nx)])
    load = own[pl.ds(3 * nx, nx)]
    disp = joined(0, start)
    box = box9(jnp.concatenate([disp[1:2], disp[:1], disp[-1:], disp[-2:-1]], axis=0))
    box = jnp.concatenate([box[:2], jnp.zeros_like(disp[2:-2]), box[2:]], axis=0)
    vel = joined(1, own[pl.ds(nx, nx)]) + k * (1.0 / 26.0) * box
    disp = disp + vel
    box = box9(disp)
    vel = KEEP * vel + joined(3, load) + push(k, three(box), disp)
    far = outer(4) + outer(5) * (1.0 / 26.0) * jnp.concatenate([box[:1], box[-1:]], axis=0)
    disp = disp + vel
    box = box9(jnp.concatenate([far[:1], disp, far[1:]], axis=0))
    boxes = box[:-2] + box[1:-1] + box[2:]
    vel = KEEP * vel + joined(3, load) + push(k, boxes, disp)
    disp = disp + vel
    box = box9(disp)
    boxes = box[:-2] + box[1:-1] + box[2:]
    vel = KEEP * vel[1:-1] + load + push(k[1:-1], boxes, disp[1:-1])
    disp = disp[1:-1] + vel
    fine_disp[...] = disp
    fine_vel[...] = vel
    rest = restrict(jnp.concatenate([disp, vel], axis=0), left, right)

    cy, cz = ny // 2, nz // 2
    wide_disp = coarse[pl.ds(0, half)]
    wide_k = coarse[pl.ds(2 * half, half)]
    out_disp = outer(6)[:, :cy, :cz]
    out_moved = outer(6)[:, :cy, cz:]
    out_k = outer(6)[:, cy:, :cz]
    none = [jnp.zeros_like(wide_disp[:1])] * (half - 2)
    ends = jnp.concatenate([out_disp[:1], *none, out_disp[1:]], axis=0)
    wide_vel = coarse[pl.ds(half, half)] + wide_k * (1.0 / 6.0) * ends
    inner = jnp.concatenate([wide_disp[:1], wide_disp[-1:]], axis=0)
    out_moved = out_moved + out_k * (1.0 / 6.0) * inner
    moved = jnp.concatenate([out_moved[:1], wide_disp + wide_vel, out_moved[1:]], axis=0)
    image_disp, image_vel = coarse_step(moved, wide_vel, wide_k)
    first = lax.axis_index("tm") == 0
    image_disp = jnp.where(first, 0.0, image_disp)
    image_vel = jnp.where(first, 0.0, image_vel)
    old[pl.ds(0, half)] = image_disp
    old[pl.ds(half, half)] = image_vel
    message[pl.ds(0, half)] = rest[:half] - image_disp
    message[pl.ds(half, half)] = rest[half:] - image_vel
    message[pl.ds(2 * half, half)] = wide_k


def chain_kernel(times, jumps, partners, *refs):
    inputs = refs[: len(partners)]
    outputs = refs[len(partners) : len(partners) + len(jumps)]
    window = refs[-1]
    half = inputs[0].shape[0] // 3
    slab = lax.axis_index("slab")
    reach = times - 1
    window[...] = jnp.zeros(window.shape, F32)
    for ref, place in zip(inputs, partners):
        at = (place(slab) - slab + reach) * half
        for field in range(3):
            window[field, pl.ds(at, half)] = ref[pl.ds(field * half, half)]
    disp, vel, stiff = window[0], window[1], window[2]
    powers = []
    for power in range(reach):
        for _ in range(COARSE_STEPS):
            disp, vel = coarse_step(disp, vel[1:-1], stiff[1:-1])
            stiff = stiff[1:-1]
        edge = (disp.shape[0] - half) // 2
        powers.append((disp[edge : edge + half], vel[edge : edge + half]))
    slot = lax.axis_index("tm")
    for k, output in zip(jumps, outputs):
        gap = (slot ^ k) - (slot ^ 1)
        pick_disp, pick_vel = powers[0]
        for power in range(1, reach):
            pick_disp = jnp.where(gap == power + 1, powers[power][0], pick_disp)
            pick_vel = jnp.where(gap == power + 1, powers[power][1], pick_vel)
        output[pl.ds(0, half)] = pick_disp
        output[pl.ds(half, half)] = pick_vel


def finish_kernel(jumps, *refs):
    fine_disp, fine_vel, old = refs[:3]
    parts = refs[3 : 3 + len(jumps)]
    new_disp, new_vel = refs[3 + len(jumps) : 5 + len(jumps)]
    left, right = refs[-2:]
    slot = lax.axis_index("tm")
    total = -old[...]
    for k, part in zip(jumps, parts):
        total = total + jnp.where((slot ^ k ^ 1) < slot, part[...], 0.0)
    half2, cy, cz = total.shape
    rows = half2 * cy
    flat = flat2(total)
    lane = lax.broadcasted_iota(jnp.int32, flat.shape, 1) >> 1
    for scratch, part in ((left, lane), (right, lane + cz // 2)):
        part = jnp.take_along_axis(flat, part, axis=1)
        scratch[pl.ds(0, rows, stride=2), :] = part
        scratch[pl.ds(1, rows, stride=2), :] = part
    wide = jnp.concatenate([left[...], right[...]], axis=1).reshape(half2, 2 * cy, 2 * cz)
    for i in range(fine_disp.shape[0]):
        new_disp[0, i] = fine_disp[i] + wide[i // 2]
        new_vel[0, i] = fine_vel[i] + wide[half2 // 2 + i // 2]


def local(start_disp, start_vel, stiffness, pressure, wet_tiles):
    slabs = lax.axis_size("slab")
    times = lax.axis_size("tm")
    _, nx, ny, nz = start_disp.shape
    half = nx // 2
    pair = ("slab", "tm")

    def at(s, t):
        return s * times + t

    low_pairs = [(at(s, t), at(s ^ 1, t)) for s in range(slabs) for t in range(times)]
    high_pairs = []
    for s in range(slabs):
        for t in range(times):
            if s == 0 or s == slabs - 1:
                high_pairs.append((at(s, t), at(s, t ^ 1)))
            else:
                high_pairs.append((at(s, t), at(s + 1 if s % 2 else s - 1, t)))

    packed = resident(7, ny, nz)
    coarse_cells = (ny // 2, nz // 2)
    own, coarse, send_a, send_b = pl.pallas_call(
        pack_kernel,
        out_shape=(resident(4 * nx, ny, nz), resident(3 * half, *coarse_cells), packed, packed),
        in_specs=[pl.BlockSpec(memory_space=pl.ANY)] * 5,
        out_specs=vmem(4),
        scratch_shapes=[
            pltpu.VMEM((3 * half * ny, nz // 2), F32),
            pltpu.VMEM((3 * half * ny, nz // 2), F32),
            pltpu.VMEM((nx, ny, nz), F32),
            pltpu.VMEM((nx, ny, nz), F32),
            pltpu.VMEM(wet_tiles.shape, jnp.int32),
            pltpu.SemaphoreType.DMA((5,)),
        ],
        name="pack",
    )(start_disp, start_vel, stiffness, pressure, wet_tiles)
    recv_a = lax.ppermute(send_a, pair, low_pairs)
    recv_b = lax.ppermute(send_b, pair, high_pairs)

    def fine_body(*refs):
        fine_kernel(slabs, *refs)

    grid = resident(nx, ny, nz)
    fine_disp, fine_vel, message, old = pl.pallas_call(
        fine_body,
        out_shape=(grid, grid, resident(3 * half, *coarse_cells), resident(2 * half, *coarse_cells)),
        in_specs=vmem(4),
        out_specs=vmem(4),
        scratch_shapes=[pltpu.VMEM((2 * half * ny, nz // 2), F32)] * 2,
        name="fine",
    )(*pinned(own, coarse, recv_a, recv_b))

    messages, places = [], []
    if slabs <= times and slabs & (slabs - 1) == 0:
        for k in range(slabs):
            route = [(at(s, t), at(s ^ k, t ^ 1)) for s in range(slabs) for t in range(times)]
            messages.append(lax.ppermute(message, pair, route))
            places.append(lambda s, k=k: s ^ k)
    else:
        for shift in range(1 - times, times):
            route = [(at(s - shift, t ^ 1), at(s, t)) for s in range(slabs) if 0 <= s - shift < slabs for t in range(times)]
            messages.append(lax.ppermute(message, pair, route))
            places.append(lambda s, shift=shift: s - shift)

    jumps = [*range(2, times), 0]

    def chain_body(*refs):
        chain_kernel(times, jumps, places, *refs)

    link = resident(2 * half, *coarse_cells)
    sends = pl.pallas_call(
        chain_body,
        out_shape=(link,) * len(jumps),
        in_specs=vmem(len(messages)),
        out_specs=vmem(len(jumps)),
        scratch_shapes=[pltpu.VMEM((3, (2 * times - 1) * half, *coarse_cells), F32)],
        name="chain",
    )(*pinned(*messages))
    parts = [lax.ppermute(send, "tm", [(t, t ^ k) for t in range(times)]) for k, send in zip(jumps[:-1], sends)]

    def finish_body(*refs):
        finish_kernel(jumps, *refs)

    return pl.pallas_call(
        finish_body,
        out_shape=(shape(1, nx, ny, nz), shape(1, nx, ny, nz)),
        in_specs=vmem(3 + len(jumps)),
        out_specs=vmem(2),
        scratch_shapes=[pltpu.VMEM((nx * ny, nz // 2), F32)] * 2,
        name="finish",
    )(*pinned(fine_disp, fine_vel, old, *parts, sends[-1]))


def solution(mesh):
    in_specs = (
        P("tm", "slab", "groups", None),
        P("tm", "slab", "groups", None),
        P("slab", "groups", None),
        P("slab", "groups", None),
        P("slab", "groups", None),
    )
    out_specs = (P("tm", "slab", "groups", None), P("tm", "slab", "groups", None))
    return jax.shard_map(local, mesh=mesh, in_specs=in_specs, out_specs=out_specs, check_vma=False)
```

```python
import jax
import jax.numpy as jnp
from jax import lax
from jax.experimental import pallas as pl
from jax.experimental.pallas import tpu as pltpu
from jax.sharding import PartitionSpec as P

FINE_STEPS = 4
COARSE_STEPS = 2
KEEP = 0.95
F32 = jnp.float32


def vmem(count):
    return [pl.BlockSpec(memory_space=pltpu.VMEM)] * count


def shape(*dims):
    return jax.ShapeDtypeStruct(dims, F32)


def resident(*dims):
    return pltpu.VMEM(dims, F32)


def pinned(*arrays):
    return [pltpu.with_memory_space_constraint(x, pltpu.VMEM) for x in arrays]


def dot(left, right):
    return lax.dot_general(left, right, (((1,), (0,)), ((), ())), preferred_element_type=F32)


def selector(rows, cols, down, across, value=1.0):
    row = lax.shift_right_logical(lax.broadcasted_iota(jnp.int32, (rows, cols), 0), down)
    col = lax.shift_right_logical(lax.broadcasted_iota(jnp.int32, (rows, cols), 1), across)
    return jnp.where(row == col, value, 0.0).astype(jnp.bfloat16)


def flat2(x):
    return x.reshape(x.shape[0] * x.shape[1], x.shape[2])


def around(x, axis):
    size = x.shape[axis]
    none = jnp.zeros_like(lax.slice_in_dim(x, 0, 1, axis=axis))
    before = jnp.concatenate([none, lax.slice_in_dim(x, 0, size - 1, axis=axis)], axis)
    after = jnp.concatenate([lax.slice_in_dim(x, 1, size, axis=axis), none], axis)
    return before + after


def box9(x):
    x = x + around(x, 1)
    return x + around(x, 2)


def face4(x):
    return around(x, 1) + around(x, 2)


def three(box):
    none = jnp.zeros_like(box[:1])
    return box + jnp.concatenate([none, box[:-1]], axis=0) + jnp.concatenate([box[1:], none], axis=0)


def push(stiff, boxes, disp):
    return stiff * ((boxes - disp) * (1.0 / 26.0) - disp)


def pull(stiff, faces, disp):
    return stiff * (faces * (1.0 / 6.0) - disp)


def coarse_step(disp, vel, stiff):
    mid = disp[1:-1]
    vel = KEEP * vel + pull(stiff, disp[:-2] + disp[2:] + face4(mid), mid)
    return mid + vel, vel


def restrict(x, left, right):
    planes, ny, nz = x.shape
    half, lanes = planes // 2, nz // 2
    pairs = x.reshape(half, 2, ny, nz)
    pairs = flat2(pairs[:, 0] + pairs[:, 1])
    rows = half * ny
    lane = lax.broadcasted_iota(jnp.int32, (rows // 2, lanes), 1)
    even = (lane * 2) & (lanes - 1)

    def squeeze(scratch, part):
        scratch[pl.ds(0, rows), :] = part
        both = scratch[pl.ds(0, rows // 2, stride=2), :] + scratch[pl.ds(1, rows // 2, stride=2), :]
        return jnp.take_along_axis(both, even, axis=1) + jnp.take_along_axis(both, even + 1, axis=1)

    out = jnp.where(lane < lanes // 2, squeeze(left, pairs[:, :lanes]), squeeze(right, pairs[:, lanes:]))
    return (0.125 * out).reshape(half, ny // 2, lanes)


def pack_kernel(disp, vel, stiff, press, tiles, own, coarse, send_a, send_b, left, right, vel_in, press_in, tiles_in, sems):
    nx, ny, nz = stiff.shape
    half = nx // 2
    moves = [
        pltpu.make_async_copy(disp.at[0], own.at[pl.ds(0, nx)], sems.at[0]),
        pltpu.make_async_copy(stiff, own.at[pl.ds(2 * nx, nx)], sems.at[1]),
        pltpu.make_async_copy(vel.at[0], vel_in, sems.at[2]),
        pltpu.make_async_copy(tiles, tiles_in, sems.at[3]),
        pltpu.make_async_copy(press, press_in, sems.at[4]),
    ]
    for move in moves:
        move.start()
    slab = lax.axis_index("slab")
    for move in moves:
        move.wait()
    start = own[pl.ds(0, nx)]
    k = own[pl.ds(2 * nx, nx)]
    speed = vel_in[...]
    wet = flat2(tiles_in[...]).astype(F32).astype(jnp.bfloat16)
    shift = (nz // tiles.shape[2]).bit_length() - 1
    load = dot(wet, selector(tiles.shape[2], nz, 0, shift)).reshape(nx, ny, nz) * press_in[...]
    boxes = box9(start)
    first = KEEP * speed + load + push(k, three(boxes), start)
    moved = start + first
    inner = slice(1, nx - 1)
    box_moved = box9(moved[inner])
    near = jnp.concatenate([box_moved[:1] + box_moved[1:2], box_moved[-2:-1] + box_moved[-1:]], axis=0)
    spots = (1, nx - 2)

    def at(x):
        return jnp.concatenate([x[i : i + 1] for i in spots], axis=0)

    second = KEEP * at(first) + at(load) + push(at(k), near, at(moved))

    fields = restrict(jnp.concatenate([start, speed, k], axis=0), left, right)
    wide_disp, wide_vel, wide_k = fields[:half], fields[half : 2 * half], fields[2 * half :]
    none = jnp.zeros_like(wide_disp[:1])
    faces = face4(wide_disp) + jnp.concatenate([none, wide_disp[:-1]], axis=0) + jnp.concatenate([wide_disp[1:], none], axis=0)
    wide_first = KEEP * wide_vel + pull(wide_k, faces, wide_disp)

    own[pl.ds(nx, nx)] = first
    own[pl.ds(3 * nx, nx)] = load
    coarse[pl.ds(0, half)] = wide_disp
    coarse[pl.ds(half, half)] = wide_first
    coarse[pl.ds(2 * half, half)] = wide_k

    def fill(target, edge, spot, end, which):
        share = k[edge] * (1.0 / 26.0)
        planes = (start[edge], first[edge], k[edge], load[edge] + share * box_moved[spot - 1], second[which], k[spot])
        for i, plane in enumerate(planes):
            target[pl.ds(i * ny, ny), :] = plane
        cy, cz = ny // 2, nz // 2
        target[pl.ds(len(planes) * ny, cy), pl.ds(0, cz)] = wide_disp[end]
        target[pl.ds(len(planes) * ny, cy), pl.ds(cz, cz)] = wide_disp[end] + wide_first[end]

    @pl.when(slab % 2 == 0)
    def _():
        fill(send_a, nx - 1, nx - 2, half - 1, 1)
        fill(send_b, 0, 1, 0, 0)

    @pl.when(slab % 2 == 1)
    def _():
        fill(send_a, 0, 1, 0, 0)
        fill(send_b, nx - 1, nx - 2, half - 1, 1)


def fine_kernel(count, own, coarse, recv_a, recv_b, fine_disp, fine_vel, message, old, left, right):
    nx, ny, nz = fine_disp.shape
    half = nx // 2
    slab = lax.axis_index("slab")
    even = slab % 2 == 0
    a, b = recv_a[...], recv_b[...]
    low = jnp.where(slab > 0, jnp.where(even, b, a), 0.0)
    high = jnp.where(slab < count - 1, jnp.where(even, a, b), 0.0)

    def plane(message, i):
        return message[i * ny : (i + 1) * ny][None]

    def outer(i):
        return jnp.concatenate([plane(low, i), plane(high, i)], axis=0)

    def joined(i, inner):
        return jnp.concatenate([plane(low, i), inner, plane(high, i)], axis=0)

    start = own[pl.ds(0, nx)]
    k = joined(2, own[pl.ds(2 * nx, nx)])
    load = own[pl.ds(3 * nx, nx)]
    disp = joined(0, start)
    box = box9(jnp.concatenate([disp[1:2], disp[:1], disp[-1:], disp[-2:-1]], axis=0))
    box = jnp.concatenate([box[:2], jnp.zeros_like(disp[2:-2]), box[2:]], axis=0)
    vel = joined(1, own[pl.ds(nx, nx)]) + k * (1.0 / 26.0) * box
    disp = disp + vel
    box = box9(disp)
    vel = KEEP * vel + joined(3, load) + push(k, three(box), disp)
    far = outer(4) + outer(5) * (1.0 / 26.0) * jnp.concatenate([box[:1], box[-1:]], axis=0)
    disp = disp + vel
    box = box9(jnp.concatenate([far[:1], disp, far[1:]], axis=0))
    boxes = box[:-2] + box[1:-1] + box[2:]
    vel = KEEP * vel + joined(3, load) + push(k, boxes, disp)
    disp = disp + vel
    box = box9(disp)
    boxes = box[:-2] + box[1:-1] + box[2:]
    vel = KEEP * vel[1:-1] + load + push(k[1:-1], boxes, disp[1:-1])
    disp = disp[1:-1] + vel
    fine_disp[...] = disp
    fine_vel[...] = vel
    rest = restrict(jnp.concatenate([disp, vel], axis=0), left, right)

    cy, cz = ny // 2, nz // 2
    wide_disp = coarse[pl.ds(0, half)]
    wide_k = coarse[pl.ds(2 * half, half)]
    ends = jnp.concatenate([low[6 * ny :][None], high[6 * ny :][None]], axis=0)
    out_disp = ends[:, :, :cz]
    out_moved = ends[:, :, cz:]
    out_k = restrict(jnp.concatenate([plane(low, 2), plane(low, 5), plane(high, 2), plane(high, 5)], axis=0), left, right)
    none = [jnp.zeros_like(wide_disp[:1])] * (half - 2)
    ends = jnp.concatenate([out_disp[:1], *none, out_disp[1:]], axis=0)
    wide_vel = coarse[pl.ds(half, half)] + wide_k * (1.0 / 6.0) * ends
    inner = jnp.concatenate([wide_disp[:1], wide_disp[-1:]], axis=0)
    out_moved = out_moved + out_k * (1.0 / 6.0) * inner
    moved = jnp.concatenate([out_moved[:1], wide_disp + wide_vel, out_moved[1:]], axis=0)
    image_disp, image_vel = coarse_step(moved, wide_vel, wide_k)
    first = lax.axis_index("tm") == 0
    image_disp = jnp.where(first, 0.0, image_disp)
    image_vel = jnp.where(first, 0.0, image_vel)
    old[pl.ds(0, half)] = image_disp
    old[pl.ds(half, half)] = image_vel
    message[pl.ds(0, half)] = rest[:half] - image_disp
    message[pl.ds(half, half)] = rest[half:] - image_vel
    message[pl.ds(2 * half, half)] = wide_k


def chain_kernel(times, jumps, partners, *refs):
    inputs = refs[: len(partners)]
    outputs = refs[len(partners) : len(partners) + len(jumps)]
    window = refs[-1]
    half = inputs[0].shape[0] // 3
    slab = lax.axis_index("slab")
    reach = times - 1
    window[...] = jnp.zeros(window.shape, F32)
    for ref, place in zip(inputs, partners):
        at = (place(slab) - slab + reach) * half
        for field in range(3):
            window[field, pl.ds(at, half)] = ref[pl.ds(field * half, half)]
    disp, vel, stiff = window[0], window[1], window[2]
    powers = []
    for power in range(reach):
        for _ in range(COARSE_STEPS):
            disp, vel = coarse_step(disp, vel[1:-1], stiff[1:-1])
            stiff = stiff[1:-1]
        edge = (disp.shape[0] - half) // 2
        powers.append((disp[edge : edge + half], vel[edge : edge + half]))
    slot = lax.axis_index("tm")
    for k, output in zip(jumps, outputs):
        gap = (slot ^ k) - (slot ^ 1)
        pick_disp, pick_vel = powers[0]
        for power in range(1, reach):
            pick_disp = jnp.where(gap == power + 1, powers[power][0], pick_disp)
            pick_vel = jnp.where(gap == power + 1, powers[power][1], pick_vel)
        output[pl.ds(0, half)] = pick_disp
        output[pl.ds(half, half)] = pick_vel


def finish_kernel(jumps, *refs):
    fine_disp, fine_vel, old = refs[:3]
    parts = refs[3 : 3 + len(jumps)]
    new_disp, new_vel = refs[3 + len(jumps) : 5 + len(jumps)]
    left, right = refs[-2:]
    slot = lax.axis_index("tm")
    total = -old[...]
    for k, part in zip(jumps, parts):
        total = total + jnp.where((slot ^ k ^ 1) < slot, part[...], 0.0)
    half2, cy, cz = total.shape
    rows = half2 * cy
    flat = flat2(total)
    lane = lax.broadcasted_iota(jnp.int32, flat.shape, 1) >> 1
    for scratch, part in ((left, lane), (right, lane + cz // 2)):
        part = jnp.take_along_axis(flat, part, axis=1)
        scratch[pl.ds(0, rows, stride=2), :] = part
        scratch[pl.ds(1, rows, stride=2), :] = part
    wide = jnp.concatenate([left[...], right[...]], axis=1).reshape(half2, 2 * cy, 2 * cz)
    for i in range(fine_disp.shape[0]):
        new_disp[0, i] = fine_disp[i] + wide[i // 2]
        new_vel[0, i] = fine_vel[i] + wide[half2 // 2 + i // 2]


def local(start_disp, start_vel, stiffness, pressure, wet_tiles):
    slabs = lax.axis_size("slab")
    times = lax.axis_size("tm")
    _, nx, ny, nz = start_disp.shape
    half = nx // 2
    pair = ("slab", "tm")

    def at(s, t):
        return s * times + t

    low_pairs = [(at(s, t), at(s ^ 1, t)) for s in range(slabs) for t in range(times)]
    high_pairs = []
    for s in range(slabs):
        for t in range(times):
            if s == 0 or s == slabs - 1:
                high_pairs.append((at(s, t), at(s, t ^ 1)))
            else:
                high_pairs.append((at(s, t), at(s + 1 if s % 2 else s - 1, t)))

    packed = resident(6 * ny + ny // 2, nz)
    coarse_cells = (ny // 2, nz // 2)
    own, coarse, send_a, send_b = pl.pallas_call(
        pack_kernel,
        out_shape=(resident(4 * nx, ny, nz), resident(3 * half, *coarse_cells), packed, packed),
        in_specs=[pl.BlockSpec(memory_space=pl.ANY)] * 5,
        out_specs=vmem(4),
        scratch_shapes=[
            pltpu.VMEM((3 * half * ny, nz // 2), F32),
            pltpu.VMEM((3 * half * ny, nz // 2), F32),
            pltpu.VMEM((nx, ny, nz), F32),
            pltpu.VMEM((nx, ny, nz), F32),
            pltpu.VMEM(wet_tiles.shape, jnp.int32),
            pltpu.SemaphoreType.DMA((5,)),
        ],
        name="pack",
    )(start_disp, start_vel, stiffness, pressure, wet_tiles)
    recv_a = lax.ppermute(send_a, pair, low_pairs)
    recv_b = lax.ppermute(send_b, pair, high_pairs)

    def fine_body(*refs):
        fine_kernel(slabs, *refs)

    grid = resident(nx, ny, nz)
    fine_disp, fine_vel, message, old = pl.pallas_call(
        fine_body,
        out_shape=(grid, grid, resident(3 * half, *coarse_cells), resident(2 * half, *coarse_cells)),
        in_specs=vmem(4),
        out_specs=vmem(4),
        scratch_shapes=[pltpu.VMEM((2 * half * ny, nz // 2), F32)] * 2,
        name="fine",
    )(*pinned(own, coarse, recv_a, recv_b))

    messages, places = [], []
    if slabs <= times and slabs & (slabs - 1) == 0:
        for k in range(slabs):
            route = [(at(s, t), at(s ^ k, t ^ 1)) for s in range(slabs) for t in range(times)]
            messages.append(lax.ppermute(message, pair, route))
            places.append(lambda s, k=k: s ^ k)
    else:
        for shift in range(1 - times, times):
            route = [(at(s - shift, t ^ 1), at(s, t)) for s in range(slabs) if 0 <= s - shift < slabs for t in range(times)]
            messages.append(lax.ppermute(message, pair, route))
            places.append(lambda s, shift=shift: s - shift)

    jumps = [*range(2, times), 0]

    def chain_body(*refs):
        chain_kernel(times, jumps, places, *refs)

    link = resident(2 * half, *coarse_cells)
    sends = pl.pallas_call(
        chain_body,
        out_shape=(link,) * len(jumps),
        in_specs=vmem(len(messages)),
        out_specs=vmem(len(jumps)),
        scratch_shapes=[pltpu.VMEM((3, (2 * times - 1) * half, *coarse_cells), F32)],
        name="chain",
    )(*pinned(*messages))
    parts = [lax.ppermute(send, "tm", [(t, t ^ k) for t in range(times)]) for k, send in zip(jumps[:-1], sends)]

    def finish_body(*refs):
        finish_kernel(jumps, *refs)

    return pl.pallas_call(
        finish_body,
        out_shape=(shape(1, nx, ny, nz), shape(1, nx, ny, nz)),
        in_specs=vmem(3 + len(jumps)),
        out_specs=vmem(2),
        scratch_shapes=[pltpu.VMEM((nx * ny, nz // 2), F32)] * 2,
        name="finish",
    )(*pinned(fine_disp, fine_vel, old, *parts, sends[-1]))


def solution(mesh):
    in_specs = (
        P("tm", "slab", "groups", None),
        P("tm", "slab", "groups", None),
        P("slab", "groups", None),
        P("slab", "groups", None),
        P("slab", "groups", None),
    )
    out_specs = (P("tm", "slab", "groups", None), P("tm", "slab", "groups", None))
    return jax.shard_map(local, mesh=mesh, in_specs=in_specs, out_specs=out_specs, check_vma=False)
```

```python
import jax
import jax.numpy as jnp
from jax import lax
from jax.experimental import pallas as pl
from jax.experimental.pallas import tpu as pltpu
from jax.sharding import PartitionSpec as P

FINE_STEPS = 4
COARSE_STEPS = 2
KEEP = 0.95
F32 = jnp.float32


def vmem(count):
    return [pl.BlockSpec(memory_space=pltpu.VMEM)] * count


def shape(*dims):
    return jax.ShapeDtypeStruct(dims, F32)


def resident(*dims):
    return pltpu.VMEM(dims, F32)


def pinned(*arrays):
    return [pltpu.with_memory_space_constraint(x, pltpu.VMEM) for x in arrays]


def dot(left, right):
    return lax.dot_general(left, right, (((1,), (0,)), ((), ())), preferred_element_type=F32)


def selector(rows, cols, down, across, value=1.0):
    row = lax.shift_right_logical(lax.broadcasted_iota(jnp.int32, (rows, cols), 0), down)
    col = lax.shift_right_logical(lax.broadcasted_iota(jnp.int32, (rows, cols), 1), across)
    return jnp.where(row == col, value, 0.0).astype(jnp.bfloat16)


def flat2(x):
    return x.reshape(x.shape[0] * x.shape[1], x.shape[2])


def around(x, axis):
    size = x.shape[axis]
    none = jnp.zeros_like(lax.slice_in_dim(x, 0, 1, axis=axis))
    before = jnp.concatenate([none, lax.slice_in_dim(x, 0, size - 1, axis=axis)], axis)
    after = jnp.concatenate([lax.slice_in_dim(x, 1, size, axis=axis), none], axis)
    return before + after


def box9(x):
    x = x + around(x, 1)
    return x + around(x, 2)


def face4(x):
    return around(x, 1) + around(x, 2)


def three(box):
    none = jnp.zeros_like(box[:1])
    return box + jnp.concatenate([none, box[:-1]], axis=0) + jnp.concatenate([box[1:], none], axis=0)


def push(stiff, boxes, disp):
    return stiff * ((boxes - disp) * (1.0 / 26.0) - disp)


def pull(stiff, faces, disp):
    return stiff * (faces * (1.0 / 6.0) - disp)


def coarse_step(disp, vel, stiff):
    mid = disp[1:-1]
    vel = KEEP * vel + pull(stiff, disp[:-2] + disp[2:] + face4(mid), mid)
    return mid + vel, vel


def restrict(x, left, right):
    planes, ny, nz = x.shape
    half, lanes = planes // 2, nz // 2
    pairs = x.reshape(half, 2, ny, nz)
    pairs = flat2(pairs[:, 0] + pairs[:, 1])
    rows = half * ny
    lane = lax.broadcasted_iota(jnp.int32, (rows // 2, lanes), 1)
    even = (lane * 2) & (lanes - 1)

    def squeeze(scratch, part):
        scratch[pl.ds(0, rows), :] = part
        both = scratch[pl.ds(0, rows // 2, stride=2), :] + scratch[pl.ds(1, rows // 2, stride=2), :]
        return jnp.take_along_axis(both, even, axis=1) + jnp.take_along_axis(both, even + 1, axis=1)

    out = jnp.where(lane < lanes // 2, squeeze(left, pairs[:, :lanes]), squeeze(right, pairs[:, lanes:]))
    return (0.125 * out).reshape(half, ny // 2, lanes)


def pack_kernel(disp, vel, stiff, press, tiles, own, coarse, send_a, send_b, left, right, vel_in, press_in, tiles_in, sems):
    nx, ny, nz = stiff.shape
    half = nx // 2
    moves = [
        pltpu.make_async_copy(disp.at[0], own.at[pl.ds(0, nx)], sems.at[0]),
        pltpu.make_async_copy(stiff, own.at[pl.ds(2 * nx, nx)], sems.at[1]),
        pltpu.make_async_copy(vel.at[0], vel_in, sems.at[2]),
        pltpu.make_async_copy(tiles, tiles_in, sems.at[3]),
        pltpu.make_async_copy(press, press_in, sems.at[4]),
    ]
    for move in moves:
        move.start()
    slab = lax.axis_index("slab")
    for move in moves:
        move.wait()
    start = own[pl.ds(0, nx)]
    k = own[pl.ds(2 * nx, nx)]
    speed = vel_in[...]
    wet = flat2(tiles_in[...]).astype(F32).astype(jnp.bfloat16)
    shift = (nz // tiles.shape[2]).bit_length() - 1
    load = dot(wet, selector(tiles.shape[2], nz, 0, shift)).reshape(nx, ny, nz) * press_in[...]
    boxes = box9(start)
    first = KEEP * speed + load + push(k, three(boxes), start)
    moved = start + first
    inner = slice(1, nx - 1)
    box_moved = box9(moved[inner])
    near = jnp.concatenate([box_moved[:1] + box_moved[1:2], box_moved[-2:-1] + box_moved[-1:]], axis=0)
    spots = (1, nx - 2)

    def at(x):
        return jnp.concatenate([x[i : i + 1] for i in spots], axis=0)

    second = KEEP * at(first) + at(load) + push(at(k), near, at(moved))

    fields = restrict(jnp.concatenate([start, speed, k], axis=0), left, right)
    wide_disp, wide_vel, wide_k = fields[:half], fields[half : 2 * half], fields[2 * half :]
    none = jnp.zeros_like(wide_disp[:1])
    faces = face4(wide_disp) + jnp.concatenate([none, wide_disp[:-1]], axis=0) + jnp.concatenate([wide_disp[1:], none], axis=0)
    wide_first = KEEP * wide_vel + pull(wide_k, faces, wide_disp)

    own[pl.ds(nx, nx)] = first
    own[pl.ds(3 * nx, nx)] = load
    coarse[pl.ds(0, half)] = wide_disp
    coarse[pl.ds(half, half)] = wide_first
    coarse[pl.ds(2 * half, half)] = wide_k

    def fill(target, edge, spot, end, which):
        share = k[edge] * (1.0 / 26.0)
        planes = (start[edge], first[edge], k[edge], load[edge] + share * box_moved[spot - 1], second[which], k[spot])
        for i, plane in enumerate(planes):
            target[pl.ds(i * ny, ny), :] = plane
        cy, cz = ny // 2, nz // 2
        target[pl.ds(len(planes) * ny, cy), pl.ds(0, cz)] = wide_disp[end]
        target[pl.ds(len(planes) * ny, cy), pl.ds(cz, cz)] = wide_disp[end] + wide_first[end]

    @pl.when(slab % 2 == 0)
    def _():
        fill(send_a, nx - 1, nx - 2, half - 1, 1)
        fill(send_b, 0, 1, 0, 0)

    @pl.when(slab % 2 == 1)
    def _():
        fill(send_a, 0, 1, 0, 0)
        fill(send_b, nx - 1, nx - 2, half - 1, 1)


def fine_kernel(count, own, coarse, recv_a, recv_b, fine_disp, fine_vel, message, old, left, right):
    nx, ny, nz = fine_disp.shape
    half = nx // 2
    slab = lax.axis_index("slab")
    even = slab % 2 == 0
    a, b = recv_a[...], recv_b[...]
    low = jnp.where(slab > 0, jnp.where(even, b, a), 0.0)
    high = jnp.where(slab < count - 1, jnp.where(even, a, b), 0.0)

    def plane(message, i):
        return message[i * ny : (i + 1) * ny][None]

    def outer(i):
        return jnp.concatenate([plane(low, i), plane(high, i)], axis=0)

    def joined(i, inner):
        return jnp.concatenate([plane(low, i), inner, plane(high, i)], axis=0)

    start = own[pl.ds(0, nx)]
    k = joined(2, own[pl.ds(2 * nx, nx)])
    load = own[pl.ds(3 * nx, nx)]
    disp = joined(0, start)
    box = box9(jnp.concatenate([disp[1:2], disp[:1], disp[-1:], disp[-2:-1]], axis=0))
    box = jnp.concatenate([box[:2], jnp.zeros_like(disp[2:-2]), box[2:]], axis=0)
    vel = joined(1, own[pl.ds(nx, nx)]) + k * (1.0 / 26.0) * box
    disp = disp + vel
    box = box9(disp)
    vel = KEEP * vel + joined(3, load) + push(k, three(box), disp)
    far = outer(4) + outer(5) * (1.0 / 26.0) * jnp.concatenate([box[:1], box[-1:]], axis=0)
    disp = disp + vel
    box = box9(jnp.concatenate([far[:1], disp, far[1:]], axis=0))
    boxes = box[:-2] + box[1:-1] + box[2:]
    vel = KEEP * vel + joined(3, load) + push(k, boxes, disp)
    disp = disp + vel
    box = box9(disp)
    boxes = box[:-2] + box[1:-1] + box[2:]
    vel = KEEP * vel[1:-1] + load + push(k[1:-1], boxes, disp[1:-1])
    disp = disp[1:-1] + vel
    fine_disp[...] = disp
    fine_vel[...] = vel
    rest = restrict(jnp.concatenate([disp, vel], axis=0), left, right)

    cy, cz = ny // 2, nz // 2
    wide_disp = coarse[pl.ds(0, half)]
    wide_k = coarse[pl.ds(2 * half, half)]
    ends = jnp.concatenate([low[6 * ny :][None], high[6 * ny :][None]], axis=0)
    out_disp = ends[:, :, :cz]
    out_moved = ends[:, :, cz:]
    out_k = restrict(jnp.concatenate([plane(low, 2), plane(low, 5), plane(high, 2), plane(high, 5)], axis=0), left, right)
    none = [jnp.zeros_like(wide_disp[:1])] * (half - 2)
    ends = jnp.concatenate([out_disp[:1], *none, out_disp[1:]], axis=0)
    wide_vel = coarse[pl.ds(half, half)] + wide_k * (1.0 / 6.0) * ends
    inner = jnp.concatenate([wide_disp[:1], wide_disp[-1:]], axis=0)
    out_moved = out_moved + out_k * (1.0 / 6.0) * inner
    moved = jnp.concatenate([out_moved[:1], wide_disp + wide_vel, out_moved[1:]], axis=0)
    image_disp, image_vel = coarse_step(moved, wide_vel, wide_k)
    first = lax.axis_index("tm") == 0
    image_disp = jnp.where(first, 0.0, image_disp)
    image_vel = jnp.where(first, 0.0, image_vel)
    old[pl.ds(0, half)] = image_disp
    old[pl.ds(half, half)] = image_vel
    message[pl.ds(0, half)] = rest[:half] - image_disp
    message[pl.ds(half, half)] = rest[half:] - image_vel
    message[pl.ds(2 * half, half)] = wide_k


def chain_kernel(times, jumps, partners, *refs):
    inputs = refs[: len(partners)]
    outputs = refs[len(partners) : len(partners) + len(jumps)]
    window = refs[-1]
    half = inputs[0].shape[0] // 3
    slab = lax.axis_index("slab")
    reach = times - 1
    window[...] = jnp.zeros(window.shape, F32)
    for ref, place in zip(inputs, partners):
        at = (place(slab) - slab + reach) * half
        for field in range(3):
            window[field, pl.ds(at, half)] = ref[pl.ds(field * half, half)]
    disp, vel, stiff = window[0], window[1], window[2]
    powers = []
    for power in range(reach):
        for _ in range(COARSE_STEPS):
            disp, vel = coarse_step(disp, vel[1:-1], stiff[1:-1])
            stiff = stiff[1:-1]
        edge = (disp.shape[0] - half) // 2
        powers.append((disp[edge : edge + half], vel[edge : edge + half]))
    slot = lax.axis_index("tm")
    for k, output in zip(jumps, outputs):
        gap = (slot ^ k) - (slot ^ 1)
        pick_disp, pick_vel = powers[0]
        for power in range(1, reach):
            pick_disp = jnp.where(gap == power + 1, powers[power][0], pick_disp)
            pick_vel = jnp.where(gap == power + 1, powers[power][1], pick_vel)
        output[pl.ds(0, half)] = pick_disp
        output[pl.ds(half, half)] = pick_vel


def finish_kernel(jumps, *refs):
    fine_disp, fine_vel, old = refs[:3]
    parts = refs[3 : 3 + len(jumps)]
    new_disp, new_vel = refs[3 + len(jumps) : 5 + len(jumps)]
    left, right = refs[-2:]
    slot = lax.axis_index("tm")
    total = -old[...]
    for k, part in zip(jumps, parts):
        total = total + jnp.where((slot ^ k ^ 1) < slot, part[...], 0.0)
    half2, cy, cz = total.shape
    rows = half2 * cy
    flat = flat2(total)
    lane = lax.broadcasted_iota(jnp.int32, flat.shape, 1) >> 1
    for scratch, part in ((left, lane), (right, lane + cz // 2)):
        part = jnp.take_along_axis(flat, part, axis=1)
        scratch[pl.ds(0, rows, stride=2), :] = part
        scratch[pl.ds(1, rows, stride=2), :] = part
    wide = jnp.concatenate([left[...], right[...]], axis=1).reshape(half2, 2 * cy, 2 * cz)
    for i in range(fine_disp.shape[0]):
        new_disp[0, i] = fine_disp[i] + wide[i // 2]
        new_vel[0, i] = fine_vel[i] + wide[half2 // 2 + i // 2]


def local(start_disp, start_vel, stiffness, pressure, wet_tiles):
    slabs = lax.axis_size("slab")
    times = lax.axis_size("tm")
    _, nx, ny, nz = start_disp.shape
    half = nx // 2
    pair = ("slab", "tm")

    def at(s, t):
        return s * times + t

    low_pairs = [(at(s, t), at(s ^ 1, t)) for s in range(slabs) for t in range(times)]
    high_pairs = []
    for s in range(slabs):
        for t in range(times):
            if s == 0 or s == slabs - 1:
                high_pairs.append((at(s, t), at(s, t ^ 1)))
            else:
                high_pairs.append((at(s, t), at(s + 1 if s % 2 else s - 1, t)))

    packed = resident(6 * ny + ny // 2, nz)
    coarse_cells = (ny // 2, nz // 2)
    own, coarse, send_a, send_b = pl.pallas_call(
        pack_kernel,
        out_shape=(resident(4 * nx, ny, nz), resident(3 * half, *coarse_cells), packed, packed),
        in_specs=[pl.BlockSpec(memory_space=pl.ANY)] * 5,
        out_specs=vmem(4),
        scratch_shapes=[
            pltpu.VMEM((3 * half * ny, nz // 2), F32),
            pltpu.VMEM((3 * half * ny, nz // 2), F32),
            pltpu.VMEM((nx, ny, nz), F32),
            pltpu.VMEM((nx, ny, nz), F32),
            pltpu.VMEM(wet_tiles.shape, jnp.int32),
            pltpu.SemaphoreType.DMA((5,)),
        ],
        name="pack",
    )(start_disp, start_vel, stiffness, pressure, wet_tiles)
    recv_a = lax.ppermute(send_a, pair, low_pairs)
    recv_b = lax.ppermute(send_b, pair, high_pairs)

    def fine_body(*refs):
        fine_kernel(slabs, *refs)

    grid = resident(nx, ny, nz)
    fine_disp, fine_vel, message, old = pl.pallas_call(
        fine_body,
        out_shape=(grid, grid, resident(3 * half, *coarse_cells), resident(2 * half, *coarse_cells)),
        in_specs=vmem(4),
        out_specs=vmem(4),
        scratch_shapes=[pltpu.VMEM((2 * half * ny, nz // 2), F32)] * 2,
        name="fine",
    )(*pinned(own, coarse, recv_a, recv_b))

    messages, places = [], []
    if slabs <= times and slabs & (slabs - 1) == 0:
        for k in range(slabs):
            route = []
            for s in range(slabs):
                for t in range(times):
                    reach = times - 1 - min(t, t ^ 1)
                    route.append((at(s, t), at(s ^ k if abs((s ^ k) - s) <= reach else s, t ^ 1)))
            messages.append(lax.ppermute(message, pair, route))
            places.append(lambda s, k=k: s ^ k)
    else:
        for shift in range(1 - times, times):
            route = [(at(s - shift, t ^ 1), at(s, t)) for s in range(slabs) if 0 <= s - shift < slabs for t in range(times)]
            messages.append(lax.ppermute(message, pair, route))
            places.append(lambda s, shift=shift: s - shift)

    jumps = [*range(2, times), 0]

    def chain_body(*refs):
        chain_kernel(times, jumps, places, *refs)

    link = resident(2 * half, *coarse_cells)
    sends = pl.pallas_call(
        chain_body,
        out_shape=(link,) * len(jumps),
        in_specs=vmem(len(messages)),
        out_specs=vmem(len(jumps)),
        scratch_shapes=[pltpu.VMEM((3, (2 * times - 1) * half, *coarse_cells), F32)],
        name="chain",
    )(*pinned(*messages))
    parts = [lax.ppermute(send, "tm", [(t, t ^ k) for t in range(times)]) for k, send in zip(jumps[:-1], sends)]

    def finish_body(*refs):
        finish_kernel(jumps, *refs)

    return pl.pallas_call(
        finish_body,
        out_shape=(shape(1, nx, ny, nz), shape(1, nx, ny, nz)),
        in_specs=vmem(3 + len(jumps)),
        out_specs=vmem(2),
        scratch_shapes=[pltpu.VMEM((nx * ny, nz // 2), F32)] * 2,
        name="finish",
    )(*pinned(fine_disp, fine_vel, old, *parts, sends[-1]))


def solution(mesh):
    in_specs = (
        P("tm", "slab", "groups", None),
        P("tm", "slab", "groups", None),
        P("slab", "groups", None),
        P("slab", "groups", None),
        P("slab", "groups", None),
    )
    out_specs = (P("tm", "slab", "groups", None), P("tm", "slab", "groups", None))
    return jax.shard_map(local, mesh=mesh, in_specs=in_specs, out_specs=out_specs, check_vma=False)
```

```python
import jax
import jax.numpy as jnp
from jax import lax
from jax.experimental import pallas as pl
from jax.experimental.pallas import tpu as pltpu
from jax.sharding import PartitionSpec as P

FINE_STEPS = 4
COARSE_STEPS = 2
KEEP = 0.95
F32 = jnp.float32


def vmem(count):
    return [pl.BlockSpec(memory_space=pltpu.VMEM)] * count


def shape(*dims):
    return jax.ShapeDtypeStruct(dims, F32)


def resident(*dims):
    return pltpu.VMEM(dims, F32)


def pinned(*arrays):
    return [pltpu.with_memory_space_constraint(x, pltpu.VMEM) for x in arrays]


def dot(left, right):
    return lax.dot_general(left, right, (((1,), (0,)), ((), ())), preferred_element_type=F32)


def selector(rows, cols, down, across, value=1.0):
    row = lax.shift_right_logical(lax.broadcasted_iota(jnp.int32, (rows, cols), 0), down)
    col = lax.shift_right_logical(lax.broadcasted_iota(jnp.int32, (rows, cols), 1), across)
    return jnp.where(row == col, value, 0.0).astype(jnp.bfloat16)


def flat2(x):
    return x.reshape(x.shape[0] * x.shape[1], x.shape[2])


def around(x, axis):
    size = x.shape[axis]
    none = jnp.zeros_like(lax.slice_in_dim(x, 0, 1, axis=axis))
    before = jnp.concatenate([none, lax.slice_in_dim(x, 0, size - 1, axis=axis)], axis)
    after = jnp.concatenate([lax.slice_in_dim(x, 1, size, axis=axis), none], axis)
    return before + after


def box9(x):
    x = x + around(x, 1)
    return x + around(x, 2)


def face4(x):
    return around(x, 1) + around(x, 2)


def three(box):
    none = jnp.zeros_like(box[:1])
    return box + jnp.concatenate([none, box[:-1]], axis=0) + jnp.concatenate([box[1:], none], axis=0)


def push(stiff, boxes, disp):
    return stiff * ((boxes - disp) * (1.0 / 26.0) - disp)


def pull(stiff, faces, disp):
    return stiff * (faces * (1.0 / 6.0) - disp)


def coarse_step(disp, vel, stiff):
    mid = disp[1:-1]
    vel = KEEP * vel + pull(stiff, disp[:-2] + disp[2:] + face4(mid), mid)
    return mid + vel, vel


def restrict(x, left, right):
    planes, ny, nz = x.shape
    half, lanes = planes // 2, nz // 2
    pairs = x.reshape(half, 2, ny, nz)
    pairs = flat2(pairs[:, 0] + pairs[:, 1])
    rows = half * ny
    lane = lax.broadcasted_iota(jnp.int32, (rows // 2, lanes), 1)
    even = (lane * 2) & (lanes - 1)

    def squeeze(scratch, part):
        scratch[pl.ds(0, rows), :] = part
        both = scratch[pl.ds(0, rows // 2, stride=2), :] + scratch[pl.ds(1, rows // 2, stride=2), :]
        return jnp.take_along_axis(both, even, axis=1) + jnp.take_along_axis(both, even + 1, axis=1)

    out = jnp.where(lane < lanes // 2, squeeze(left, pairs[:, :lanes]), squeeze(right, pairs[:, lanes:]))
    return (0.125 * out).reshape(half, ny // 2, lanes)


def pack_kernel(count, disp, vel, stiff, press, tiles, own, coarse, send_a, send_b, left, right, vel_in, press_in, tiles_in, sems):
    nx, ny, nz = stiff.shape
    half = nx // 2
    moves = [
        pltpu.make_async_copy(disp.at[0], own.at[pl.ds(0, nx)], sems.at[0]),
        pltpu.make_async_copy(stiff, own.at[pl.ds(2 * nx, nx)], sems.at[1]),
        pltpu.make_async_copy(vel.at[0], vel_in, sems.at[2]),
        pltpu.make_async_copy(tiles, tiles_in, sems.at[3]),
        pltpu.make_async_copy(press, press_in, sems.at[4]),
    ]
    for move in moves:
        move.start()
    slab = lax.axis_index("slab")
    for move in moves:
        move.wait()
    start = own[pl.ds(0, nx)]
    k = own[pl.ds(2 * nx, nx)]
    speed = vel_in[...]
    wet = flat2(tiles_in[...]).astype(F32).astype(jnp.bfloat16)
    shift = (nz // tiles.shape[2]).bit_length() - 1
    load = dot(wet, selector(tiles.shape[2], nz, 0, shift)).reshape(nx, ny, nz) * press_in[...]
    boxes = box9(start)
    first = KEEP * speed + load + push(k, three(boxes), start)
    moved = start + first
    inner = slice(1, nx - 1)
    box_moved = box9(moved[inner])
    near = jnp.concatenate([box_moved[:1] + box_moved[1:2], box_moved[-2:-1] + box_moved[-1:]], axis=0)
    spots = (1, nx - 2)

    def at(x):
        return jnp.concatenate([x[i : i + 1] for i in spots], axis=0)

    second = KEEP * at(first) + at(load) + push(at(k), near, at(moved))

    fields = restrict(jnp.concatenate([start, speed, k], axis=0), left, right)
    wide_disp, wide_vel, wide_k = fields[:half], fields[half : 2 * half], fields[2 * half :]
    none = jnp.zeros_like(wide_disp[:1])
    faces = face4(wide_disp) + jnp.concatenate([none, wide_disp[:-1]], axis=0) + jnp.concatenate([wide_disp[1:], none], axis=0)
    wide_first = KEEP * wide_vel + pull(wide_k, faces, wide_disp)

    own[pl.ds(nx, nx)] = first
    own[pl.ds(3 * nx, nx)] = load
    coarse[pl.ds(0, half)] = wide_disp
    coarse[pl.ds(half, half)] = wide_first
    coarse[pl.ds(2 * half, half)] = wide_k

    def fill(target, edge, spot, end, which):
        share = k[edge] * (1.0 / 26.0)
        planes = (start[edge], first[edge], k[edge], load[edge] + share * box_moved[spot - 1], second[which], k[spot])
        for i, plane in enumerate(planes):
            target[pl.ds(i * ny, ny), :] = plane
        cy, cz = ny // 2, nz // 2
        target[pl.ds(len(planes) * ny, cy), pl.ds(0, cz)] = wide_disp[end]
        target[pl.ds(len(planes) * ny, cy), pl.ds(cz, cz)] = wide_disp[end] + wide_first[end]

    @pl.when(slab % 2 == 0)
    def _():
        fill(send_a, nx - 1, nx - 2, half - 1, 1)
        fill(send_b, 0, 1, 0, 0)

    @pl.when(slab % 2 == 1)
    def _():
        fill(send_a, 0, 1, 0, 0)
        fill(send_b, nx - 1, nx - 2, half - 1, 1)

    @pl.when((slab == 0) | (slab == count - 1))
    def _():
        send_b[...] = jnp.zeros(send_b.shape, F32)


def fine_kernel(own, coarse, recv_a, recv_b, fine_disp, fine_vel, message, old, left, right):
    nx, ny, nz = fine_disp.shape
    half = nx // 2
    slab = lax.axis_index("slab")
    even = slab % 2 == 0
    a, b = recv_a[...], recv_b[...]
    low = jnp.where(even, b, a)
    high = jnp.where(even, a, b)

    def plane(message, i):
        return message[i * ny : (i + 1) * ny][None]

    def outer(i):
        return jnp.concatenate([plane(low, i), plane(high, i)], axis=0)

    def joined(i, inner):
        return jnp.concatenate([plane(low, i), inner, plane(high, i)], axis=0)

    start = own[pl.ds(0, nx)]
    k = joined(2, own[pl.ds(2 * nx, nx)])
    load = own[pl.ds(3 * nx, nx)]
    disp = joined(0, start)
    box = box9(jnp.concatenate([disp[1:2], disp[:1], disp[-1:], disp[-2:-1]], axis=0))
    box = jnp.concatenate([box[:2], jnp.zeros_like(disp[2:-2]), box[2:]], axis=0)
    vel = joined(1, own[pl.ds(nx, nx)]) + k * (1.0 / 26.0) * box
    disp = disp + vel
    box = box9(disp)
    vel = KEEP * vel + joined(3, load) + push(k, three(box), disp)
    far = outer(4) + outer(5) * (1.0 / 26.0) * jnp.concatenate([box[:1], box[-1:]], axis=0)
    disp = disp + vel
    wide = jnp.concatenate([far[:1], disp, far[1:]], axis=0)
    boxes = box9(wide[:-2] + wide[1:-1] + wide[2:])
    vel = KEEP * vel + joined(3, load) + push(k, boxes, disp)
    disp = disp + vel
    boxes = box9(disp[:-2] + disp[1:-1] + disp[2:])
    vel = KEEP * vel[1:-1] + load + push(k[1:-1], boxes, disp[1:-1])
    disp = disp[1:-1] + vel
    fine_disp[...] = disp
    fine_vel[...] = vel
    rest = restrict(jnp.concatenate([disp, vel], axis=0), left, right)

    cy, cz = ny // 2, nz // 2
    wide_disp = coarse[pl.ds(0, half)]
    wide_k = coarse[pl.ds(2 * half, half)]
    ends = jnp.concatenate([low[6 * ny :][None], high[6 * ny :][None]], axis=0)
    out_disp = ends[:, :, :cz]
    out_moved = ends[:, :, cz:]
    out_k = restrict(jnp.concatenate([plane(low, 2), plane(low, 5), plane(high, 2), plane(high, 5)], axis=0), left, right)
    none = [jnp.zeros_like(wide_disp[:1])] * (half - 2)
    ends = jnp.concatenate([out_disp[:1], *none, out_disp[1:]], axis=0)
    wide_vel = coarse[pl.ds(half, half)] + wide_k * (1.0 / 6.0) * ends
    inner = jnp.concatenate([wide_disp[:1], wide_disp[-1:]], axis=0)
    out_moved = out_moved + out_k * (1.0 / 6.0) * inner
    moved = jnp.concatenate([out_moved[:1], wide_disp + wide_vel, out_moved[1:]], axis=0)
    image_disp, image_vel = coarse_step(moved, wide_vel, wide_k)
    first = lax.axis_index("tm") == 0
    image_disp = jnp.where(first, 0.0, image_disp)
    image_vel = jnp.where(first, 0.0, image_vel)
    old[pl.ds(0, half)] = image_disp
    old[pl.ds(half, half)] = image_vel
    message[pl.ds(0, half)] = rest[:half] - image_disp
    message[pl.ds(half, half)] = rest[half:] - image_vel
    message[pl.ds(2 * half, half)] = wide_k


def chain_kernel(times, jumps, partners, *refs):
    inputs = refs[: len(partners)]
    outputs = refs[len(partners) : len(partners) + len(jumps)]
    window = refs[-1]
    half = inputs[0].shape[0] // 3
    slab = lax.axis_index("slab")
    reach = times - 1
    window[...] = jnp.zeros(window.shape, F32)
    for ref, place in zip(inputs, partners):
        at = (place(slab) - slab + reach) * half
        for field in range(3):
            window[field, pl.ds(at, half)] = ref[pl.ds(field * half, half)]
    disp, vel, stiff = window[0], window[1], window[2]
    powers = []
    for power in range(reach):
        for _ in range(COARSE_STEPS):
            disp, vel = coarse_step(disp, vel[1:-1], stiff[1:-1])
            stiff = stiff[1:-1]
        edge = (disp.shape[0] - half) // 2
        powers.append((disp[edge : edge + half], vel[edge : edge + half]))
    slot = lax.axis_index("tm")
    for k, output in zip(jumps, outputs):
        gap = (slot ^ k) - (slot ^ 1)
        pick_disp, pick_vel = powers[0]
        for power in range(1, reach):
            pick_disp = jnp.where(gap == power + 1, powers[power][0], pick_disp)
            pick_vel = jnp.where(gap == power + 1, powers[power][1], pick_vel)
        output[pl.ds(0, half)] = pick_disp
        output[pl.ds(half, half)] = pick_vel


def finish_kernel(jumps, *refs):
    fine_disp, fine_vel, old = refs[:3]
    parts = refs[3 : 3 + len(jumps)]
    new_disp, new_vel = refs[3 + len(jumps) : 5 + len(jumps)]
    left, right = refs[-2:]
    slot = lax.axis_index("tm")
    total = -old[...]
    for k, part in zip(jumps, parts):
        total = total + jnp.where((slot ^ k ^ 1) < slot, part[...], 0.0)
    half2, cy, cz = total.shape
    rows = half2 * cy
    flat = flat2(total)
    lane = lax.broadcasted_iota(jnp.int32, flat.shape, 1) >> 1
    for scratch, part in ((left, lane), (right, lane + cz // 2)):
        part = jnp.take_along_axis(flat, part, axis=1)
        scratch[pl.ds(0, rows, stride=2), :] = part
        scratch[pl.ds(1, rows, stride=2), :] = part
    wide = jnp.concatenate([left[...], right[...]], axis=1).reshape(half2, 2 * cy, 2 * cz)
    for i in range(fine_disp.shape[0]):
        new_disp[0, i] = fine_disp[i] + wide[i // 2]
        new_vel[0, i] = fine_vel[i] + wide[half2 // 2 + i // 2]


def local(start_disp, start_vel, stiffness, pressure, wet_tiles):
    slabs = lax.axis_size("slab")
    times = lax.axis_size("tm")
    _, nx, ny, nz = start_disp.shape
    half = nx // 2
    pair = ("slab", "tm")

    def at(s, t):
        return s * times + t

    low_pairs = [(at(s, t), at(s ^ 1, t)) for s in range(slabs) for t in range(times)]
    high_pairs = []
    for s in range(slabs):
        for t in range(times):
            if s == 0 or s == slabs - 1:
                high_pairs.append((at(s, t), at(s, t ^ 1)))
            else:
                high_pairs.append((at(s, t), at(s + 1 if s % 2 else s - 1, t)))

    packed = resident(6 * ny + ny // 2, nz)
    coarse_cells = (ny // 2, nz // 2)
    def pack_body(*refs):
        pack_kernel(slabs, *refs)

    own, coarse, send_a, send_b = pl.pallas_call(
        pack_body,
        out_shape=(resident(4 * nx, ny, nz), resident(3 * half, *coarse_cells), packed, packed),
        in_specs=[pl.BlockSpec(memory_space=pl.ANY)] * 5,
        out_specs=vmem(4),
        scratch_shapes=[
            pltpu.VMEM((3 * half * ny, nz // 2), F32),
            pltpu.VMEM((3 * half * ny, nz // 2), F32),
            pltpu.VMEM((nx, ny, nz), F32),
            pltpu.VMEM((nx, ny, nz), F32),
            pltpu.VMEM(wet_tiles.shape, jnp.int32),
            pltpu.SemaphoreType.DMA((5,)),
        ],
        name="pack",
    )(start_disp, start_vel, stiffness, pressure, wet_tiles)
    recv_a = lax.ppermute(send_a, pair, low_pairs)
    recv_b = lax.ppermute(send_b, pair, high_pairs)

    grid = resident(nx, ny, nz)
    fine_disp, fine_vel, message, old = pl.pallas_call(
        fine_kernel,
        out_shape=(grid, grid, resident(3 * half, *coarse_cells), resident(2 * half, *coarse_cells)),
        in_specs=vmem(4),
        out_specs=vmem(4),
        scratch_shapes=[pltpu.VMEM((2 * half * ny, nz // 2), F32)] * 2,
        name="fine",
    )(*pinned(own, coarse, recv_a, recv_b))

    messages, places = [], []
    if slabs <= times and slabs & (slabs - 1) == 0:
        for k in range(slabs):
            route = []
            for s in range(slabs):
                for t in range(times):
                    reach = times - 1 - min(t, t ^ 1)
                    route.append((at(s, t), at(s ^ k if abs((s ^ k) - s) <= reach else s, t ^ 1)))
            messages.append(lax.ppermute(message, pair, route))
            places.append(lambda s, k=k: s ^ k)
    else:
        for shift in range(1 - times, times):
            route = [(at(s - shift, t ^ 1), at(s, t)) for s in range(slabs) if 0 <= s - shift < slabs for t in range(times)]
            messages.append(lax.ppermute(message, pair, route))
            places.append(lambda s, shift=shift: s - shift)

    jumps = [*range(2, times), 0]

    def chain_body(*refs):
        chain_kernel(times, jumps, places, *refs)

    link = resident(2 * half, *coarse_cells)
    sends = pl.pallas_call(
        chain_body,
        out_shape=(link,) * len(jumps),
        in_specs=vmem(len(messages)),
        out_specs=vmem(len(jumps)),
        scratch_shapes=[pltpu.VMEM((3, (2 * times - 1) * half, *coarse_cells), F32)],
        name="chain",
    )(*pinned(*messages))
    parts = [lax.ppermute(send, "tm", [(t, t ^ k) for t in range(times)]) for k, send in zip(jumps[:-1], sends)]

    def finish_body(*refs):
        finish_kernel(jumps, *refs)

    return pl.pallas_call(
        finish_body,
        out_shape=(shape(1, nx, ny, nz), shape(1, nx, ny, nz)),
        in_specs=vmem(3 + len(jumps)),
        out_specs=vmem(2),
        scratch_shapes=[pltpu.VMEM((nx * ny, nz // 2), F32)] * 2,
        name="finish",
    )(*pinned(fine_disp, fine_vel, old, *parts, sends[-1]))


def solution(mesh):
    in_specs = (
        P("tm", "slab", "groups", None),
        P("tm", "slab", "groups", None),
        P("slab", "groups", None),
        P("slab", "groups", None),
        P("slab", "groups", None),
    )
    out_specs = (P("tm", "slab", "groups", None), P("tm", "slab", "groups", None))
    return jax.shard_map(local, mesh=mesh, in_specs=in_specs, out_specs=out_specs, check_vma=False)
```

```python
import jax
import jax.numpy as jnp
from jax import lax
from jax.experimental import pallas as pl
from jax.experimental.pallas import tpu as pltpu
from jax.sharding import PartitionSpec as P

FINE_STEPS = 4
COARSE_STEPS = 2
KEEP = 0.95
F32 = jnp.float32


def vmem(count):
    return [pl.BlockSpec(memory_space=pltpu.VMEM)] * count


def shape(*dims):
    return jax.ShapeDtypeStruct(dims, F32)


def resident(*dims):
    return pltpu.VMEM(dims, F32)


def pinned(*arrays):
    return [pltpu.with_memory_space_constraint(x, pltpu.VMEM) for x in arrays]


def dot(left, right):
    return lax.dot_general(left, right, (((1,), (0,)), ((), ())), preferred_element_type=F32)


def selector(rows, cols, down, across, value=1.0):
    row = lax.shift_right_logical(lax.broadcasted_iota(jnp.int32, (rows, cols), 0), down)
    col = lax.shift_right_logical(lax.broadcasted_iota(jnp.int32, (rows, cols), 1), across)
    return jnp.where(row == col, value, 0.0).astype(jnp.bfloat16)


def flat2(x):
    return x.reshape(x.shape[0] * x.shape[1], x.shape[2])


def around(x, axis):
    size = x.shape[axis]
    none = jnp.zeros_like(lax.slice_in_dim(x, 0, 1, axis=axis))
    before = jnp.concatenate([none, lax.slice_in_dim(x, 0, size - 1, axis=axis)], axis)
    after = jnp.concatenate([lax.slice_in_dim(x, 1, size, axis=axis), none], axis)
    return before + after


def box9(x):
    x = x + around(x, 1)
    return x + around(x, 2)


def face4(x):
    return around(x, 1) + around(x, 2)


def three(box):
    none = jnp.zeros_like(box[:1])
    return box + jnp.concatenate([none, box[:-1]], axis=0) + jnp.concatenate([box[1:], none], axis=0)


def push(stiff, boxes, disp):
    return stiff * ((boxes - disp) * (1.0 / 26.0) - disp)


def stepped(rest, stiff, planes, disp):
    along = planes + around(planes, 1)
    rest = rest + stiff * ((along - disp) * (1.0 / 26.0) - disp)
    return rest + (stiff * (1.0 / 26.0)) * around(along, 2)


def pull(stiff, faces, disp):
    return stiff * (faces * (1.0 / 6.0) - disp)


def coarse_step(disp, vel, stiff):
    mid = disp[1:-1]
    vel = KEEP * vel + pull(stiff, disp[:-2] + disp[2:] + around(mid, 1), mid)
    vel = vel + (stiff * (1.0 / 6.0)) * around(mid, 2)
    return mid + vel, vel


def restrict(x, left, right):
    planes, ny, nz = x.shape
    half, lanes = planes // 2, nz // 2
    pairs = x.reshape(half, 2, ny, nz)
    pairs = flat2(pairs[:, 0] + pairs[:, 1])
    rows = half * ny
    lane = lax.broadcasted_iota(jnp.int32, (rows // 2, lanes), 1)
    even = (lane * 2) & (lanes - 1)

    def squeeze(scratch, part):
        scratch[pl.ds(0, rows), :] = part
        both = scratch[pl.ds(0, rows // 2, stride=2), :] + scratch[pl.ds(1, rows // 2, stride=2), :]
        return jnp.take_along_axis(both, even, axis=1) + jnp.take_along_axis(both, even + 1, axis=1)

    out = jnp.where(lane < lanes // 2, squeeze(left, pairs[:, :lanes]), squeeze(right, pairs[:, lanes:]))
    return (0.125 * out).reshape(half, ny // 2, lanes)


def pack_kernel(count, disp, vel, stiff, press, tiles, own, coarse, send_a, send_b, left, right, vel_in, press_in, tiles_in, sems):
    nx, ny, nz = stiff.shape
    half = nx // 2
    moves = [
        pltpu.make_async_copy(disp.at[0], own.at[pl.ds(0, nx)], sems.at[0]),
        pltpu.make_async_copy(stiff, own.at[pl.ds(2 * nx, nx)], sems.at[1]),
        pltpu.make_async_copy(vel.at[0], vel_in, sems.at[2]),
        pltpu.make_async_copy(tiles, tiles_in, sems.at[3]),
        pltpu.make_async_copy(press, press_in, sems.at[4]),
    ]
    for i, move in enumerate(moves):
        move.start(priority=i % 2)
    slab = lax.axis_index("slab")
    for move in moves:
        move.wait()
    start = own[pl.ds(0, nx)]
    k = own[pl.ds(2 * nx, nx)]
    speed = vel_in[...]
    wet = flat2(tiles_in[...]).astype(F32).astype(jnp.bfloat16)
    shift = (nz // tiles.shape[2]).bit_length() - 1
    load = dot(wet, selector(tiles.shape[2], nz, 0, shift)).reshape(nx, ny, nz) * press_in[...]
    first = stepped(KEEP * speed + load, k, three(start), start)
    moved = start + first
    inner = slice(1, nx - 1)
    box_moved = box9(moved[inner])
    near = jnp.concatenate([box_moved[:1] + box_moved[1:2], box_moved[-2:-1] + box_moved[-1:]], axis=0)
    spots = (1, nx - 2)

    def at(x):
        return jnp.concatenate([x[i : i + 1] for i in spots], axis=0)

    second = KEEP * at(first) + at(load) + push(at(k), near, at(moved))

    fields = restrict(jnp.concatenate([start, speed, k], axis=0), left, right)
    wide_disp, wide_vel, wide_k = fields[:half], fields[half : 2 * half], fields[2 * half :]
    none = jnp.zeros_like(wide_disp[:1])
    faces = face4(wide_disp) + jnp.concatenate([none, wide_disp[:-1]], axis=0) + jnp.concatenate([wide_disp[1:], none], axis=0)
    wide_first = KEEP * wide_vel + pull(wide_k, faces, wide_disp)

    own[pl.ds(nx, nx)] = first
    own[pl.ds(3 * nx, nx)] = load
    coarse[pl.ds(0, half)] = wide_disp
    coarse[pl.ds(half, half)] = wide_first
    coarse[pl.ds(2 * half, half)] = wide_k

    def fill(target, edge, spot, end, which):
        share = k[edge] * (1.0 / 26.0)
        planes = (start[edge], first[edge], k[edge], load[edge] + share * box_moved[spot - 1], second[which], k[spot])
        for i, plane in enumerate(planes):
            target[pl.ds(i * ny, ny), :] = plane
        cy, cz = ny // 2, nz // 2
        target[pl.ds(len(planes) * ny, cy), pl.ds(0, cz)] = wide_disp[end]
        target[pl.ds(len(planes) * ny, cy), pl.ds(cz, cz)] = wide_disp[end] + wide_first[end]

    @pl.when(slab % 2 == 0)
    def _():
        fill(send_a, nx - 1, nx - 2, half - 1, 1)
        fill(send_b, 0, 1, 0, 0)

    @pl.when(slab % 2 == 1)
    def _():
        fill(send_a, 0, 1, 0, 0)
        fill(send_b, nx - 1, nx - 2, half - 1, 1)

    @pl.when((slab == 0) | (slab == count - 1))
    def _():
        send_b[...] = jnp.zeros(send_b.shape, F32)


def fine_kernel(own, coarse, recv_a, recv_b, fine_disp, fine_vel, message, old, left, right):
    nx, ny, nz = fine_disp.shape
    half = nx // 2
    slab = lax.axis_index("slab")
    even = slab % 2 == 0
    a, b = recv_a[...], recv_b[...]
    low = jnp.where(even, b, a)
    high = jnp.where(even, a, b)

    def plane(message, i):
        return message[i * ny : (i + 1) * ny][None]

    def outer(i):
        return jnp.concatenate([plane(low, i), plane(high, i)], axis=0)

    def joined(i, inner):
        return jnp.concatenate([plane(low, i), inner, plane(high, i)], axis=0)

    start = own[pl.ds(0, nx)]
    k = joined(2, own[pl.ds(2 * nx, nx)])
    load = own[pl.ds(3 * nx, nx)]
    disp = joined(0, start)
    box = box9(jnp.concatenate([disp[1:2], disp[:1], disp[-1:], disp[-2:-1]], axis=0))
    box = jnp.concatenate([box[:2], jnp.zeros_like(disp[2:-2]), box[2:]], axis=0)
    vel = joined(1, own[pl.ds(nx, nx)]) + k * (1.0 / 26.0) * box
    disp = disp + vel
    box = box9(disp)
    vel = KEEP * vel + joined(3, load) + push(k, three(box), disp)
    far = outer(4) + outer(5) * (1.0 / 26.0) * jnp.concatenate([box[:1], box[-1:]], axis=0)
    disp = disp + vel
    wide = jnp.concatenate([far[:1], disp, far[1:]], axis=0)
    vel = stepped(KEEP * vel + joined(3, load), k, wide[:-2] + wide[1:-1] + wide[2:], disp)
    disp = disp + vel
    vel = stepped(KEEP * vel[1:-1] + load, k[1:-1], disp[:-2] + disp[1:-1] + disp[2:], disp[1:-1])
    disp = disp[1:-1] + vel
    fine_disp[...] = disp
    fine_vel[...] = vel
    rest = restrict(jnp.concatenate([disp, vel], axis=0), left, right)

    cy, cz = ny // 2, nz // 2
    wide_disp = coarse[pl.ds(0, half)]
    wide_k = coarse[pl.ds(2 * half, half)]
    ends = jnp.concatenate([low[6 * ny :][None], high[6 * ny :][None]], axis=0)
    out_disp = ends[:, :, :cz]
    out_moved = ends[:, :, cz:]
    out_k = restrict(jnp.concatenate([plane(low, 2), plane(low, 5), plane(high, 2), plane(high, 5)], axis=0), left, right)
    none = [jnp.zeros_like(wide_disp[:1])] * (half - 2)
    ends = jnp.concatenate([out_disp[:1], *none, out_disp[1:]], axis=0)
    wide_vel = coarse[pl.ds(half, half)] + wide_k * (1.0 / 6.0) * ends
    inner = jnp.concatenate([wide_disp[:1], wide_disp[-1:]], axis=0)
    out_moved = out_moved + out_k * (1.0 / 6.0) * inner
    moved = jnp.concatenate([out_moved[:1], wide_disp + wide_vel, out_moved[1:]], axis=0)
    image_disp, image_vel = coarse_step(moved, wide_vel, wide_k)
    first = lax.axis_index("tm") == 0
    image_disp = jnp.where(first, 0.0, image_disp)
    image_vel = jnp.where(first, 0.0, image_vel)
    old[pl.ds(0, half)] = image_disp
    old[pl.ds(half, half)] = image_vel
    message[pl.ds(0, half)] = rest[:half] - image_disp
    message[pl.ds(half, half)] = rest[half:] - image_vel
    message[pl.ds(2 * half, half)] = wide_k


def chain_kernel(times, jumps, partners, *refs):
    inputs = refs[: len(partners)]
    outputs = refs[len(partners) : len(partners) + len(jumps)]
    window = refs[-1]
    half = inputs[0].shape[0] // 3
    slab = lax.axis_index("slab")
    reach = times - 1
    window[...] = jnp.zeros(window.shape, F32)
    for ref, place in zip(inputs, partners):
        at = (place(slab) - slab + reach) * half
        for field in range(3):
            window[field, pl.ds(at, half)] = ref[pl.ds(field * half, half)]
    disp, vel, stiff = window[0], window[1], window[2]
    powers = []
    for power in range(reach):
        for _ in range(COARSE_STEPS):
            disp, vel = coarse_step(disp, vel[1:-1], stiff[1:-1])
            stiff = stiff[1:-1]
        edge = (disp.shape[0] - half) // 2
        powers.append((disp[edge : edge + half], vel[edge : edge + half]))
    slot = lax.axis_index("tm")
    for k, output in zip(jumps, outputs):
        gap = (slot ^ k) - (slot ^ 1)
        pick_disp, pick_vel = powers[0]
        for power in range(1, reach):
            pick_disp = jnp.where(gap == power + 1, powers[power][0], pick_disp)
            pick_vel = jnp.where(gap == power + 1, powers[power][1], pick_vel)
        output[pl.ds(0, half)] = pick_disp
        output[pl.ds(half, half)] = pick_vel


def finish_kernel(jumps, *refs):
    fine_disp, fine_vel, old = refs[:3]
    parts = refs[3 : 3 + len(jumps)]
    new_disp, new_vel = refs[3 + len(jumps) : 5 + len(jumps)]
    left, right = refs[-2:]
    slot = lax.axis_index("tm")
    total = -old[...]
    for k, part in zip(jumps, parts):
        total = total + jnp.where((slot ^ k ^ 1) < slot, part[...], 0.0)
    half2, cy, cz = total.shape
    rows = half2 * cy
    flat = flat2(total)
    lane = lax.broadcasted_iota(jnp.int32, flat.shape, 1) >> 1
    for scratch, part in ((left, lane), (right, lane + cz // 2)):
        part = jnp.take_along_axis(flat, part, axis=1)
        scratch[pl.ds(0, rows, stride=2), :] = part
        scratch[pl.ds(1, rows, stride=2), :] = part
    wide = jnp.concatenate([left[...], right[...]], axis=1).reshape(half2, 2 * cy, 2 * cz)
    for i in range(fine_disp.shape[0]):
        new_disp[0, i] = fine_disp[i] + wide[i // 2]
        new_vel[0, i] = fine_vel[i] + wide[half2 // 2 + i // 2]


def local(start_disp, start_vel, stiffness, pressure, wet_tiles):
    slabs = lax.axis_size("slab")
    times = lax.axis_size("tm")
    _, nx, ny, nz = start_disp.shape
    half = nx // 2
    pair = ("slab", "tm")

    def at(s, t):
        return s * times + t

    low_pairs = [(at(s, t), at(s ^ 1, t)) for s in range(slabs) for t in range(times)]
    high_pairs = []
    for s in range(slabs):
        for t in range(times):
            if s == 0 or s == slabs - 1:
                high_pairs.append((at(s, t), at(s, t ^ 1)))
            else:
                high_pairs.append((at(s, t), at(s + 1 if s % 2 else s - 1, t)))

    packed = resident(6 * ny + ny // 2, nz)
    coarse_cells = (ny // 2, nz // 2)
    def pack_body(*refs):
        pack_kernel(slabs, *refs)

    own, coarse, send_a, send_b = pl.pallas_call(
        pack_body,
        out_shape=(resident(4 * nx, ny, nz), resident(3 * half, *coarse_cells), packed, packed),
        in_specs=[pl.BlockSpec(memory_space=pl.ANY)] * 5,
        out_specs=vmem(4),
        scratch_shapes=[
            pltpu.VMEM((3 * half * ny, nz // 2), F32),
            pltpu.VMEM((3 * half * ny, nz // 2), F32),
            pltpu.VMEM((nx, ny, nz), F32),
            pltpu.VMEM((nx, ny, nz), F32),
            pltpu.VMEM(wet_tiles.shape, jnp.int32),
            pltpu.SemaphoreType.DMA((5,)),
        ],
        name="pack",
    )(start_disp, start_vel, stiffness, pressure, wet_tiles)
    recv_a = lax.ppermute(send_a, pair, low_pairs)
    recv_b = lax.ppermute(send_b, pair, high_pairs)

    grid = resident(nx, ny, nz)
    fine_disp, fine_vel, message, old = pl.pallas_call(
        fine_kernel,
        out_shape=(grid, grid, resident(3 * half, *coarse_cells), resident(2 * half, *coarse_cells)),
        in_specs=vmem(4),
        out_specs=vmem(4),
        scratch_shapes=[pltpu.VMEM((2 * half * ny, nz // 2), F32)] * 2,
        name="fine",
    )(*pinned(own, coarse, recv_a, recv_b))

    messages, places = [], []
    if slabs <= times and slabs & (slabs - 1) == 0:
        for k in range(slabs):
            route = []
            for s in range(slabs):
                for t in range(times):
                    reach = times - 1 - min(t, t ^ 1)
                    route.append((at(s, t), at(s ^ k if abs((s ^ k) - s) <= reach else s, t ^ 1)))
            messages.append(lax.ppermute(message, pair, route))
            places.append(lambda s, k=k: s ^ k)
    else:
        for shift in range(1 - times, times):
            route = [(at(s - shift, t ^ 1), at(s, t)) for s in range(slabs) if 0 <= s - shift < slabs for t in range(times)]
            messages.append(lax.ppermute(message, pair, route))
            places.append(lambda s, shift=shift: s - shift)

    jumps = [*range(2, times), 0]

    def chain_body(*refs):
        chain_kernel(times, jumps, places, *refs)

    link = resident(2 * half, *coarse_cells)
    sends = pl.pallas_call(
        chain_body,
        out_shape=(link,) * len(jumps),
        in_specs=vmem(len(messages)),
        out_specs=vmem(len(jumps)),
        scratch_shapes=[pltpu.VMEM((3, (2 * times - 1) * half, *coarse_cells), F32)],
        name="chain",
    )(*pinned(*messages))
    parts = [lax.ppermute(send, "tm", [(t, t ^ k) for t in range(times)]) for k, send in zip(jumps[:-1], sends)]

    def finish_body(*refs):
        finish_kernel(jumps, *refs)

    return pl.pallas_call(
        finish_body,
        out_shape=(shape(1, nx, ny, nz), shape(1, nx, ny, nz)),
        in_specs=vmem(3 + len(jumps)),
        out_specs=vmem(2),
        scratch_shapes=[pltpu.VMEM((nx * ny, nz // 2), F32)] * 2,
        name="finish",
    )(*pinned(fine_disp, fine_vel, old, *parts, sends[-1]))


def solution(mesh):
    in_specs = (
        P("tm", "slab", "groups", None),
        P("tm", "slab", "groups", None),
        P("slab", "groups", None),
        P("slab", "groups", None),
        P("slab", "groups", None),
    )
    out_specs = (P("tm", "slab", "groups", None), P("tm", "slab", "groups", None))
    return jax.shard_map(local, mesh=mesh, in_specs=in_specs, out_specs=out_specs, check_vma=False)
```

```python
import jax
import jax.numpy as jnp
from jax import lax
from jax.experimental import pallas as pl
from jax.experimental.pallas import tpu as pltpu
from jax.sharding import PartitionSpec as P

FINE_STEPS = 4
COARSE_STEPS = 2
KEEP = 0.95
F32 = jnp.float32


def vmem(count):
    return [pl.BlockSpec(memory_space=pltpu.VMEM)] * count


def shape(*dims):
    return jax.ShapeDtypeStruct(dims, F32)


def resident(*dims):
    return pltpu.VMEM(dims, F32)


def pinned(*arrays):
    return [pltpu.with_memory_space_constraint(x, pltpu.VMEM) for x in arrays]


def dot(left, right):
    return lax.dot_general(left, right, (((1,), (0,)), ((), ())), preferred_element_type=F32)


def selector(rows, cols, down, across, value=1.0):
    row = lax.shift_right_logical(lax.broadcasted_iota(jnp.int32, (rows, cols), 0), down)
    col = lax.shift_right_logical(lax.broadcasted_iota(jnp.int32, (rows, cols), 1), across)
    return jnp.where(row == col, value, 0.0).astype(jnp.bfloat16)


def flat2(x):
    return x.reshape(x.shape[0] * x.shape[1], x.shape[2])


def around(x, axis):
    size = x.shape[axis]
    none = jnp.zeros_like(lax.slice_in_dim(x, 0, 1, axis=axis))
    before = jnp.concatenate([none, lax.slice_in_dim(x, 0, size - 1, axis=axis)], axis)
    after = jnp.concatenate([lax.slice_in_dim(x, 1, size, axis=axis), none], axis)
    return before + after


def box9(x):
    x = x + around(x, 1)
    return x + around(x, 2)


def face4(x):
    return around(x, 1) + around(x, 2)


def three(box):
    none = jnp.zeros_like(box[:1])
    return box + jnp.concatenate([none, box[:-1]], axis=0) + jnp.concatenate([box[1:], none], axis=0)


def push(stiff, boxes, disp):
    return stiff * ((boxes - disp) * (1.0 / 26.0) - disp)


def stepped(rest, stiff, planes, disp):
    along = planes + around(planes, 1)
    rest = rest + stiff * ((along - disp) * (1.0 / 26.0) - disp)
    return rest + (stiff * (1.0 / 26.0)) * around(along, 2)


def pull(stiff, faces, disp):
    return stiff * (faces * (1.0 / 6.0) - disp)


def coarse_step(disp, vel, stiff):
    mid = disp[1:-1]
    vel = KEEP * vel + pull(stiff, disp[:-2] + disp[2:] + around(mid, 1), mid)
    vel = vel + (stiff * (1.0 / 6.0)) * around(mid, 2)
    return mid + vel, vel


def restrict(x, left, right):
    planes, ny, nz = x.shape
    half, lanes = planes // 2, nz // 2
    pairs = x.reshape(half, 2, ny, nz)
    pairs = flat2(pairs[:, 0] + pairs[:, 1])
    rows = half * ny
    lane = lax.broadcasted_iota(jnp.int32, (rows // 2, lanes), 1)
    even = (lane * 2) & (lanes - 1)

    def squeeze(scratch, part):
        scratch[pl.ds(0, rows), :] = part
        both = scratch[pl.ds(0, rows // 2, stride=2), :] + scratch[pl.ds(1, rows // 2, stride=2), :]
        return jnp.take_along_axis(both, even, axis=1) + jnp.take_along_axis(both, even + 1, axis=1)

    out = jnp.where(lane < lanes // 2, squeeze(left, pairs[:, :lanes]), squeeze(right, pairs[:, lanes:]))
    return (0.125 * out).reshape(half, ny // 2, lanes)


def pack_kernel(count, disp, vel, stiff, press, tiles, own, coarse, send_a, send_b, left, right, vel_in, press_in, tiles_in, sems):
    nx, ny, nz = stiff.shape
    half = nx // 2
    moves = [
        pltpu.make_async_copy(disp.at[0], own.at[pl.ds(0, nx)], sems.at[0]),
        pltpu.make_async_copy(stiff, own.at[pl.ds(2 * nx, nx)], sems.at[1]),
        pltpu.make_async_copy(vel.at[0], vel_in, sems.at[2]),
        pltpu.make_async_copy(tiles, tiles_in, sems.at[3]),
        pltpu.make_async_copy(press, press_in, sems.at[4]),
    ]
    for i, move in enumerate(moves):
        move.start(priority=i % 2)
    slab = lax.axis_index("slab")
    for move in moves:
        move.wait()
    start = own[pl.ds(0, nx)]
    k = own[pl.ds(2 * nx, nx)]
    speed = vel_in[...]
    wet = flat2(tiles_in[...]).astype(F32).astype(jnp.bfloat16)
    shift = (nz // tiles.shape[2]).bit_length() - 1
    load = dot(wet, selector(tiles.shape[2], nz, 0, shift)).reshape(nx, ny, nz) * press_in[...]
    first = stepped(KEEP * speed + load, k, three(start), start)
    moved = start + first
    inner = slice(1, nx - 1)
    box_moved = box9(moved[inner])
    near = jnp.concatenate([box_moved[:1] + box_moved[1:2], box_moved[-2:-1] + box_moved[-1:]], axis=0)
    spots = (1, nx - 2)

    def at(x):
        return jnp.concatenate([x[i : i + 1] for i in spots], axis=0)

    second = KEEP * at(first) + at(load) + push(at(k), near, at(moved))

    fields = restrict(jnp.concatenate([start, speed, k], axis=0), left, right)
    wide_disp, wide_vel, wide_k = fields[:half], fields[half : 2 * half], fields[2 * half :]
    none = jnp.zeros_like(wide_disp[:1])
    faces = face4(wide_disp) + jnp.concatenate([none, wide_disp[:-1]], axis=0) + jnp.concatenate([wide_disp[1:], none], axis=0)
    wide_first = KEEP * wide_vel + pull(wide_k, faces, wide_disp)

    own[pl.ds(nx, nx)] = first
    own[pl.ds(3 * nx, nx)] = load
    coarse[pl.ds(0, half)] = wide_disp
    coarse[pl.ds(half, half)] = wide_first
    coarse[pl.ds(2 * half, half)] = wide_k

    def fill(target, edge, spot, end, which):
        share = k[edge] * (1.0 / 26.0)
        planes = (start[edge], first[edge], k[edge], load[edge] + share * box_moved[spot - 1], second[which], k[spot])
        for i, plane in enumerate(planes):
            target[pl.ds(i * ny, ny), :] = plane
        cy, cz = ny // 2, nz // 2
        target[pl.ds(len(planes) * ny, cy), pl.ds(0, cz)] = wide_disp[end]
        target[pl.ds(len(planes) * ny, cy), pl.ds(cz, cz)] = wide_disp[end] + wide_first[end]

    @pl.when(slab % 2 == 0)
    def _():
        fill(send_a, nx - 1, nx - 2, half - 1, 1)
        fill(send_b, 0, 1, 0, 0)

    @pl.when(slab % 2 == 1)
    def _():
        fill(send_a, 0, 1, 0, 0)
        fill(send_b, nx - 1, nx - 2, half - 1, 1)

    @pl.when((slab == 0) | (slab == count - 1))
    def _():
        send_b[...] = jnp.zeros(send_b.shape, F32)


def fine_kernel(own, coarse, recv_a, recv_b, fine_disp, fine_vel, message, old, left, right):
    nx, ny, nz = fine_disp.shape
    half = nx // 2
    slab = lax.axis_index("slab")
    even = slab % 2 == 0
    a, b = recv_a[...], recv_b[...]
    low = jnp.where(even, b, a)
    high = jnp.where(even, a, b)

    def plane(message, i):
        return message[i * ny : (i + 1) * ny][None]

    def outer(i):
        return jnp.concatenate([plane(low, i), plane(high, i)], axis=0)

    def joined(i, inner):
        return jnp.concatenate([plane(low, i), inner, plane(high, i)], axis=0)

    start = own[pl.ds(0, nx)]
    k = joined(2, own[pl.ds(2 * nx, nx)])
    load = own[pl.ds(3 * nx, nx)]
    disp = joined(0, start)
    box = box9(jnp.concatenate([disp[1:2], disp[:1], disp[-1:], disp[-2:-1]], axis=0))
    box = jnp.concatenate([box[:2], jnp.zeros_like(disp[2:-2]), box[2:]], axis=0)
    vel = joined(1, own[pl.ds(nx, nx)]) + k * (1.0 / 26.0) * box
    disp = disp + vel
    along = disp + around(disp, 1)
    vel = KEEP * vel + joined(3, load) + push(k, three(along), disp)
    shifted = around(along, 2)
    vel = vel + (k * (1.0 / 26.0)) * three(shifted)
    box = along + shifted
    far = outer(4) + outer(5) * (1.0 / 26.0) * jnp.concatenate([box[:1], box[-1:]], axis=0)
    disp = disp + vel
    wide = jnp.concatenate([far[:1], disp, far[1:]], axis=0)
    vel = stepped(KEEP * vel + joined(3, load), k, wide[:-2] + wide[1:-1] + wide[2:], disp)
    disp = disp + vel
    vel = stepped(KEEP * vel[1:-1] + load, k[1:-1], disp[:-2] + disp[1:-1] + disp[2:], disp[1:-1])
    disp = disp[1:-1] + vel
    fine_disp[...] = disp
    fine_vel[...] = vel
    rest = restrict(jnp.concatenate([disp, vel], axis=0), left, right)

    cy, cz = ny // 2, nz // 2
    wide_disp = coarse[pl.ds(0, half)]
    wide_k = coarse[pl.ds(2 * half, half)]
    ends = jnp.concatenate([low[6 * ny :][None], high[6 * ny :][None]], axis=0)
    out_disp = ends[:, :, :cz]
    out_moved = ends[:, :, cz:]
    out_k = restrict(jnp.concatenate([plane(low, 2), plane(low, 5), plane(high, 2), plane(high, 5)], axis=0), left, right)
    none = [jnp.zeros_like(wide_disp[:1])] * (half - 2)
    ends = jnp.concatenate([out_disp[:1], *none, out_disp[1:]], axis=0)
    wide_vel = coarse[pl.ds(half, half)] + wide_k * (1.0 / 6.0) * ends
    inner = jnp.concatenate([wide_disp[:1], wide_disp[-1:]], axis=0)
    out_moved = out_moved + out_k * (1.0 / 6.0) * inner
    moved = jnp.concatenate([out_moved[:1], wide_disp + wide_vel, out_moved[1:]], axis=0)
    image_disp, image_vel = coarse_step(moved, wide_vel, wide_k)
    first = lax.axis_index("tm") == 0
    image_disp = jnp.where(first, 0.0, image_disp)
    image_vel = jnp.where(first, 0.0, image_vel)
    old[pl.ds(0, half)] = image_disp
    old[pl.ds(half, half)] = image_vel
    message[pl.ds(0, half)] = rest[:half] - image_disp
    message[pl.ds(half, half)] = rest[half:] - image_vel
    message[pl.ds(2 * half, half)] = wide_k


def chain_kernel(times, jumps, partners, *refs):
    inputs = refs[: len(partners)]
    outputs = refs[len(partners) : len(partners) + len(jumps)]
    window = refs[-1]
    half = inputs[0].shape[0] // 3
    slab = lax.axis_index("slab")
    reach = times - 1
    window[...] = jnp.zeros(window.shape, F32)
    for ref, place in zip(inputs, partners):
        at = (place(slab) - slab + reach) * half
        for field in range(3):
            window[field, pl.ds(at, half)] = ref[pl.ds(field * half, half)]
    disp, vel, stiff = window[0], window[1], window[2]
    powers = []
    for power in range(reach):
        for _ in range(COARSE_STEPS):
            disp, vel = coarse_step(disp, vel[1:-1], stiff[1:-1])
            stiff = stiff[1:-1]
        edge = (disp.shape[0] - half) // 2
        powers.append((disp[edge : edge + half], vel[edge : edge + half]))
    slot = lax.axis_index("tm")
    for k, output in zip(jumps, outputs):
        gap = (slot ^ k) - (slot ^ 1)
        pick_disp, pick_vel = powers[0]
        for power in range(1, reach):
            pick_disp = jnp.where(gap == power + 1, powers[power][0], pick_disp)
            pick_vel = jnp.where(gap == power + 1, powers[power][1], pick_vel)
        output[pl.ds(0, half)] = pick_disp
        output[pl.ds(half, half)] = pick_vel


def finish_kernel(jumps, *refs):
    fine_disp, fine_vel, old = refs[:3]
    parts = refs[3 : 3 + len(jumps)]
    new_disp, new_vel = refs[3 + len(jumps) : 5 + len(jumps)]
    left, right = refs[-2:]
    slot = lax.axis_index("tm")
    total = -old[...]
    for k, part in zip(jumps, parts):
        total = total + jnp.where((slot ^ k ^ 1) < slot, part[...], 0.0)
    half2, cy, cz = total.shape
    rows = half2 * cy
    flat = flat2(total)
    lane = lax.broadcasted_iota(jnp.int32, flat.shape, 1) >> 1
    for scratch, part in ((left, lane), (right, lane + cz // 2)):
        part = jnp.take_along_axis(flat, part, axis=1)
        scratch[pl.ds(0, rows, stride=2), :] = part
        scratch[pl.ds(1, rows, stride=2), :] = part
    wide = jnp.concatenate([left[...], right[...]], axis=1).reshape(half2, 2 * cy, 2 * cz)
    for i in range(fine_disp.shape[0]):
        new_disp[0, i] = fine_disp[i] + wide[i // 2]
        new_vel[0, i] = fine_vel[i] + wide[half2 // 2 + i // 2]


def local(start_disp, start_vel, stiffness, pressure, wet_tiles):
    slabs = lax.axis_size("slab")
    times = lax.axis_size("tm")
    _, nx, ny, nz = start_disp.shape
    half = nx // 2
    pair = ("slab", "tm")

    def at(s, t):
        return s * times + t

    low_pairs = [(at(s, t), at(s ^ 1, t)) for s in range(slabs) for t in range(times)]
    high_pairs = []
    for s in range(slabs):
        for t in range(times):
            if s == 0 or s == slabs - 1:
                high_pairs.append((at(s, t), at(s, t ^ 1)))
            else:
                high_pairs.append((at(s, t), at(s + 1 if s % 2 else s - 1, t)))

    packed = resident(6 * ny + ny // 2, nz)
    coarse_cells = (ny // 2, nz // 2)
    def pack_body(*refs):
        pack_kernel(slabs, *refs)

    own, coarse, send_a, send_b = pl.pallas_call(
        pack_body,
        out_shape=(resident(4 * nx, ny, nz), resident(3 * half, *coarse_cells), packed, packed),
        in_specs=[pl.BlockSpec(memory_space=pl.ANY)] * 5,
        out_specs=vmem(4),
        scratch_shapes=[
            pltpu.VMEM((3 * half * ny, nz // 2), F32),
            pltpu.VMEM((3 * half * ny, nz // 2), F32),
            pltpu.VMEM((nx, ny, nz), F32),
            pltpu.VMEM((nx, ny, nz), F32),
            pltpu.VMEM(wet_tiles.shape, jnp.int32),
            pltpu.SemaphoreType.DMA((5,)),
        ],
        name="pack",
    )(start_disp, start_vel, stiffness, pressure, wet_tiles)
    recv_a = lax.ppermute(send_a, pair, low_pairs)
    recv_b = lax.ppermute(send_b, pair, high_pairs)

    grid = resident(nx, ny, nz)
    fine_disp, fine_vel, message, old = pl.pallas_call(
        fine_kernel,
        out_shape=(grid, grid, resident(3 * half, *coarse_cells), resident(2 * half, *coarse_cells)),
        in_specs=vmem(4),
        out_specs=vmem(4),
        scratch_shapes=[pltpu.VMEM((2 * half * ny, nz // 2), F32)] * 2,
        name="fine",
    )(*pinned(own, coarse, recv_a, recv_b))

    messages, places = [], []
    if slabs <= times and slabs & (slabs - 1) == 0:
        for k in range(slabs):
            route = []
            for s in range(slabs):
                for t in range(times):
                    reach = times - 1 - min(t, t ^ 1)
                    route.append((at(s, t), at(s ^ k if abs((s ^ k) - s) <= reach else s, t ^ 1)))
            messages.append(lax.ppermute(message, pair, route))
            places.append(lambda s, k=k: s ^ k)
    else:
        for shift in range(1 - times, times):
            route = [(at(s - shift, t ^ 1), at(s, t)) for s in range(slabs) if 0 <= s - shift < slabs for t in range(times)]
            messages.append(lax.ppermute(message, pair, route))
            places.append(lambda s, shift=shift: s - shift)

    jumps = [*range(2, times), 0]

    def chain_body(*refs):
        chain_kernel(times, jumps, places, *refs)

    link = resident(2 * half, *coarse_cells)
    sends = pl.pallas_call(
        chain_body,
        out_shape=(link,) * len(jumps),
        in_specs=vmem(len(messages)),
        out_specs=vmem(len(jumps)),
        scratch_shapes=[pltpu.VMEM((3, (2 * times - 1) * half, *coarse_cells), F32)],
        name="chain",
    )(*pinned(*messages))
    parts = [lax.ppermute(send, "tm", [(t, t ^ k) for t in range(times)]) for k, send in zip(jumps[:-1], sends)]

    def finish_body(*refs):
        finish_kernel(jumps, *refs)

    return pl.pallas_call(
        finish_body,
        out_shape=(shape(1, nx, ny, nz), shape(1, nx, ny, nz)),
        in_specs=vmem(3 + len(jumps)),
        out_specs=vmem(2),
        scratch_shapes=[pltpu.VMEM((nx * ny, nz // 2), F32)] * 2,
        name="finish",
    )(*pinned(fine_disp, fine_vel, old, *parts, sends[-1]))


def solution(mesh):
    in_specs = (
        P("tm", "slab", "groups", None),
        P("tm", "slab", "groups", None),
        P("slab", "groups", None),
        P("slab", "groups", None),
        P("slab", "groups", None),
    )
    out_specs = (P("tm", "slab", "groups", None), P("tm", "slab", "groups", None))
    return jax.shard_map(local, mesh=mesh, in_specs=in_specs, out_specs=out_specs, check_vma=False)
```

```python
import jax
import jax.numpy as jnp
from jax import lax
from jax.experimental import pallas as pl
from jax.experimental.pallas import tpu as pltpu
from jax.sharding import PartitionSpec as P

FINE_STEPS = 4
COARSE_STEPS = 2
KEEP = 0.95
F32 = jnp.float32


def vmem(count):
    return [pl.BlockSpec(memory_space=pltpu.VMEM)] * count


def shape(*dims):
    return jax.ShapeDtypeStruct(dims, F32)


def resident(*dims):
    return pltpu.VMEM(dims, F32)


def pinned(*arrays):
    return [pltpu.with_memory_space_constraint(x, pltpu.VMEM) for x in arrays]


def dot(left, right):
    return lax.dot_general(left, right, (((1,), (0,)), ((), ())), preferred_element_type=F32)


def selector(rows, cols, down, across, value=1.0):
    row = lax.shift_right_logical(lax.broadcasted_iota(jnp.int32, (rows, cols), 0), down)
    col = lax.shift_right_logical(lax.broadcasted_iota(jnp.int32, (rows, cols), 1), across)
    return jnp.where(row == col, value, 0.0).astype(jnp.bfloat16)


def flat2(x):
    return x.reshape(x.shape[0] * x.shape[1], x.shape[2])


def around(x, axis):
    size = x.shape[axis]
    none = jnp.zeros_like(lax.slice_in_dim(x, 0, 1, axis=axis))
    before = jnp.concatenate([none, lax.slice_in_dim(x, 0, size - 1, axis=axis)], axis)
    after = jnp.concatenate([lax.slice_in_dim(x, 1, size, axis=axis), none], axis)
    return before + after


def box9(x):
    x = x + around(x, 1)
    return x + around(x, 2)


def face4(x):
    return around(x, 1) + around(x, 2)


def three(box):
    none = jnp.zeros_like(box[:1])
    return box + jnp.concatenate([none, box[:-1]], axis=0) + jnp.concatenate([box[1:], none], axis=0)


def push(stiff, boxes, disp):
    return stiff * ((boxes - disp) * (1.0 / 26.0) - disp)


def stepped(rest, stiff, planes, disp):
    along = planes + around(planes, 1)
    rest = rest + stiff * ((along - disp) * (1.0 / 26.0) - disp)
    return rest + (stiff * (1.0 / 26.0)) * around(along, 2)


def pull(stiff, faces, disp):
    return stiff * (faces * (1.0 / 6.0) - disp)


def coarse_step(disp, vel, stiff):
    mid = disp[1:-1]
    vel = KEEP * vel + pull(stiff, disp[:-2] + disp[2:] + around(mid, 1), mid)
    vel = vel + (stiff * (1.0 / 6.0)) * around(mid, 2)
    return mid + vel, vel


def restrict(x, left, right):
    planes, ny, nz = x.shape
    half, lanes = planes // 2, nz // 2
    pairs = x.reshape(half, 2, ny, nz)
    pairs = flat2(pairs[:, 0] + pairs[:, 1])
    rows = half * ny
    lane = lax.broadcasted_iota(jnp.int32, (rows // 2, lanes), 1)
    even = (lane * 2) & (lanes - 1)

    def squeeze(scratch, part):
        scratch[pl.ds(0, rows), :] = part
        both = scratch[pl.ds(0, rows // 2, stride=2), :] + scratch[pl.ds(1, rows // 2, stride=2), :]
        return jnp.take_along_axis(both, even, axis=1) + jnp.take_along_axis(both, even + 1, axis=1)

    out = jnp.where(lane < lanes // 2, squeeze(left, pairs[:, :lanes]), squeeze(right, pairs[:, lanes:]))
    return (0.125 * out).reshape(half, ny // 2, lanes)


def pack_kernel(count, disp, vel, stiff, press, tiles, own, coarse, send_a, send_b, left, right, vel_in, press_in, tiles_in, sems):
    nx, ny, nz = stiff.shape
    half = nx // 2
    moves = [
        pltpu.make_async_copy(disp.at[0], own.at[pl.ds(0, nx)], sems.at[0]),
        pltpu.make_async_copy(stiff, own.at[pl.ds(2 * nx, nx)], sems.at[1]),
        pltpu.make_async_copy(vel.at[0], vel_in, sems.at[2]),
        pltpu.make_async_copy(tiles, tiles_in, sems.at[3]),
        pltpu.make_async_copy(press, press_in, sems.at[4]),
    ]
    for i, move in enumerate(moves):
        move.start(priority=i % 2)
    slab = lax.axis_index("slab")
    for move in moves:
        move.wait()
    start = own[pl.ds(0, nx)]
    k = own[pl.ds(2 * nx, nx)]
    speed = vel_in[...]
    wet = flat2(tiles_in[...]).astype(F32).astype(jnp.bfloat16)
    shift = (nz // tiles.shape[2]).bit_length() - 1
    load = dot(wet, selector(tiles.shape[2], nz, 0, shift)).reshape(nx, ny, nz) * press_in[...]
    first = stepped(KEEP * speed + load, k, three(start), start)
    moved = start + first
    inner = slice(1, nx - 1)
    box_moved = box9(moved[inner])
    near = jnp.concatenate([box_moved[:1] + box_moved[1:2], box_moved[-2:-1] + box_moved[-1:]], axis=0)
    spots = (1, nx - 2)

    def at(x):
        return jnp.concatenate([x[i : i + 1] for i in spots], axis=0)

    second = KEEP * at(first) + at(load) + push(at(k), near, at(moved))

    fields = restrict(jnp.concatenate([start, speed, k], axis=0), left, right)
    wide_disp, wide_vel, wide_k = fields[:half], fields[half : 2 * half], fields[2 * half :]
    none = jnp.zeros_like(wide_disp[:1])
    faces = face4(wide_disp) + jnp.concatenate([none, wide_disp[:-1]], axis=0) + jnp.concatenate([wide_disp[1:], none], axis=0)
    wide_first = KEEP * wide_vel + pull(wide_k, faces, wide_disp)

    own[pl.ds(nx, nx)] = first
    own[pl.ds(3 * nx, nx)] = load
    coarse[pl.ds(0, half)] = wide_disp
    coarse[pl.ds(half, half)] = wide_first
    coarse[pl.ds(2 * half, half)] = wide_k

    def fill(target, edge, spot, end, which):
        share = k[edge] * (1.0 / 26.0)
        planes = (start[edge], first[edge], k[edge], load[edge] + share * box_moved[spot - 1], second[which], k[spot])
        for i, plane in enumerate(planes):
            target[pl.ds(i * ny, ny), :] = plane
        cy, cz = ny // 2, nz // 2
        target[pl.ds(len(planes) * ny, cy), pl.ds(0, cz)] = wide_disp[end]
        target[pl.ds(len(planes) * ny, cy), pl.ds(cz, cz)] = wide_disp[end] + wide_first[end]

    @pl.when(slab % 2 == 0)
    def _():
        fill(send_a, nx - 1, nx - 2, half - 1, 1)
        fill(send_b, 0, 1, 0, 0)

    @pl.when(slab % 2 == 1)
    def _():
        fill(send_a, 0, 1, 0, 0)
        fill(send_b, nx - 1, nx - 2, half - 1, 1)

    @pl.when((slab == 0) | (slab == count - 1))
    def _():
        send_b[...] = jnp.zeros(send_b.shape, F32)


def fine_kernel(own, coarse, recv_a, recv_b, fine_disp, fine_vel, message, old, left, right):
    nx, ny, nz = fine_disp.shape
    half = nx // 2
    slab = lax.axis_index("slab")
    even = slab % 2 == 0
    a, b = recv_a[...], recv_b[...]
    low = jnp.where(even, b, a)
    high = jnp.where(even, a, b)

    def plane(message, i):
        return message[i * ny : (i + 1) * ny][None]

    def outer(i):
        return jnp.concatenate([plane(low, i), plane(high, i)], axis=0)

    def joined(i, inner):
        return jnp.concatenate([plane(low, i), inner, plane(high, i)], axis=0)

    start = own[pl.ds(0, nx)]
    k = joined(2, own[pl.ds(2 * nx, nx)])
    load = own[pl.ds(3 * nx, nx)]
    disp = joined(0, start)
    crossed = jnp.concatenate([disp[1:2], disp[:1], disp[-1:], disp[-2:-1]], axis=0)
    crossed = crossed + around(crossed, 1)
    none = jnp.zeros_like(disp[2:-2])
    share = k * (1.0 / 26.0)
    vel = joined(1, own[pl.ds(nx, nx)]) + share * jnp.concatenate([crossed[:2], none, crossed[2:]], axis=0)
    crossed = around(crossed, 2)
    vel = vel + share * jnp.concatenate([crossed[:2], none, crossed[2:]], axis=0)
    disp = disp + vel
    along = disp + around(disp, 1)
    vel = KEEP * vel + joined(3, load) + push(k, three(along), disp)
    shifted = around(along, 2)
    vel = vel + (k * (1.0 / 26.0)) * three(shifted)
    box = along + shifted
    far = outer(4) + outer(5) * (1.0 / 26.0) * jnp.concatenate([box[:1], box[-1:]], axis=0)
    disp = disp + vel
    wide = jnp.concatenate([far[:1], disp, far[1:]], axis=0)
    vel = stepped(KEEP * vel + joined(3, load), k, wide[:-2] + wide[1:-1] + wide[2:], disp)
    disp = disp + vel
    vel = stepped(KEEP * vel[1:-1] + load, k[1:-1], disp[:-2] + disp[1:-1] + disp[2:], disp[1:-1])
    disp = disp[1:-1] + vel
    fine_disp[...] = disp
    fine_vel[...] = vel
    rest = restrict(jnp.concatenate([disp, vel], axis=0), left, right)

    cy, cz = ny // 2, nz // 2
    wide_disp = coarse[pl.ds(0, half)]
    wide_k = coarse[pl.ds(2 * half, half)]
    ends = jnp.concatenate([low[6 * ny :][None], high[6 * ny :][None]], axis=0)
    out_disp = ends[:, :, :cz]
    out_moved = ends[:, :, cz:]
    out_k = restrict(jnp.concatenate([plane(low, 2), plane(low, 5), plane(high, 2), plane(high, 5)], axis=0), left, right)
    none = [jnp.zeros_like(wide_disp[:1])] * (half - 2)
    ends = jnp.concatenate([out_disp[:1], *none, out_disp[1:]], axis=0)
    wide_vel = coarse[pl.ds(half, half)] + wide_k * (1.0 / 6.0) * ends
    inner = jnp.concatenate([wide_disp[:1], wide_disp[-1:]], axis=0)
    out_moved = out_moved + out_k * (1.0 / 6.0) * inner
    moved = jnp.concatenate([out_moved[:1], wide_disp + wide_vel, out_moved[1:]], axis=0)
    image_disp, image_vel = coarse_step(moved, wide_vel, wide_k)
    first = lax.axis_index("tm") == 0
    image_disp = jnp.where(first, 0.0, image_disp)
    image_vel = jnp.where(first, 0.0, image_vel)
    old[pl.ds(0, half)] = image_disp
    old[pl.ds(half, half)] = image_vel
    message[pl.ds(0, half)] = rest[:half] - image_disp
    message[pl.ds(half, half)] = rest[half:] - image_vel
    message[pl.ds(2 * half, half)] = wide_k


def chain_kernel(times, jumps, partners, *refs):
    inputs = refs[: len(partners)]
    outputs = refs[len(partners) : len(partners) + len(jumps)]
    window = refs[-1]
    half = inputs[0].shape[0] // 3
    slab = lax.axis_index("slab")
    reach = times - 1
    window[...] = jnp.zeros(window.shape, F32)
    for ref, place in zip(inputs, partners):
        at = (place(slab) - slab + reach) * half
        for field in range(3):
            window[field, pl.ds(at, half)] = ref[pl.ds(field * half, half)]
    disp, vel, stiff = window[0], window[1], window[2]
    powers = []
    for power in range(reach):
        for _ in range(COARSE_STEPS):
            disp, vel = coarse_step(disp, vel[1:-1], stiff[1:-1])
            stiff = stiff[1:-1]
        edge = (disp.shape[0] - half) // 2
        powers.append((disp[edge : edge + half], vel[edge : edge + half]))
    slot = lax.axis_index("tm")
    for k, output in zip(jumps, outputs):
        gap = (slot ^ k) - (slot ^ 1)
        pick_disp, pick_vel = powers[0]
        for power in range(1, reach):
            pick_disp = jnp.where(gap == power + 1, powers[power][0], pick_disp)
            pick_vel = jnp.where(gap == power + 1, powers[power][1], pick_vel)
        output[pl.ds(0, half)] = pick_disp
        output[pl.ds(half, half)] = pick_vel


def finish_kernel(jumps, *refs):
    fine_disp, fine_vel, old = refs[:3]
    parts = refs[3 : 3 + len(jumps)]
    new_disp, new_vel = refs[3 + len(jumps) : 5 + len(jumps)]
    left, right = refs[-2:]
    slot = lax.axis_index("tm")
    total = -old[...]
    for k, part in zip(jumps, parts):
        total = total + jnp.where((slot ^ k ^ 1) < slot, part[...], 0.0)
    half2, cy, cz = total.shape
    rows = half2 * cy
    flat = flat2(total)
    lane = lax.broadcasted_iota(jnp.int32, flat.shape, 1) >> 1
    for scratch, part in ((left, lane), (right, lane + cz // 2)):
        part = jnp.take_along_axis(flat, part, axis=1)
        scratch[pl.ds(0, rows, stride=2), :] = part
        scratch[pl.ds(1, rows, stride=2), :] = part
    wide = jnp.concatenate([left[...], right[...]], axis=1).reshape(half2, 2 * cy, 2 * cz)
    for i in range(fine_disp.shape[0]):
        new_disp[0, i] = fine_disp[i] + wide[i // 2]
        new_vel[0, i] = fine_vel[i] + wide[half2 // 2 + i // 2]


def local(start_disp, start_vel, stiffness, pressure, wet_tiles):
    slabs = lax.axis_size("slab")
    times = lax.axis_size("tm")
    _, nx, ny, nz = start_disp.shape
    half = nx // 2
    pair = ("slab", "tm")

    def at(s, t):
        return s * times + t

    low_pairs = [(at(s, t), at(s ^ 1, t)) for s in range(slabs) for t in range(times)]
    high_pairs = []
    for s in range(slabs):
        for t in range(times):
            if s == 0 or s == slabs - 1:
                high_pairs.append((at(s, t), at(s, t ^ 1)))
            else:
                high_pairs.append((at(s, t), at(s + 1 if s % 2 else s - 1, t)))

    packed = resident(6 * ny + ny // 2, nz)
    coarse_cells = (ny // 2, nz // 2)
    def pack_body(*refs):
        pack_kernel(slabs, *refs)

    own, coarse, send_a, send_b = pl.pallas_call(
        pack_body,
        out_shape=(resident(4 * nx, ny, nz), resident(3 * half, *coarse_cells), packed, packed),
        in_specs=[pl.BlockSpec(memory_space=pl.ANY)] * 5,
        out_specs=vmem(4),
        scratch_shapes=[
            pltpu.VMEM((3 * half * ny, nz // 2), F32),
            pltpu.VMEM((3 * half * ny, nz // 2), F32),
            pltpu.VMEM((nx, ny, nz), F32),
            pltpu.VMEM((nx, ny, nz), F32),
            pltpu.VMEM(wet_tiles.shape, jnp.int32),
            pltpu.SemaphoreType.DMA((5,)),
        ],
        name="pack",
    )(start_disp, start_vel, stiffness, pressure, wet_tiles)
    recv_a = lax.ppermute(send_a, pair, low_pairs)
    recv_b = lax.ppermute(send_b, pair, high_pairs)

    grid = resident(nx, ny, nz)
    fine_disp, fine_vel, message, old = pl.pallas_call(
        fine_kernel,
        out_shape=(grid, grid, resident(3 * half, *coarse_cells), resident(2 * half, *coarse_cells)),
        in_specs=vmem(4),
        out_specs=vmem(4),
        scratch_shapes=[pltpu.VMEM((2 * half * ny, nz // 2), F32)] * 2,
        name="fine",
    )(*pinned(own, coarse, recv_a, recv_b))

    messages, places = [], []
    if slabs <= times and slabs & (slabs - 1) == 0:
        for k in range(slabs):
            route = []
            for s in range(slabs):
                for t in range(times):
                    reach = times - 1 - min(t, t ^ 1)
                    route.append((at(s, t), at(s ^ k if abs((s ^ k) - s) <= reach else s, t ^ 1)))
            messages.append(lax.ppermute(message, pair, route))
            places.append(lambda s, k=k: s ^ k)
    else:
        for shift in range(1 - times, times):
            route = [(at(s - shift, t ^ 1), at(s, t)) for s in range(slabs) if 0 <= s - shift < slabs for t in range(times)]
            messages.append(lax.ppermute(message, pair, route))
            places.append(lambda s, shift=shift: s - shift)

    jumps = [*range(2, times), 0]

    def chain_body(*refs):
        chain_kernel(times, jumps, places, *refs)

    link = resident(2 * half, *coarse_cells)
    sends = pl.pallas_call(
        chain_body,
        out_shape=(link,) * len(jumps),
        in_specs=vmem(len(messages)),
        out_specs=vmem(len(jumps)),
        scratch_shapes=[pltpu.VMEM((3, (2 * times - 1) * half, *coarse_cells), F32)],
        name="chain",
    )(*pinned(*messages))
    parts = [lax.ppermute(send, "tm", [(t, t ^ k) for t in range(times)]) for k, send in zip(jumps[:-1], sends)]

    def finish_body(*refs):
        finish_kernel(jumps, *refs)

    return pl.pallas_call(
        finish_body,
        out_shape=(shape(1, nx, ny, nz), shape(1, nx, ny, nz)),
        in_specs=vmem(3 + len(jumps)),
        out_specs=vmem(2),
        scratch_shapes=[pltpu.VMEM((nx * ny, nz // 2), F32)] * 2,
        name="finish",
    )(*pinned(fine_disp, fine_vel, old, *parts, sends[-1]))


def solution(mesh):
    in_specs = (
        P("tm", "slab", "groups", None),
        P("tm", "slab", "groups", None),
        P("slab", "groups", None),
        P("slab", "groups", None),
        P("slab", "groups", None),
    )
    out_specs = (P("tm", "slab", "groups", None), P("tm", "slab", "groups", None))
    return jax.shard_map(local, mesh=mesh, in_specs=in_specs, out_specs=out_specs, check_vma=False)
```
